256 devices in a mesh: gx: 8 (over y, z_hi), gy: 8 (over z_lo, core), gz: 4 (over x).
Axes of the slice: x: 4, y: 4, z: 8 (z_hi: 2, z_lo: 4; z = z_hi * 4 + z_lo), core: 2. Of those that a mesh axis runs over, the one named last changes fastest.
Arguments:
- latents: bfloat16 [262144, 128], P(('gx', 'gy', 'gz')), may hold values from -6 to 6
- grad_mixed: bfloat16 [262144, 128], P(('gx', 'gy', 'gz')), may hold values from -6 to 6
- neighbours: int32 [262144, 16], P(('gx', 'gy', 'gz')), may hold values from 0 to 1535, as said below
- send_list: int32 [1024, 64], P(('gx', 'gy', 'gz')), may hold values from 0 to 1023
- cluster: int32 [262144], P(('gx', 'gy', 'gz')), may hold values from 0 to 255
- w_send: bfloat16 [128, 128], replicated, may hold values from -0.5 to 0.5
- w_recv: bfloat16 [128, 128], replicated, may hold values from -0.5 to 0.5
- w_edge: bfloat16 [128, 128], replicated, may hold values from -0.5 to 0.5
- edge_gain: float32 [128], replicated, may hold values from 0.1 to 1.9
- w_self: bfloat16 [128, 128], replicated, may hold values from -0.5 to 0.5
- w_agg: bfloat16 [128, 128], replicated, may hold values from -0.5 to 0.5
- w_node: bfloat16 [128, 128], replicated, may hold values from -0.5 to 0.5
- node_gain: float32 [128], replicated, may hold values from 0.1 to 1.9
- w_pool_in: bfloat16 [128, 128], replicated, may hold values from -0.25 to 0.25
- w_pool_out: bfloat16 [128, 128], replicated, may hold values from -0.5 to 0.5
Outputs:
- mixed: bfloat16 [262144, 128], P(('gx', 'gy', 'gz'))
- grad_latents: float32 [262144, 128], P(('gx', 'gy', 'gz'))
- grad_matrices: float32 [8, 128, 128], replicated
- grad_gains: float32 [2, 128], replicated
The draws below stay inside these ranges and needn't reach their ends.
Inputs may be any that keep to these rules, and one draw needn't show every extreme that they name: Entries below 1024 are a device's own particles; entry 1024 + k * 64 + r is row r of its k-th received cell in the order of the steps. The table is cut into tiles of 64 rows; a device's particle r, of own tile t = r // 64, has all its neighbours in own tile t, own tile (t + 1) mod (16), or received tile t mod (8), the rows from 1024 + that tile's number * 64 on. `send_list`: indices of the sending device's own particles. `cluster`: cluster numbers count within the particle's group of gz devices.
All inputs are finite; a program needn't handle non-finite values.
Results may differ from the reference program's by a relative error of at most 0.025.
Values may be sent and summed in bfloat16 or wider, within the bound.
A program may use at most 128 MiB of HBM per device.

```python
import jax
import jax.numpy as jnp
from jax import lax

WIDTH = 128
NEIGH = 16
PART_DEV = 1024
GHOST = 64
TILE = 64
CLUSTERS = 256
PARTICLES = 262144
N_GX = 8
N_GY = 8
N_GZ = 4
DEVICES = 256


def draw_neighbours(key, part):
    tile_count = PART_DEV // TILE
    local_rows = jnp.arange(PARTICLES, dtype=jnp.int32) % PART_DEV
    owning = (local_rows // TILE)[:, None]
    window_slot = jax.random.randint(key, (PARTICLES, NEIGH), 0, 3 * TILE, dtype=jnp.int32)
    offset = window_slot % TILE
    own_row = owning * TILE + offset
    next_row = (owning + 1) % tile_count * TILE + offset
    ghost_row = PART_DEV + owning % (tile_count // 2) * TILE + offset
    picked = jnp.where(window_slot < TILE, own_row, jnp.where(window_slot < 2 * TILE, next_row, ghost_row))
    return picked.astype(jnp.int32)


def plant(drawn, rng, smallest, top_value):
    spot = [jax.random.randint(jax.random.fold_in(rng, axis), (), 0, length) for axis, length in enumerate(drawn.shape)]
    widest = drawn.shape.index(max(drawn.shape))
    beside = spot[:widest] + [(spot[widest] + 1) % drawn.shape[widest]] + spot[widest + 1:]
    return drawn.at[tuple(spot)].set(smallest).at[tuple(beside)].set(top_value)


def levels(key, shape, cuts, low, top_value):
    factor_of = 1.0
    for position, blocks in cuts:
        heights = jax.random.uniform(jax.random.fold_in(jax.random.fold_in(key, 6), position), (blocks,), jnp.float32, low / len(cuts), top_value / len(cuts))
        factor_of = factor_of * jnp.repeat(jnp.exp(heights), shape[position] // blocks).reshape((-1,) + (1,) * (len(shape) - 1 - position))
    return factor_of


def noise(rng, shape, width, limit, shards=(), kind=jnp.bfloat16):
    drawn = width * jax.random.normal(rng, shape, jnp.float32)
    if shards:
        drawn = drawn * levels(rng, shape, shards, -0.22, 0.18)
    return jnp.clip(drawn, -limit, limit).astype(kind)


def setup_inputs(seed: int = 0) -> dict:
    seeds = jax.random.split(jax.random.key(seed), 16)
    latents = noise(seeds[0], (PARTICLES, WIDTH), 1.0, 6.0, ((0, 256),))
    grad_mixed = noise(seeds[1], (PARTICLES, WIDTH), 1.0, 6.0, ((0, 256),))
    neighbours = draw_neighbours(jax.random.fold_in(seeds[15], 71), 0)
    send_list = plant(jax.random.randint(seeds[3], (4 * DEVICES, GHOST), 0, PART_DEV), jax.random.fold_in(seeds[3], 1), 0, PART_DEV - 1).astype(jnp.int32)
    cluster = plant(jax.random.randint(seeds[4], (PARTICLES,), 0, CLUSTERS), jax.random.fold_in(seeds[4], 1), 0, CLUSTERS - 1).astype(jnp.int32)
    w_send = noise(seeds[5], (WIDTH, WIDTH), WIDTH ** -0.5, 0.5)
    w_recv = noise(seeds[6], (WIDTH, WIDTH), WIDTH ** -0.5, 0.5)
    w_edge = noise(seeds[7], (WIDTH, WIDTH), WIDTH ** -0.5, 0.5)
    edge_gain = jnp.clip(1.0 + 0.18 * jax.random.normal(seeds[8], (WIDTH,), jnp.float32), 0.1, 1.9)
    w_self = noise(seeds[9], (WIDTH, WIDTH), WIDTH ** -0.5, 0.5)
    w_agg = noise(seeds[10], (WIDTH, WIDTH), WIDTH ** -0.5, 0.5)
    w_node = noise(seeds[11], (WIDTH, WIDTH), WIDTH ** -0.5, 0.5)
    node_gain = jnp.clip(1.0 + 0.18 * jax.random.normal(seeds[12], (WIDTH,), jnp.float32), 0.1, 1.9)
    w_pool_in = noise(seeds[13], (WIDTH, WIDTH), (4 * WIDTH) ** -0.5, 0.25)
    w_pool_out = noise(seeds[14], (WIDTH, WIDTH), WIDTH ** -0.5, 0.5)
    return dict(latents=latents, grad_mixed=grad_mixed, neighbours=neighbours, send_list=send_list, cluster=cluster, w_send=w_send, w_recv=w_recv, w_edge=w_edge, edge_gain=edge_gain, w_self=w_self, w_agg=w_agg, w_node=w_node, node_gain=node_gain, w_pool_in=w_pool_in, w_pool_out=w_pool_out)


EPS = 1e-05

def matmul_f32(left, right):
    return jnp.dot(left, right, preferred_element_type=jnp.float32)

def silu_slope(values):
    logistic = jax.nn.sigmoid(values)
    return logistic * (1.0 + values * (1.0 - logistic))

def norm_rows(values):
    centred = values - lax.optimization_barrier(jnp.mean(values, axis=-1, keepdims=True))
    inv_std = lax.rsqrt(lax.optimization_barrier(jnp.mean(centred * centred, axis=-1, keepdims=True)) + EPS)
    return (centred * inv_std, inv_std)

def norm_back(grad_normed, normed, inv_std):
    first_mean = lax.optimization_barrier(jnp.mean(grad_normed, axis=-1, keepdims=True))
    second_mean = lax.optimization_barrier(jnp.mean(grad_normed * normed, axis=-1, keepdims=True))
    return (grad_normed - first_mean - normed * second_mean) * inv_std

def matrix_rescale(mats):
    return mats * lax.rsqrt(lax.optimization_barrier(jnp.mean(mats * mats, axis=(1, 2), keepdims=True)) + 1e-06)

def block_split(row_count):
    block_rows = min(512, row_count)
    return (block_rows, row_count // block_rows)

def edge_block(proj_ext, recv_block, index_block, w_edge):
    feat_width = proj_ext.shape[1]
    pre_edge = proj_ext[index_block].astype(jnp.float32) + recv_block[:, None, :].astype(jnp.float32)
    pre_edge = pre_edge.reshape(-1, feat_width)
    act_edge = jax.nn.silu(pre_edge).astype(jnp.bfloat16)
    message = matmul_f32(act_edge, w_edge)
    normed, inv_std = norm_rows(message)
    return (pre_edge, act_edge, normed, inv_std)

def fine_forward(latents, proj_ext, neighbours, w_recv, w_edge, edge_gain, w_self, w_agg, w_node, node_gain):
    row_count, feat_width = latents.shape
    block_rows, blocks = block_split(row_count)
    recv_rows = matmul_f32(latents, w_recv).astype(jnp.bfloat16)

    def one_block(inputs):
        index_block, recv_block = inputs
        pre_edge, act_edge, normed, inv_std = edge_block(proj_ext, recv_block, index_block, w_edge)
        return (normed * edge_gain).reshape(block_rows, -1, feat_width).sum(axis=1)
    gathered = lax.map(one_block, (neighbours.reshape(blocks, block_rows, -1), recv_rows.reshape(blocks, block_rows, feat_width)))
    agg_rows = gathered.reshape(row_count, feat_width).astype(jnp.bfloat16)
    pre_node = matmul_f32(latents, w_self) + matmul_f32(agg_rows, w_agg)
    act_node = jax.nn.silu(pre_node).astype(jnp.bfloat16)
    normed_node, inv_node = norm_rows(matmul_f32(act_node, w_node))
    fine_latents = (latents.astype(jnp.float32) + normed_node * node_gain).astype(jnp.bfloat16)
    return (fine_latents, (recv_rows, agg_rows, pre_node, act_node, normed_node, inv_node))

def fine_backward(grad_fine, latents, proj_ext, neighbours, saved_state, w_send, w_recv, w_edge, edge_gain, w_self, w_agg, w_node, node_gain):
    recv_rows, agg_rows, pre_node, act_node, normed_node, inv_node = saved_state
    row_count, feat_width = latents.shape
    neigh_count = neighbours.shape[1]
    block_rows, blocks = block_split(row_count)
    grad_node_gain = lax.optimization_barrier(jnp.sum(grad_fine * normed_node, axis=0))
    grad_out = norm_back(grad_fine * node_gain, normed_node, inv_node).astype(jnp.bfloat16)
    grad_w_node = matmul_f32(act_node.T, grad_out)
    grad_pre_node = (matmul_f32(grad_out, w_node.T) * silu_slope(pre_node)).astype(jnp.bfloat16)
    grad_w_self = matmul_f32(latents.T, grad_pre_node)
    grad_w_agg = matmul_f32(agg_rows.T, grad_pre_node)
    grad_lat = grad_fine + matmul_f32(grad_pre_node, w_self.T)
    grad_agg = matmul_f32(grad_pre_node, w_agg.T)

    def one_block(carried, inputs):
        grad_proj, grad_w_edge, grad_edge_gain = carried
        index_block, recv_block, agg_block = inputs
        pre_edge, act_edge, normed, inv_std = edge_block(proj_ext, recv_block, index_block, w_edge)
        grad_message = jnp.broadcast_to(agg_block[:, None, :], (block_rows, neigh_count, feat_width)).reshape(-1, feat_width)
        grad_edge_gain = grad_edge_gain + lax.optimization_barrier(jnp.sum(grad_message * normed, axis=0))
        grad_edge = norm_back(grad_message * edge_gain, normed, inv_std).astype(jnp.bfloat16)
        grad_w_edge = grad_w_edge + matmul_f32(act_edge.T, grad_edge)
        grad_pre_b = (matmul_f32(grad_edge, w_edge.T) * silu_slope(pre_edge)).astype(jnp.bfloat16)
        grad_pre = lax.optimization_barrier(grad_pre_b).astype(jnp.float32)
        grad_proj = grad_proj.at[index_block.reshape(-1)].add(grad_pre)
        grad_recv = grad_pre.reshape(block_rows, neigh_count, feat_width).sum(axis=1)
        return ((grad_proj, grad_w_edge, grad_edge_gain), grad_recv)
    initial = (jnp.zeros(proj_ext.shape, jnp.float32), jnp.zeros((feat_width, feat_width), jnp.float32), jnp.zeros((feat_width,), jnp.float32))
    scanned = (neighbours.reshape(blocks, block_rows, -1), recv_rows.reshape(blocks, block_rows, feat_width), grad_agg.reshape(blocks, block_rows, feat_width))
    (grad_proj, grad_w_edge, grad_edge_gain), grad_recv = lax.scan(one_block, initial, scanned)
    grad_recv = grad_recv.reshape(row_count, feat_width).astype(jnp.bfloat16)
    grad_w_recv = matmul_f32(latents.T, grad_recv)
    grad_lat = grad_lat + matmul_f32(grad_recv, w_recv.T)
    grad_proj = grad_proj.astype(jnp.bfloat16)
    grad_w_send = matmul_f32(latents.T, grad_proj[:row_count])
    grad_lat = grad_lat + matmul_f32(grad_proj[:row_count], w_send.T)
    matrices = (grad_w_send, grad_w_recv, grad_w_edge, grad_w_self, grad_w_agg, grad_w_node)
    return (grad_lat, grad_proj[row_count:], matrices, (grad_edge_gain, grad_node_gain))

def cluster_forward(pooled, w_pool_in, w_pool_out):
    pooled_b = pooled.astype(jnp.bfloat16)
    pre_pool = matmul_f32(pooled_b, w_pool_in)
    act_pool = jax.nn.silu(pre_pool).astype(jnp.bfloat16)
    delta_rows = matmul_f32(act_pool, w_pool_out).astype(jnp.bfloat16)
    return (pooled_b, pre_pool, act_pool, delta_rows)

def cluster_backward(grad_delta, pre_pool, w_pool_in, w_pool_out):
    grad_delta_b = grad_delta.astype(jnp.bfloat16)
    grad_pre_pool = (matmul_f32(grad_delta_b, w_pool_out.T) * silu_slope(pre_pool)).astype(jnp.bfloat16)
    grad_pooled = matmul_f32(grad_pre_pool, w_pool_in.T).astype(jnp.bfloat16)
    return (grad_delta_b, grad_pre_pool, grad_pooled)

def rim_pieces(cell_rows):
    return jnp.stack([jnp.roll(cell_rows[:, :, :, 1, 0], 1, 0), jnp.roll(cell_rows[:, :, :, 1, 1], 1, 0), jnp.roll(cell_rows[:, :, :, 0, 0], -1, 0), jnp.roll(cell_rows[:, :, :, 0, 1], -1, 0), jnp.roll(cell_rows[:, :, :, 0, 1], 1, 1), jnp.roll(cell_rows[:, :, :, 1, 1], 1, 1), jnp.roll(cell_rows[:, :, :, 0, 0], -1, 1), jnp.roll(cell_rows[:, :, :, 1, 0], -1, 1)], axis=3)

def return_pieces(pieces):
    first_cell = jnp.roll(pieces[:, :, :, 2], 1, 0) + jnp.roll(pieces[:, :, :, 6], 1, 1)
    second_cell = jnp.roll(pieces[:, :, :, 3], 1, 0) + jnp.roll(pieces[:, :, :, 4], -1, 1)
    third_cell = jnp.roll(pieces[:, :, :, 0], -1, 0) + jnp.roll(pieces[:, :, :, 7], 1, 1)
    fourth_cell = jnp.roll(pieces[:, :, :, 1], -1, 0) + jnp.roll(pieces[:, :, :, 5], -1, 1)
    return jnp.stack([first_cell, second_cell, third_cell, fourth_cell], axis=3)

def reference(latents, grad_mixed, neighbours, send_list, cluster, w_send, w_recv, w_edge, edge_gain, w_self, w_agg, w_node, node_gain, w_pool_in, w_pool_out):
    dev_count = N_GX * N_GY * N_GZ
    group_count = N_GX * N_GY
    lat_all = latents.reshape(dev_count, PART_DEV, WIDTH)
    cot_all = grad_mixed.reshape(dev_count, PART_DEV, WIDTH)
    neigh_all = neighbours.reshape(dev_count, PART_DEV, NEIGH)
    send_all = send_list.reshape(dev_count, 4 * GHOST)
    clus_all = cluster.reshape(dev_count, PART_DEV)
    labels = jnp.arange(CLUSTERS, dtype=jnp.int32)

    def pick_rows(table, picks):
        return table[picks]
    cell_rows = jax.vmap(pick_rows)(lat_all, send_all).reshape(N_GX, N_GY, N_GZ, 2, 2, GHOST, WIDTH)
    ghost_all = rim_pieces(cell_rows).reshape(dev_count, 8 * GHOST, WIDTH)

    def projections(own_lat, ghost_lat):
        return jnp.concatenate([matmul_f32(own_lat, w_send).astype(jnp.bfloat16), matmul_f32(ghost_lat, w_send).astype(jnp.bfloat16)], axis=0)

    def forward_one(inputs):
        own_lat, ghost_lat, neigh_dev = inputs
        return fine_forward(own_lat, projections(own_lat, ghost_lat), neigh_dev, w_recv, w_edge, edge_gain, w_self, w_agg, w_node, node_gain)[0]
    fine_all = lax.map(forward_one, (lat_all, ghost_all, neigh_all))

    def onehot_of(clus_dev):
        return (clus_dev[:, None] == labels[None, :]).astype(jnp.bfloat16)

    def pool_one(inputs):
        values, clus_dev = inputs
        return matmul_f32(onehot_of(clus_dev).T, values)
    pooled = lax.map(pool_one, (fine_all, clus_all)).reshape(group_count, N_GZ, CLUSTERS, WIDTH).sum(axis=1)
    pooled_b, pre_pool, act_pool, delta_rows = jax.vmap(cluster_forward, (0, None, None))(pooled, w_pool_in, w_pool_out)
    group_of = jnp.arange(dev_count, dtype=jnp.int32) // N_GZ
    delta_dev = delta_rows[group_of]

    def unpool_one(inputs):
        values, clus_dev, delta_one = inputs
        return (values.astype(jnp.float32) + matmul_f32(onehot_of(clus_dev), delta_one)).astype(jnp.bfloat16)
    mixed_out = lax.map(unpool_one, (fine_all, clus_all, delta_dev))
    grad_delta = lax.map(pool_one, (cot_all, clus_all)).reshape(group_count, N_GZ, CLUSTERS, WIDTH).sum(axis=1)
    grad_delta_b, grad_pre_pool, grad_pooled = jax.vmap(cluster_backward, (0, 0, None, None))(grad_delta, pre_pool, w_pool_in, w_pool_out)
    grad_pool_in = jnp.einsum('gcd,gce->de', pooled_b.astype(jnp.float32), grad_pre_pool.astype(jnp.float32), precision=lax.Precision.HIGHEST)
    grad_pool_out = jnp.einsum('gcd,gce->de', act_pool.astype(jnp.float32), grad_delta_b.astype(jnp.float32), precision=lax.Precision.HIGHEST)
    grad_pooled_dev = grad_pooled[group_of]

    def backward_one(carried, inputs):
        mats_sum, gains_sum = carried
        own_lat, ghost_lat, neigh_dev, clus_dev, cot_dev, pooled_grad = inputs
        proj_ext = projections(own_lat, ghost_lat)
        fine_latents, saved_state = fine_forward(own_lat, proj_ext, neigh_dev, w_recv, w_edge, edge_gain, w_self, w_agg, w_node, node_gain)
        grad_fine = cot_dev.astype(jnp.float32) + matmul_f32(onehot_of(clus_dev), pooled_grad)
        grad_lat, grad_ghost, matrices, gains = fine_backward(grad_fine, own_lat, proj_ext, neigh_dev, saved_state, w_send, w_recv, w_edge, edge_gain, w_self, w_agg, w_node, node_gain)
        ghost_send = matmul_f32(ghost_lat.T, grad_ghost)
        ghost_back = matmul_f32(grad_ghost, w_send.T)
        mats_sum = mats_sum + jnp.stack(matrices) + jnp.stack([ghost_send] + [jnp.zeros_like(ghost_send)] * 5)
        gains_sum = gains_sum + jnp.stack(gains)
        return ((mats_sum, gains_sum), (grad_lat, ghost_back))
    initial = (jnp.zeros((6, WIDTH, WIDTH), jnp.float32), jnp.zeros((2, WIDTH), jnp.float32))
    (mats_sum, gains_sum), (grad_lat_all, ghost_back) = lax.scan(backward_one, initial, (lat_all, ghost_all, neigh_all, clus_all, cot_all, grad_pooled_dev))
    totals = return_pieces(ghost_back.reshape(N_GX, N_GY, N_GZ, 8, GHOST, WIDTH)).reshape(dev_count, 4 * GHOST, WIDTH)

    def add_back(grad_dev, picks, total_rows):
        return grad_dev.at[picks].add(total_rows)
    grad_lat_all = jax.vmap(add_back)(grad_lat_all, send_all, totals)
    grad_scale = float(dev_count * PART_DEV) ** (-0.5)
    grad_matrices = matrix_rescale(jnp.concatenate([mats_sum, jnp.stack([grad_pool_in, grad_pool_out])], axis=0))
    grad_gains = gains_sum * grad_scale
    return (mixed_out.reshape(-1, WIDTH), grad_lat_all.reshape(-1, WIDTH), grad_matrices, grad_gains)
```

```python
import functools

import jax
import jax.numpy as jnp
from jax import lax
from jax.experimental import pallas as pl
from jax.experimental.pallas import tpu as pltpu
from jax.sharding import PartitionSpec as P

EPS = 1e-05
W = 128
ROWS = 1024
NEIGH = 16
TILE = 64
PAIRS = ROWS // W
GHOSTS = 512
CLUSTERS = 256
SLOTS = 192
CHUNK = 256
STEPS = TILE * NEIGH // CHUNK
GAIN_ROWS = 16
F32 = jnp.float32
BF16 = jnp.bfloat16
MESH = pl.DeviceIdType.MESH


def mm(a, b):
    return lax.dot_general(a, b, (((1,), (0,)), ((), ())), preferred_element_type=F32)


def nt(a, b):
    return lax.dot_general(a, b, (((1,), (1,)), ((), ())), preferred_element_type=F32)


def sigmoid(v):
    return 0.5 * jnp.tanh(0.5 * v) + 0.5


def mean0(v):
    return jnp.sum(v, axis=0, keepdims=True) * (1.0 / W)


def norm_cols(z):
    centred = z - mean0(z)
    inv = lax.rsqrt(mean0(centred * centred) + EPS)
    return centred * inv, inv


def low_half():
    return lax.broadcasted_iota(jnp.int32, (W, W), 1) < TILE


def swap(v):
    return pltpu.roll(v, TILE, 1)


def spread_halves(block, low):
    other = swap(block)
    return jnp.where(low, block, other), jnp.where(low, other, block)


def column_of(row):
    return jnp.transpose(jnp.broadcast_to(row, (W, W)))


def kernel(sizes, *refs):
    (lat, gm, nb, send, clus, w_send, w_recv, w_edge, w_self, w_agg, w_node, w_pin, w_pout, egain, ngain) = refs[:15]
    mixed_o, grad_o, mats_o, gains_o = refs[15:19]
    (sbuf, ghost, ret, backbuf, pg, pf, early, early_in, early_mid, early_out, late, late_in, late_mid, late_out,
     lat_t, gm_t, oh_send, oh_clus, tab, tab_sh, gtab, gtab_sh, recv_t, wsa_t,
     oh_all, act_all, slope_all, norm_all, inv_all, sum_t, agg_t, an_t, nslope_t, nn_t, ninv_t, fine_t, gfine_t,
     gy_t, gpn_t, gc_t, grecv_t, gz_tmp, gp_tmp, gp_own, gp_ghost, dw_edge, sums) = refs[19:66]
    (halo_s, halo_r, ret_s, ret_r, pg_s, pg_r, pf_s, pf_r,
     e1s, e1r, e2s, e2r, e3s, e3r, l1s, l1r, l2s, l2r, l3s, l3r) = refs[66:]
    n_x, n_y, n_z = sizes
    n_a, n_b = n_x * n_z, n_y
    c_rows = 4 * W // n_a
    gx, gy, gz = lax.axis_index("gx"), lax.axis_index("gy"), lax.axis_index("gz")
    x_up = (lax.rem(gx + 1, n_x), gy, gz)
    x_low = (lax.rem(gx + n_x - 1, n_x), gy, gz)
    y_up = (gx, lax.rem(gy + 1, n_y), gz)
    y_low = (gx, lax.rem(gy + n_y - 1, n_y), gz)
    rank_a = ((gx // 2) * 2 + lax.rem(gy, 2)) * n_z + gz
    rank_b = lax.rem(gx, 2) * (n_y // 2) + gy // 2

    def z_peer(k):
        return lax.rem(gz + k, n_z)

    def a_peer(k):
        return lax.rem(rank_a + k, n_a)

    def a_dev(r):
        yc = r // n_z
        return ((yc // 2) * 2 + lax.rem(gx, 2), (gy // 2) * 2 + lax.rem(yc, 2), lax.rem(r, n_z))

    def b_peer(k):
        return lax.rem(rank_b + k, n_b)

    def b_dev(r):
        return ((gx // 2) * 2 + r // (n_y // 2), lax.rem(r, n_y // 2) * 2 + lax.rem(gy, 2), gz)

    def remote(src, dst, s, r, dev):
        return pltpu.make_async_remote_copy(
            src_ref=src, dst_ref=dst, send_sem=s, recv_sem=r, device_id=dev, device_id_type=MESH
        )

    def drain(ref, sem):
        pltpu.make_async_copy(ref, ref, sem).wait()

    barrier = pltpu.get_barrier_semaphore()
    for dev in (x_up, x_low, y_up, y_low):
        pl.semaphore_signal(barrier, inc=1, device_id=dev, device_id_type=MESH)

    def greet_a(k, c):
        pl.semaphore_signal(barrier, inc=1, device_id=a_dev(a_peer(k)), device_id_type=MESH)
        return c

    def greet_b(k, c):
        pl.semaphore_signal(barrier, inc=1, device_id=b_dev(b_peer(k)), device_id_type=MESH)
        return c

    lax.fori_loop(1, n_a, greet_a, 0)
    lax.fori_loop(1, n_b, greet_b, 0)

    lane_row = lax.broadcasted_iota(jnp.int32, (TILE, W), 1)
    send_f = send[...].astype(F32)
    for q in range(4):
        col = jnp.transpose(jnp.broadcast_to(send_f[q : q + 1, :], (W, TILE))).astype(jnp.int32)
        for b in range(PAIRS):
            hot = jnp.where(col == lane_row + b * W, 1.0, 0.0).astype(BF16)
            oh_send[q * TILE : (q + 1) * TILE, b * W : (b + 1) * W] = hot
    cells = mm(oh_send[...], lat[...]).astype(BF16)
    for slot, q in enumerate((2, 3, 0, 1, 1, 3, 0, 2)):
        sbuf[slot * TILE : (slot + 1) * TILE, :] = cells[q * TILE : (q + 1) * TILE, :]
    pl.semaphore_wait(barrier, 4 + n_a - 1 + n_b - 1)
    halo_to = (x_up, x_low, y_up, y_low)
    halo = [
        remote(sbuf.at[pl.ds(q * W, W)], ghost.at[pl.ds(q * W, W)], halo_s.at[q], halo_r.at[q], halo_to[q])
        for q in range(4)
    ]
    for c in halo:
        c.start()

    eye = jnp.where(
        lax.broadcasted_iota(jnp.int32, (W, W), 0) == lax.broadcasted_iota(jnp.int32, (W, W), 1), 1.0, 0.0
    ).astype(BF16)
    gm_t[...] = nt(eye, gm[...]).astype(BF16)
    cl_id = lax.broadcasted_iota(jnp.int32, (CLUSTERS, W), 0)
    for b in range(PAIRS):
        oh_clus[:, b * W : (b + 1) * W] = jnp.where(clus[:, b * W : (b + 1) * W] == cl_id, 1.0, 0.0).astype(BF16)

    def pool_send(buf, sems_s, sems_r):
        def go(k, c):
            to = (gx, gy, z_peer(k))
            remote(buf.at[gz], buf.at[gz], sems_s.at[k], sems_r.at[gz], to).start()
            return c

        lax.fori_loop(1, n_z, go, 0)

    def pool_wait(buf, sems_s, sems_r):
        def go(k, c):
            src = lax.rem(gz + n_z - k, n_z)
            remote(buf.at[gz], buf.at[src], sems_s.at[k], sems_r.at[src], (gx, gy, z_peer(k))).wait_recv()
            return c

        lax.fori_loop(1, n_z, go, 0)

    def pool_done(buf, sems_s, sems_r):
        def go(k, c):
            remote(buf.at[gz], buf.at[gz], sems_s.at[k], sems_r.at[gz], (gx, gy, z_peer(k))).wait_send()
            return c

        lax.fori_loop(1, n_z, go, 0)

    pg[gz] = nt(gm_t[...], oh_clus[...]).astype(BF16)
    pool_send(pg, pg_s, pg_r)

    lat_t[...] = nt(eye, lat[...]).astype(BF16)
    we_t = jnp.transpose(w_edge[...].astype(F32)).astype(BF16)
    wsend_t = jnp.transpose(w_send[...].astype(F32)).astype(BF16)
    wrecv_t = jnp.transpose(w_recv[...].astype(F32)).astype(BF16)
    wnode_t = jnp.transpose(w_node[...].astype(F32)).astype(BF16)
    wsa_t[:, :W] = jnp.transpose(w_self[...].astype(F32)).astype(BF16)
    wsa_t[:, W:] = jnp.transpose(w_agg[...].astype(F32)).astype(BF16)
    tab[...] = mm(wsend_t, lat_t[...]).astype(BF16)
    lat_roll = jnp.concatenate([lat[TILE:, :], lat[:TILE, :]], axis=0)
    tab_sh[...] = nt(wsend_t, lat_roll).astype(BF16)
    recv_t[...] = mm(wrecv_t, lat_t[...]).astype(BF16).astype(F32)
    eg = column_of(egain[...])
    ng = column_of(ngain[...])

    for c in halo:
        c.wait()
    gh = ghost[...]
    gtab[...] = nt(wsend_t, gh).astype(BF16)
    gtab_sh[...] = nt(wsend_t, jnp.concatenate([gh[TILE:, :], gh[:TILE, :]], axis=0)).astype(BF16)

    def forward(u, carry):
        low = low_half()
        slot_id = lax.broadcasted_iota(jnp.int32, (SLOTS, W), 0)
        at = pl.multiple_of(u * W, W)
        at_g = pl.multiple_of(lax.rem(u, GHOSTS // W) * W, W)
        picks = nb[:, pl.ds(at, W)]
        low8 = low[:8, :]
        first, second = picks[:8, :], picks[8:, :]
        picks_of = (jnp.where(low8, first, swap(second)), jnp.where(low8, swap(first), second))
        recv_of = spread_halves(recv_t[:, pl.ds(at, W)], low)
        sums_of = []
        for half in range(2):
            t = 2 * u + half
            chosen = picks_of[half]
            local = jnp.where(chosen >= ROWS, (chosen & (TILE - 1)) + 2 * TILE, (chosen - t * TILE) & (ROWS - 1))
            own, far = (tab, gtab) if half == 0 else (tab_sh, gtab_sh)
            window = jnp.concatenate([own[:, pl.ds(at, W)], far[:, pl.ds(at_g, TILE)]], axis=1)
            total = None
            for q in range(STEPS):
                lanes = slice(q * CHUNK, (q + 1) * CHUNK)
                hot = jnp.concatenate(
                    [jnp.where(local[c : c + 1, :] == slot_id, 1.0, 0.0).astype(BF16) for c in (2 * q, 2 * q + 1)], axis=1
                )
                oh_all[t, :, lanes] = hot
                pre = mm(window, hot) + jnp.concatenate([recv_of[half]] * 2, axis=1)
                s = sigmoid(pre)
                act = pre * s
                act_b = act.astype(BF16)
                act_all[t, :, lanes] = act_b
                slope_all[t, :, lanes] = (s + act * (1.0 - s)).astype(BF16)
                normed, inv = norm_cols(mm(we_t, act_b))
                norm_all[t, :, lanes] = normed.astype(BF16)
                inv_all[t, :, lanes] = inv
                part = normed[:, :W] + normed[:, W:]
                total = part if total is None else total + part
            sums_of.append(total + swap(total))
        total = jnp.where(low, sums_of[0], sums_of[1])
        sum_t[:, pl.ds(at, W)] = total
        agg_b = (total * eg).astype(BF16)
        agg_t[:, pl.ds(at, W)] = agg_b
        lat_b = lat_t[:, pl.ds(at, W)]
        pn = mm(wsa_t[...], jnp.concatenate([lat_b, agg_b], axis=0))
        s = sigmoid(pn)
        an = pn * s
        an_b = an.astype(BF16)
        an_t[:, pl.ds(at, W)] = an_b
        nslope_t[:, pl.ds(at, W)] = s + an * (1.0 - s)
        nn, ninv = norm_cols(mm(wnode_t, an_b))
        nn_t[:, pl.ds(at, W)] = nn
        ninv_t[:, pl.ds(at, W)] = ninv
        fine_t[:, pl.ds(at, W)] = (lat_b.astype(F32) + nn * ng).astype(BF16)
        return carry

    lax.fori_loop(0, PAIRS, forward, 0)

    pf[gz] = nt(fine_t[...], oh_clus[...]).astype(BF16)
    pool_send(pf, pf_s, pf_r)
    wpin_t = jnp.transpose(w_pin[...].astype(F32)).astype(BF16)
    wpout_t = jnp.transpose(w_pout[...].astype(F32)).astype(BF16)
    pool_wait(pg, pg_s, pg_r)
    gd = pg[0].astype(F32)
    for k in range(1, n_z):
        gd = gd + pg[k].astype(F32)
    gd_b = gd.astype(BF16)
    gac = mm(w_pout[...], gd_b)
    pool_wait(pf, pf_s, pf_r)
    pooled = pf[0].astype(F32)
    for k in range(1, n_z):
        pooled = pooled + pf[k].astype(F32)
    pooled_b = pooled.astype(BF16)
    pc = mm(wpin_t, pooled_b)
    s = sigmoid(pc)
    ac = pc * s
    ac_b = ac.astype(BF16)
    delta_b = mm(wpout_t, ac_b).astype(BF16)
    gpc_b = (gac * (s + ac * (1.0 - s))).astype(BF16)
    gpool_b = mm(w_pin[...], gpc_b).astype(BF16)
    both = jnp.concatenate([delta_b, gpool_b], axis=0)
    dw_pin = nt(pooled_b, gpc_b) * (1.0 / n_z)
    dw_pout = nt(ac_b, gd_b) * (1.0 / n_z)

    sums[...] = jnp.zeros_like(sums)

    def node_back(u, carry):
        at = pl.multiple_of(u * W, W)
        added = mm(both, oh_clus[:, pl.ds(at, W)])
        mixed = fine_t[:, pl.ds(at, W)].astype(F32) + added[:W, :]
        mixed_o[pl.ds(at, W), :] = jnp.transpose(mixed).astype(BF16)
        gf = gm_t[:, pl.ds(at, W)].astype(F32) + added[W:, :]
        gfine_t[:, pl.ds(at, W)] = gf
        nn = nn_t[:, pl.ds(at, W)]
        sums[1] += gf * nn
        gn = gf * ng
        gy_b = ((gn - mean0(gn) - nn * mean0(gn * nn)) * ninv_t[:, pl.ds(at, W)]).astype(BF16)
        gy_t[:, pl.ds(at, W)] = gy_b
        gpn_b = (mm(w_node[...], gy_b) * nslope_t[:, pl.ds(at, W)]).astype(BF16)
        gpn_t[:, pl.ds(at, W)] = gpn_b
        ga = mm(w_agg[...], gpn_b)
        sums[0] += ga * sum_t[:, pl.ds(at, W)]
        g = ga * eg
        gc_t[:, pl.ds(at, W)] = g - mean0(g)
        return carry

    lax.fori_loop(0, PAIRS, node_back, 0)

    def put(buf, index, mat, width):
        per = W // c_rows
        buf[index * per : (index + 1) * per, :c_rows, :] = mat.reshape(per, c_rows, W).astype(BF16)

    def reduce_out(buf, into, s, r):
        into[rank_a] = buf[rank_a]

        def go(k, c):
            to = a_peer(k)
            remote(buf.at[to], into.at[rank_a], s, r, a_dev(to)).start()
            return c

        lax.fori_loop(1, n_a, go, 0)

    def reduce_mid(buf, into, mid, s, r, s2, r2):
        drain(into.at[pl.ds(0, n_a - 1)], r)
        total = into[0].astype(F32)
        for k in range(1, n_a):
            total = total + into[k].astype(F32)
        mid[rank_b] = total.astype(BF16)

        def go(k, c):
            remote(mid.at[rank_b], mid.at[rank_b], s2, r2, b_dev(b_peer(k))).start()
            return c

        lax.fori_loop(1, n_b, go, 0)

    def gather_out(mid, out, s2, r2, s3, r3):
        drain(mid.at[pl.ds(0, n_b - 1)], r2)
        total = mid[0].astype(F32)
        for k in range(1, n_b):
            total = total + mid[k].astype(F32)
        out[rank_a] = total.astype(BF16)

        def go(k, c):
            remote(out.at[rank_a], out.at[rank_a], s3, r3, a_dev(a_peer(k))).start()
            return c

        lax.fori_loop(1, n_a, go, 0)

    def finish(buf, mid, out, s, s2, s3, r3):
        drain(out.at[pl.ds(0, n_a - 1)], r3)
        drain(buf.at[pl.ds(0, n_a - 1)], s)
        drain(mid.at[pl.ds(0, n_b - 1)], s2)
        drain(out.at[pl.ds(0, n_a - 1)], s3)

    def row_sums(v):
        hi = v.astype(BF16)
        lo = (v - hi.astype(F32)).astype(BF16)
        ones = jnp.ones((GAIN_ROWS, W), BF16)
        return nt(ones, hi) + nt(ones, lo)

    dw_sa = nt(jnp.concatenate([lat_t[...], agg_t[...]], axis=0), gpn_t[...])
    put(early, 0, dw_sa[:W, :], c_rows)
    put(early, 1, dw_sa[W:, :], c_rows)
    put(early, 2, nt(an_t[...], gy_t[...]), c_rows)
    put(early, 3, dw_pin, c_rows)
    which = lax.broadcasted_iota(jnp.int32, (GAIN_ROWS, W), 0)
    gain_rows = jnp.where(which == 0, row_sums(sums[0]), row_sums(sums[1])).astype(BF16)
    for k in range(n_a):
        early[k, c_rows:, :] = gain_rows
    reduce_out(early, early_in, e1s, e1r)

    gp_own[...] = jnp.zeros_like(gp_own)
    gp_ghost[...] = jnp.zeros_like(gp_ghost)
    dw_edge[...] = jnp.zeros_like(dw_edge)

    def backward(u, carry):
        low = low_half()
        at = pl.multiple_of(u * W, W)
        at_g = pl.multiple_of(lax.rem(u, GHOSTS // W) * W, W)
        gc_of = spread_halves(gc_t[:, pl.ds(at, W)], low)
        back_of = []
        for half in range(2):
            t = 2 * u + half
            gc = jnp.concatenate([gc_of[half]] * 2, axis=1)
            total = None
            for q in range(STEPS):
                lanes = slice(q * CHUNK, (q + 1) * CHUNK)
                normed = norm_all[t, :, lanes].astype(F32)
                gz_b = ((gc - normed * mean0(gc * normed)) * inv_all[t, :, lanes]).astype(BF16)
                gz_tmp[half, :, lanes] = gz_b
                gpre = mm(w_edge[...], gz_b) * slope_all[t, :, lanes].astype(F32)
                gp_tmp[half, :, lanes] = gpre.astype(BF16)
                part = gpre[:, :W] + gpre[:, W:]
                total = part if total is None else total + part
            dw_edge[...] += nt(act_all[t], gz_tmp[half])
            window = nt(oh_all[t], gp_tmp[half])
            gp_own[pl.ds(at + half * TILE, W), :] += window[:W, :]
            gp_ghost[pl.ds(at_g + half * TILE, TILE), :] += window[W:, :]
            back_of.append(total + swap(total))
        grecv_t[:, pl.ds(at, W)] = jnp.where(low, back_of[0], back_of[1]).astype(BF16)
        return carry

    lax.fori_loop(0, PAIRS // 2, backward, 0)
    reduce_mid(early, early_in, early_mid, e1s, e1r, e2s, e2r)
    lax.fori_loop(PAIRS // 2, PAIRS, backward, 0)
    gather_out(early_mid, early_out, e2s, e2r, e3s, e3r)

    backbuf[...] = gp_ghost[...].astype(BF16)
    back_to = (x_low, x_up, y_low, y_up)
    back = [
        remote(backbuf.at[pl.ds(q * W, W)], ret.at[pl.ds(q * W, W)], ret_s.at[q], ret_r.at[q], back_to[q])
        for q in range(4)
    ]
    for c in back:
        c.start()

    gp_own[:TILE, :] += gp_own[ROWS:, :]
    own_b = gp_own[:ROWS, :].astype(BF16)
    ghost_t = nt(eye, ghost[...]).astype(BF16)
    put(late, 0, mm(lat_t[...], own_b) + mm(ghost_t, backbuf[...]), c_rows)
    put(late, 1, nt(lat_t[...], grecv_t[...]), c_rows)
    put(late, 2, dw_edge[...], c_rows)
    put(late, 3, dw_pout, c_rows)
    reduce_out(late, late_in, l1s, l1r)

    gfine_t[...] += (
        mm(w_self[...], gpn_t[...]) + mm(w_recv[...], grecv_t[...]) + nt(w_send[...], own_b)
    )
    for c in back:
        c.wait()
    side_a = jnp.concatenate([ret[q * TILE : (q + 1) * TILE, :] for q in (2, 3, 0, 1)], axis=0)
    side_b = jnp.concatenate([ret[q * TILE : (q + 1) * TILE, :] for q in (6, 4, 7, 5)], axis=0)
    ret_t = (nt(w_send[...], side_a) + nt(w_send[...], side_b)).astype(BF16)
    reduce_mid(late, late_in, late_mid, l1s, l1r, l2s, l2r)
    gfine_t[...] += mm(ret_t, oh_send[...])
    for b in range(PAIRS):
        grad_o[b * W : (b + 1) * W, :] = jnp.transpose(gfine_t[:, b * W : (b + 1) * W])
    gather_out(late_mid, late_out, l2s, l2r, l3s, l3r)

    def emit(out, index, place):
        per = W // c_rows
        mat = out[index * per : (index + 1) * per, :c_rows, :].astype(F32).reshape(W, W)
        mats_o[place] = mat * lax.rsqrt(jnp.mean(mat * mat, keepdims=True) + 1e-06)

    finish(early, early_mid, early_out, e1s, e2s, e3s, e3r)
    for index, place in enumerate((3, 4, 5, 6)):
        emit(early_out, index, place)
    scale = float(ROWS * n_x * n_y * n_z) ** (-0.5)
    gains_o[...] = early_out[0, c_rows : c_rows + 2, :].astype(F32) * scale
    pool_done(pg, pg_s, pg_r)
    pool_done(pf, pf_s, pf_r)
    finish(late, late_mid, late_out, l1s, l2s, l3s, l3r)
    for index, place in enumerate((0, 1, 2, 7)):
        emit(late_out, index, place)


def solution(mesh):
    sizes = tuple(mesh.shape[name] for name in ("gx", "gy", "gz"))
    n_a, n_b, n_z = sizes[0] * sizes[2], sizes[1], sizes[2]
    c_rows = 4 * W // n_a
    tiles = ROWS // TILE
    edges = TILE * NEIGH
    v = pltpu.VMEM
    dma = pltpu.SemaphoreType.DMA

    def reduce_bufs(rows):
        return [v((n_a, rows, W), BF16), v((n_a, rows, W), BF16), v((n_b, rows, W), BF16), v((n_a, rows, W), BF16)]

    scratch = [
        v((GHOSTS, W), BF16),
        v((GHOSTS, W), BF16),
        v((GHOSTS, W), BF16),
        v((GHOSTS, W), BF16),
        v((n_z, W, CLUSTERS), BF16),
        v((n_z, W, CLUSTERS), BF16),
        *reduce_bufs(c_rows + GAIN_ROWS),
        *reduce_bufs(c_rows),
        v((W, ROWS), BF16),
        v((W, ROWS), BF16),
        v((4 * TILE, ROWS), BF16),
        v((CLUSTERS, ROWS), BF16),
        v((W, ROWS), BF16),
        v((W, ROWS), BF16),
        v((W, GHOSTS), BF16),
        v((W, GHOSTS), BF16),
        v((W, ROWS), F32),
        v((W, 2 * W), BF16),
        v((tiles, SLOTS, edges), BF16),
        v((tiles, W, edges), BF16),
        v((tiles, W, edges), BF16),
        v((tiles, W, edges), BF16),
        v((tiles, 1, edges), F32),
        v((W, ROWS), F32),
        v((W, ROWS), BF16),
        v((W, ROWS), BF16),
        v((W, ROWS), F32),
        v((W, ROWS), F32),
        v((1, ROWS), F32),
        v((W, ROWS), BF16),
        v((W, ROWS), F32),
        v((W, ROWS), BF16),
        v((W, ROWS), BF16),
        v((W, ROWS), F32),
        v((W, ROWS), BF16),
        v((2, W, edges), BF16),
        v((2, W, edges), BF16),
        v((ROWS + TILE, W), F32),
        v((GHOSTS, W), F32),
        v((W, W), F32),
        v((2, W, W), F32),
        dma((4,)), dma((4,)), dma((4,)), dma((4,)),
        dma((n_z,)), dma((n_z,)), dma((n_z,)), dma((n_z,)),
        *[dma for _ in range(12)],
    ]

    def step(latents, grad_mixed, neighbours, send_list, cluster, w_send, w_recv, w_edge, edge_gain, w_self, w_agg,
             w_node, node_gain, w_pool_in, w_pool_out):
        return pl.pallas_call(
            functools.partial(kernel, sizes),
            out_shape=(
                jax.ShapeDtypeStruct((ROWS, W), BF16),
                jax.ShapeDtypeStruct((ROWS, W), F32),
                jax.ShapeDtypeStruct((8, W, W), F32),
                jax.ShapeDtypeStruct((2, W), F32),
            ),
            in_specs=[pl.BlockSpec(memory_space=pltpu.VMEM)] * 15,
            out_specs=tuple([pl.BlockSpec(memory_space=pltpu.VMEM)] * 4),
            scratch_shapes=scratch,
            compiler_params=pltpu.CompilerParams(
                collective_id=0, has_side_effects=True, vmem_limit_bytes=60 * 1024 * 1024
            ),
        )(latents, grad_mixed, neighbours.T, send_list, cluster.reshape(1, ROWS), w_send, w_recv, w_edge, w_self,
          w_agg, w_node, w_pool_in, w_pool_out, edge_gain.reshape(1, W), node_gain.reshape(1, W))

    rows = P(("gx", "gy", "gz"), None)
    in_specs = (rows, rows, rows, rows, P(("gx", "gy", "gz"))) + (P(),) * 10
    out_specs = (rows, rows, P(), P())
    return jax.shard_map(step, mesh=mesh, in_specs=in_specs, out_specs=out_specs, check_vma=False)
```

```python
import functools

import jax
import jax.numpy as jnp
from jax import lax
from jax.experimental import pallas as pl
from jax.experimental.pallas import tpu as pltpu
from jax.sharding import PartitionSpec as P

EPS = 1e-05
W = 128
ROWS = 1024
NEIGH = 16
TILE = 64
PAIRS = ROWS // W
GHOSTS = 512
CLUSTERS = 256
SLOTS = 192
CHUNK = 256
STEPS = TILE * NEIGH // CHUNK
NODE = 256
GAIN_ROWS = 16
F32 = jnp.float32
BF16 = jnp.bfloat16
MESH = pl.DeviceIdType.MESH


def mm(a, b):
    return lax.dot_general(a, b, (((1,), (0,)), ((), ())), preferred_element_type=F32)


def nt(a, b):
    return lax.dot_general(a, b, (((1,), (1,)), ((), ())), preferred_element_type=F32)


def sigmoid(v):
    return 0.5 * jnp.tanh(0.5 * v) + 0.5


def mean0(v):
    return jnp.sum(v, axis=0, keepdims=True) * (1.0 / W)


def norm_centred(centred):
    inv = lax.rsqrt(mean0(centred * centred) + EPS)
    return centred * inv, inv


def half_silu(h):
    t = jnp.tanh(h)
    up = 1.0 + t
    act = h * up
    return act, up + act * (1.0 - t)


def centred_pair(w):
    w_t = jnp.transpose(w.astype(F32))
    centred = w_t - mean0(w_t)
    high = centred.astype(BF16)
    return jnp.concatenate([high, (centred - high.astype(F32)).astype(BF16)], axis=1)


def twice(v):
    return jnp.concatenate([v, v], axis=0)


def one_hot(row, ids):
    wide = jnp.broadcast_to(row, (16, W)).astype(BF16)
    same = jnp.concatenate([wide] * (ids.shape[0] // 16), axis=0) == ids
    return jnp.where(same, jnp.ones((), BF16), jnp.zeros((), BF16))


def low_half():
    return lax.broadcasted_iota(jnp.int32, (W, W), 1) < TILE


def swap(v):
    return pltpu.roll(v, TILE, 1)


def spread_halves(block, low):
    other = swap(block)
    return jnp.where(low, block, other), jnp.where(low, other, block)


def column_of(row):
    return jnp.transpose(jnp.broadcast_to(row, (W, W)))


def kernel(sizes, *refs):
    far, near, in_sems = refs[:15], refs[-16:-1], refs[-1]
    (lat, gm, nb, send, clus, w_send, w_recv, w_edge, w_self, w_agg, w_node, w_pin, w_pout, egain, ngain) = near
    mixed_o, grad_o, mats_o, gains_o = refs[15:19]
    (sbuf, ghost, ret, backbuf, pg, pf, early, early_in, early_mid, early_out, late, late_in, late_mid, late_out,
     lat_t, gm_t, oh_send, oh_clus, tab, tab_sh, gtab, gtab_sh, recv_t, wsa_t, we_c, wn_c,
     oh_all, act_all, slope_all, norm_all, inv_all, sum_t, agg_t, an_t, nslope_t, nn_t, ninv_t, fine_t, gfine_t,
     gy_t, gpn_t, gc_t, grecv_t, gz_tmp, gp_tmp, gp_own, gp_ghost, dw_edge, sums) = refs[19:68]
    (halo_s, halo_r, ret_s, ret_r, pg_s, pg_r, pf_s, pf_r,
     e1s, e1r, e2s, e2r, e3s, e3r, l1s, l1r, l2s, l2r, l3s, l3r) = refs[68:-16]
    n_x, n_y, n_z = sizes
    n_a, n_b = n_x * n_z, n_y
    c_rows = 4 * W // n_a
    gx, gy, gz = lax.axis_index("gx"), lax.axis_index("gy"), lax.axis_index("gz")
    x_up = (lax.rem(gx + 1, n_x), gy, gz)
    x_low = (lax.rem(gx + n_x - 1, n_x), gy, gz)
    y_up = (gx, lax.rem(gy + 1, n_y), gz)
    y_low = (gx, lax.rem(gy + n_y - 1, n_y), gz)
    rank_a = ((gx // 2) * 2 + lax.rem(gy, 2)) * n_z + gz
    rank_b = lax.rem(gx, 2) * (n_y // 2) + gy // 2

    def z_peer(k):
        return lax.rem(gz + k, n_z)

    def a_peer(k):
        return lax.rem(rank_a + k, n_a)

    def a_dev(r):
        yc = r // n_z
        return ((yc // 2) * 2 + lax.rem(gx, 2), (gy // 2) * 2 + lax.rem(yc, 2), lax.rem(r, n_z))

    def b_peer(k):
        return lax.rem(rank_b + k, n_b)

    def b_dev(r):
        return ((gx // 2) * 2 + r // (n_y // 2), lax.rem(r, n_y // 2) * 2 + lax.rem(gy, 2), gz)

    def remote(src, dst, s, r, dev):
        return pltpu.make_async_remote_copy(
            src_ref=src, dst_ref=dst, send_sem=s, recv_sem=r, device_id=dev, device_id_type=MESH
        )

    def drain(ref, sem):
        pltpu.make_async_copy(ref, ref, sem).wait()

    loads = [pltpu.make_async_copy(a, b, in_sems.at[i]) for i, (a, b) in enumerate(zip(far, near))]
    for i in (3, 0, 1, 4, *range(5, 15), 2):
        loads[i].start()

    barrier = pltpu.get_barrier_semaphore()
    for dev in (x_up, x_low, y_up, y_low):
        pl.semaphore_signal(barrier, inc=1, device_id=dev, device_id_type=MESH)

    def greet_a(k, c):
        pl.semaphore_signal(barrier, inc=1, device_id=a_dev(a_peer(k)), device_id_type=MESH)
        return c

    def greet_b(k, c):
        pl.semaphore_signal(barrier, inc=1, device_id=b_dev(b_peer(k)), device_id_type=MESH)
        return c

    lax.fori_loop(1, n_a, greet_a, 0)
    lax.fori_loop(1, n_b, greet_b, 0)

    lane_row = lax.broadcasted_iota(jnp.int32, (TILE, W), 1)
    loads[3].wait()
    send_f = send[...].astype(F32)
    for q in range(4):
        col = jnp.transpose(jnp.broadcast_to(send_f[q : q + 1, :], (W, TILE))).astype(jnp.int32)
        for b in range(PAIRS):
            hot = jnp.where(col == lane_row + b * W, 1.0, 0.0).astype(BF16)
            oh_send[q * TILE : (q + 1) * TILE, b * W : (b + 1) * W] = hot
    loads[0].wait()
    cells = mm(oh_send[...], lat[...]).astype(BF16)
    for slot, q in enumerate((2, 3, 0, 1, 1, 3, 0, 2)):
        sbuf[slot * TILE : (slot + 1) * TILE, :] = cells[q * TILE : (q + 1) * TILE, :]
    pl.semaphore_wait(barrier, 4 + n_a - 1 + n_b - 1)
    halo_to = (x_up, x_low, y_up, y_low)
    halo = [
        remote(sbuf.at[pl.ds(q * W, W)], ghost.at[pl.ds(q * W, W)], halo_s.at[q], halo_r.at[q], halo_to[q])
        for q in range(4)
    ]
    for c in halo:
        c.start()

    eye = jnp.where(
        lax.broadcasted_iota(jnp.int32, (W, W), 0) == lax.broadcasted_iota(jnp.int32, (W, W), 1), 1.0, 0.0
    ).astype(BF16)
    loads[1].wait()
    loads[4].wait()
    gm_t[...] = nt(eye, gm[...]).astype(BF16)
    cl_id = lax.broadcasted_iota(jnp.int32, (CLUSTERS, W), 0).astype(F32).astype(BF16)
    clus_f = clus[...].astype(F32)
    for b in range(PAIRS):
        oh_clus[:, b * W : (b + 1) * W] = one_hot(clus_f[:, b * W : (b + 1) * W], cl_id)

    def pool_send(buf, sems_s, sems_r):
        def go(k, c):
            to = (gx, gy, z_peer(k))
            remote(buf.at[gz], buf.at[gz], sems_s.at[k], sems_r.at[gz], to).start()
            return c

        lax.fori_loop(1, n_z, go, 0)

    def pool_wait(buf, sems_s, sems_r):
        def go(k, c):
            src = lax.rem(gz + n_z - k, n_z)
            remote(buf.at[gz], buf.at[src], sems_s.at[k], sems_r.at[src], (gx, gy, z_peer(k))).wait_recv()
            return c

        lax.fori_loop(1, n_z, go, 0)

    def pool_done(buf, sems_s, sems_r):
        def go(k, c):
            remote(buf.at[gz], buf.at[gz], sems_s.at[k], sems_r.at[gz], (gx, gy, z_peer(k))).wait_send()
            return c

        lax.fori_loop(1, n_z, go, 0)

    pg[gz] = nt(gm_t[...], oh_clus[...]).astype(BF16)
    pool_send(pg, pg_s, pg_r)

    lat_t[...] = nt(eye, lat[...]).astype(BF16)
    for i in (*range(5, 15), 2):
        loads[i].wait()
    wsend_t = (jnp.transpose(w_send[...].astype(F32)) * 0.5).astype(BF16)
    wrecv_t = (jnp.transpose(w_recv[...].astype(F32)) * 0.5).astype(BF16)
    we_c[...] = centred_pair(w_edge[...])
    wn_c[...] = centred_pair(w_node[...])
    wsa_t[:, :W] = (jnp.transpose(w_self[...].astype(F32)) * 0.5).astype(BF16)
    wsa_t[:, W:] = (jnp.transpose(w_agg[...].astype(F32)) * 0.5).astype(BF16)
    w_edge_h = (w_edge[...].astype(F32) * 0.5).astype(BF16)
    w_node_h = (w_node[...].astype(F32) * 0.5).astype(BF16)
    tab[...] = mm(wsend_t, lat_t[...]).astype(BF16)
    lat_roll = jnp.concatenate([lat[TILE:, :], lat[:TILE, :]], axis=0)
    tab_sh[...] = nt(wsend_t, lat_roll).astype(BF16)
    recv_t[...] = mm(wrecv_t, lat_t[...]).astype(BF16).astype(F32)
    eg = column_of(egain[...])
    ng = column_of(ngain[...])

    def ghost_tables(first):
        part = slice(first, first + 2 * W)
        own = ghost[part, :]
        gtab[:, part] = nt(wsend_t, own).astype(BF16)
        gtab_sh[:, part] = nt(wsend_t, jnp.concatenate([own[TILE:, :], own[:TILE, :]], axis=0)).astype(BF16)

    def forward(u, carry):
        low = low_half()
        slot_id = lax.broadcasted_iota(jnp.int32, (SLOTS, W), 0).astype(F32).astype(BF16)
        at = pl.multiple_of(u * W, W)
        at_g = pl.multiple_of(lax.rem(u, GHOSTS // W) * W, W)
        picks = nb[:, pl.ds(at, W)]
        low8 = low[:8, :]
        first, second = picks[:8, :], picks[8:, :]
        picks_of = (jnp.where(low8, first, swap(second)), jnp.where(low8, swap(first), second))
        recv_of = spread_halves(recv_t[:, pl.ds(at, W)], low)
        sums_of = []
        for half in range(2):
            t = 2 * u + half
            chosen = picks_of[half]
            local = jnp.where(chosen >= ROWS, (chosen & (TILE - 1)) + 2 * TILE, (chosen - t * TILE) & (ROWS - 1))
            local = local.astype(F32)
            own, far = (tab, gtab) if half == 0 else (tab_sh, gtab_sh)
            window = jnp.concatenate([own[:, pl.ds(at, W)], far[:, pl.ds(at_g, TILE)]], axis=1)
            total = None
            for q in range(STEPS):
                lanes = slice(q * CHUNK, (q + 1) * CHUNK)
                hot = jnp.concatenate([one_hot(local[c : c + 1, :], slot_id) for c in (2 * q, 2 * q + 1)], axis=1)
                oh_all[t, :, lanes] = hot
                act, slope = half_silu(mm(window, hot) + jnp.concatenate([recv_of[half]] * 2, axis=1))
                act_b = act.astype(BF16)
                act_all[t, :, lanes] = act_b
                slope_all[t, :, lanes] = slope.astype(BF16)
                normed, inv = norm_centred(mm(we_c[...], twice(act_b)))
                norm_all[t, :, lanes] = normed.astype(BF16)
                inv_all[t, :, lanes] = inv
                part = normed[:, :W] + normed[:, W:]
                total = part if total is None else total + part
            sums_of.append(total + swap(total))
        total = jnp.where(low, sums_of[0], sums_of[1])
        sum_t[:, pl.ds(at, W)] = total
        agg_t[:, pl.ds(at, W)] = (total * eg).astype(BF16)
        return carry

    halo[2].wait()
    halo[3].wait()
    ghost_tables(2 * W)
    lax.fori_loop(0, PAIRS // 2, lambda k, c: forward((k // 2) * 4 + 2 + lax.rem(k, 2), c), 0)
    halo[0].wait()
    halo[1].wait()
    ghost_tables(0)
    lax.fori_loop(0, PAIRS // 2, lambda k, c: forward((k // 2) * 4 + lax.rem(k, 2), c), 0)

    def node_forward(u, carry):
        at = pl.multiple_of(u * NODE, NODE)
        lat_b = lat_t[:, pl.ds(at, NODE)]
        an, slope = half_silu(mm(wsa_t[...], jnp.concatenate([lat_b, agg_t[:, pl.ds(at, NODE)]], axis=0)))
        an_b = an.astype(BF16)
        an_t[:, pl.ds(at, NODE)] = an_b
        nslope_t[:, pl.ds(at, NODE)] = slope
        nn, ninv = norm_centred(mm(wn_c[...], twice(an_b)))
        nn_t[:, pl.ds(at, NODE)] = nn
        ninv_t[:, pl.ds(at, NODE)] = ninv
        fine_t[:, pl.ds(at, NODE)] = (lat_b.astype(F32) + nn * widen(ng)).astype(BF16)
        return carry

    def widen(v):
        return jnp.concatenate([v] * (NODE // W), axis=1)

    lax.fori_loop(0, ROWS // NODE, node_forward, 0)

    pf[gz] = nt(fine_t[...], oh_clus[...]).astype(BF16)
    pool_send(pf, pf_s, pf_r)
    wpin_t = jnp.transpose(w_pin[...].astype(F32)).astype(BF16)
    wpout_t = jnp.transpose(w_pout[...].astype(F32)).astype(BF16)
    pool_wait(pg, pg_s, pg_r)
    gd = pg[0].astype(F32)
    for k in range(1, n_z):
        gd = gd + pg[k].astype(F32)
    gd_b = gd.astype(BF16)
    gac = mm(w_pout[...], gd_b)
    pool_wait(pf, pf_s, pf_r)
    pooled = pf[0].astype(F32)
    for k in range(1, n_z):
        pooled = pooled + pf[k].astype(F32)
    pooled_b = pooled.astype(BF16)
    pc = mm(wpin_t, pooled_b)
    s = sigmoid(pc)
    ac = pc * s
    ac_b = ac.astype(BF16)
    delta_b = mm(wpout_t, ac_b).astype(BF16)
    gpc_b = (gac * (s + ac * (1.0 - s))).astype(BF16)
    gpool_b = mm(w_pin[...], gpc_b).astype(BF16)
    both = jnp.concatenate([delta_b, gpool_b], axis=0)
    dw_pin = nt(pooled_b, gpc_b) * (1.0 / n_z)
    dw_pout = nt(ac_b, gd_b) * (1.0 / n_z)

    sums[...] = jnp.zeros_like(sums)

    def node_back(u, carry):
        at = pl.multiple_of(u * NODE, NODE)
        added = mm(both, oh_clus[:, pl.ds(at, NODE)])
        mixed = fine_t[:, pl.ds(at, NODE)].astype(F32) + added[:W, :]
        for b in range(NODE // W):
            mixed_o[pl.ds(at + b * W, W), :] = jnp.transpose(mixed[:, b * W : (b + 1) * W]).astype(BF16)
        gf = gm_t[:, pl.ds(at, NODE)].astype(F32) + added[W:, :]
        gfine_t[:, pl.ds(at, NODE)] = gf
        nn = nn_t[:, pl.ds(at, NODE)]
        sums[1] += narrow(gf * nn)
        gn = gf * widen(ng)
        gy_b = ((gn - mean0(gn) - nn * mean0(gn * nn)) * ninv_t[:, pl.ds(at, NODE)]).astype(BF16)
        gy_t[:, pl.ds(at, NODE)] = gy_b
        gpn_b = (mm(w_node_h, gy_b) * nslope_t[:, pl.ds(at, NODE)]).astype(BF16)
        gpn_t[:, pl.ds(at, NODE)] = gpn_b
        ga = mm(w_agg[...], gpn_b)
        sums[0] += narrow(ga * sum_t[:, pl.ds(at, NODE)])
        g = ga * widen(eg)
        gc_t[:, pl.ds(at, NODE)] = g - mean0(g)
        return carry

    def narrow(v):
        total = v[:, :W]
        for b in range(1, NODE // W):
            total = total + v[:, b * W : (b + 1) * W]
        return total

    lax.fori_loop(0, ROWS // NODE, node_back, 0)

    def put(buf, index, mat, width):
        per = W // c_rows
        buf[index * per : (index + 1) * per, :c_rows, :] = mat.reshape(per, c_rows, W).astype(BF16)

    def reduce_out(buf, into, s, r):
        into[rank_a] = buf[rank_a]

        def go(k, c):
            to = a_peer(k)
            remote(buf.at[to], into.at[rank_a], s, r, a_dev(to)).start()
            return c

        lax.fori_loop(1, n_a, go, 0)

    def reduce_mid(buf, into, mid, s, r, s2, r2):
        drain(into.at[pl.ds(0, n_a - 1)], r)
        total = into[0].astype(F32)
        for k in range(1, n_a):
            total = total + into[k].astype(F32)
        mid[rank_b] = total.astype(BF16)

        def go(k, c):
            remote(mid.at[rank_b], mid.at[rank_b], s2, r2, b_dev(b_peer(k))).start()
            return c

        lax.fori_loop(1, n_b, go, 0)

    def gather_out(mid, out, s2, r2, s3, r3):
        drain(mid.at[pl.ds(0, n_b - 1)], r2)
        total = mid[0].astype(F32)
        for k in range(1, n_b):
            total = total + mid[k].astype(F32)
        out[rank_a] = total.astype(BF16)

        def go(k, c):
            remote(out.at[rank_a], out.at[rank_a], s3, r3, a_dev(a_peer(k))).start()
            return c

        lax.fori_loop(1, n_a, go, 0)

    def finish(buf, mid, out, s, s2, s3, r3):
        drain(out.at[pl.ds(0, n_a - 1)], r3)
        drain(buf.at[pl.ds(0, n_a - 1)], s)
        drain(mid.at[pl.ds(0, n_b - 1)], s2)
        drain(out.at[pl.ds(0, n_a - 1)], s3)

    def row_sums(v):
        hi = v.astype(BF16)
        lo = (v - hi.astype(F32)).astype(BF16)
        ones = jnp.ones((GAIN_ROWS, W), BF16)
        return nt(ones, hi) + nt(ones, lo)

    dw_sa = nt(jnp.concatenate([lat_t[...], agg_t[...]], axis=0), gpn_t[...])
    put(early, 0, dw_sa[:W, :], c_rows)
    put(early, 1, dw_sa[W:, :], c_rows)
    put(early, 2, nt(an_t[...], gy_t[...]), c_rows)
    put(early, 3, dw_pin, c_rows)
    which = lax.broadcasted_iota(jnp.int32, (GAIN_ROWS, W), 0)
    gain_rows = jnp.where(which == 0, row_sums(sums[0]), row_sums(sums[1])).astype(BF16)
    for k in range(n_a):
        early[k, c_rows:, :] = gain_rows
    reduce_out(early, early_in, e1s, e1r)

    gp_own[...] = jnp.zeros_like(gp_own)
    gp_ghost[...] = jnp.zeros_like(gp_ghost)
    dw_edge[...] = jnp.zeros_like(dw_edge)

    def backward(u, carry):
        low = low_half()
        at = pl.multiple_of(u * W, W)
        at_g = pl.multiple_of(lax.rem(u, GHOSTS // W) * W, W)
        gc_of = spread_halves(gc_t[:, pl.ds(at, W)], low)
        back_of = []
        for half in range(2):
            t = 2 * u + half
            gc = jnp.concatenate([gc_of[half]] * 2, axis=1)
            total = None
            for q in range(STEPS):
                lanes = slice(q * CHUNK, (q + 1) * CHUNK)
                normed = norm_all[t, :, lanes].astype(F32)
                gz_b = ((gc - normed * mean0(gc * normed)) * inv_all[t, :, lanes]).astype(BF16)
                gz_tmp[half, :, lanes] = gz_b
                gpre = mm(w_edge_h, gz_b) * slope_all[t, :, lanes].astype(F32)
                gp_tmp[half, :, lanes] = gpre.astype(BF16)
                part = gpre[:, :W] + gpre[:, W:]
                total = part if total is None else total + part
            dw_edge[...] += nt(act_all[t], gz_tmp[half])
            window = nt(oh_all[t], gp_tmp[half])
            gp_own[pl.ds(at + half * TILE, W), :] += window[:W, :]
            gp_ghost[pl.ds(at_g + half * TILE, TILE), :] += window[W:, :]
            back_of.append(total + swap(total))
        grecv_t[:, pl.ds(at, W)] = jnp.where(low, back_of[0], back_of[1]).astype(BF16)
        return carry

    back_to = (x_low, x_up, y_low, y_up)
    back = [
        remote(backbuf.at[pl.ds(q * W, W)], ret.at[pl.ds(q * W, W)], ret_s.at[q], ret_r.at[q], back_to[q])
        for q in range(4)
    ]
    lax.fori_loop(0, PAIRS // 2, lambda k, c: backward((k // 2) * 4 + lax.rem(k, 2), c), 0)
    backbuf[: 2 * W, :] = gp_ghost[: 2 * W, :].astype(BF16)
    back[0].start()
    back[1].start()
    reduce_mid(early, early_in, early_mid, e1s, e1r, e2s, e2r)
    lax.fori_loop(0, PAIRS // 2, lambda k, c: backward((k // 2) * 4 + 2 + lax.rem(k, 2), c), 0)
    backbuf[2 * W :, :] = gp_ghost[2 * W :, :].astype(BF16)
    back[2].start()
    back[3].start()

    gp_own[:TILE, :] += gp_own[ROWS:, :]
    own_b = gp_own[:ROWS, :].astype(BF16)
    ghost_t = nt(eye, ghost[...]).astype(BF16)
    put(late, 0, mm(lat_t[...], own_b) + mm(ghost_t, backbuf[...]), c_rows)
    put(late, 1, nt(lat_t[...], grecv_t[...]), c_rows)
    put(late, 2, dw_edge[...], c_rows)
    put(late, 3, dw_pout, c_rows)
    reduce_out(late, late_in, l1s, l1r)
    gather_out(early_mid, early_out, e2s, e2r, e3s, e3r)

    gfine_t[...] += (
        mm(w_self[...], gpn_t[...]) + mm(w_recv[...], grecv_t[...]) + nt(w_send[...], own_b)
    )
    for c in back:
        c.wait()
    side_a = jnp.concatenate([ret[q * TILE : (q + 1) * TILE, :] for q in (2, 3, 0, 1)], axis=0)
    side_b = jnp.concatenate([ret[q * TILE : (q + 1) * TILE, :] for q in (6, 4, 7, 5)], axis=0)
    ret_t = (nt(w_send[...], side_a) + nt(w_send[...], side_b)).astype(BF16)
    gfine_t[...] += mm(ret_t, oh_send[...])
    reduce_mid(late, late_in, late_mid, l1s, l1r, l2s, l2r)
    for b in range(PAIRS):
        grad_o[b * W : (b + 1) * W, :] = jnp.transpose(gfine_t[:, b * W : (b + 1) * W])

    def emit(out, index, place):
        per = W // c_rows
        mat = out[index * per : (index + 1) * per, :c_rows, :].astype(F32).reshape(W, W)
        mats_o[place] = mat * lax.rsqrt(jnp.mean(mat * mat, keepdims=True) + 1e-06)

    finish(early, early_mid, early_out, e1s, e2s, e3s, e3r)
    for index, place in enumerate((3, 4, 5, 6)):
        emit(early_out, index, place)
    scale = float(ROWS * n_x * n_y * n_z) ** (-0.5)
    gains_o[...] = early_out[0, c_rows : c_rows + 2, :].astype(F32) * scale
    pool_done(pg, pg_s, pg_r)
    pool_done(pf, pf_s, pf_r)
    gather_out(late_mid, late_out, l2s, l2r, l3s, l3r)
    finish(late, late_mid, late_out, l1s, l2s, l3s, l3r)
    for index, place in enumerate((0, 1, 2, 7)):
        emit(late_out, index, place)


def pass_on(*refs):
    half = len(refs) // 2
    for src, dst in zip(refs[:half], refs[half:]):
        dst[...] = src[...]


def solution(mesh):
    sizes = tuple(mesh.shape[name] for name in ("gx", "gy", "gz"))
    n_a, n_b, n_z = sizes[0] * sizes[2], sizes[1], sizes[2]
    c_rows = 4 * W // n_a
    tiles = ROWS // TILE
    edges = TILE * NEIGH
    v = pltpu.VMEM
    dma = pltpu.SemaphoreType.DMA

    def reduce_bufs(rows):
        return [v((n_a, rows, W), BF16), v((n_a, rows, W), BF16), v((n_b, rows, W), BF16), v((n_a, rows, W), BF16)]

    scratch = [
        v((GHOSTS, W), BF16),
        v((GHOSTS, W), BF16),
        v((GHOSTS, W), BF16),
        v((GHOSTS, W), BF16),
        v((n_z, W, CLUSTERS), BF16),
        v((n_z, W, CLUSTERS), BF16),
        *reduce_bufs(c_rows + GAIN_ROWS),
        *reduce_bufs(c_rows),
        v((W, ROWS), BF16),
        v((W, ROWS), BF16),
        v((4 * TILE, ROWS), BF16),
        v((CLUSTERS, ROWS), BF16),
        v((W, ROWS), BF16),
        v((W, ROWS), BF16),
        v((W, GHOSTS), BF16),
        v((W, GHOSTS), BF16),
        v((W, ROWS), F32),
        v((W, 2 * W), BF16),
        v((W, 2 * W), BF16),
        v((W, 2 * W), BF16),
        v((tiles, SLOTS, edges), BF16),
        v((tiles, W, edges), BF16),
        v((tiles, W, edges), BF16),
        v((tiles, W, edges), BF16),
        v((tiles, 1, edges), F32),
        v((W, ROWS), F32),
        v((W, ROWS), BF16),
        v((W, ROWS), BF16),
        v((W, ROWS), F32),
        v((W, ROWS), F32),
        v((1, ROWS), F32),
        v((W, ROWS), BF16),
        v((W, ROWS), F32),
        v((W, ROWS), BF16),
        v((W, ROWS), BF16),
        v((W, ROWS), F32),
        v((W, ROWS), BF16),
        v((2, W, edges), BF16),
        v((2, W, edges), BF16),
        v((ROWS + TILE, W), F32),
        v((GHOSTS, W), F32),
        v((W, W), F32),
        v((2, W, W), F32),
        dma((4,)), dma((4,)), dma((4,)), dma((4,)),
        dma((n_z,)), dma((n_z,)), dma((n_z,)), dma((n_z,)),
        *[dma for _ in range(12)],
        v((ROWS, W), BF16), v((ROWS, W), BF16), v((NEIGH, ROWS), jnp.int32), v((4, TILE), jnp.int32),
        v((1, ROWS), jnp.int32), *[v((W, W), BF16) for _ in range(8)], v((1, W), F32), v((1, W), F32),
        dma((15,)),
    ]

    def step(latents, grad_mixed, neighbours, send_list, cluster, w_send, w_recv, w_edge, edge_gain, w_self, w_agg,
             w_node, node_gain, w_pool_in, w_pool_out):
        results = pl.pallas_call(
            functools.partial(kernel, sizes),
            out_shape=(
                jax.ShapeDtypeStruct((ROWS, W), BF16),
                jax.ShapeDtypeStruct((ROWS, W), F32),
                jax.ShapeDtypeStruct((8, W, W), F32),
                jax.ShapeDtypeStruct((2, W), F32),
            ),
            in_specs=[pl.BlockSpec(memory_space=pltpu.HBM)] * 15,
            out_specs=tuple([pl.BlockSpec(memory_space=pltpu.VMEM)] * 4),
            scratch_shapes=scratch,
            compiler_params=pltpu.CompilerParams(
                collective_id=0, has_side_effects=True, vmem_limit_bytes=44 * 1024 * 1024
            ),
        )(*[pltpu.with_memory_space_constraint(x, pltpu.HBM) for x in (
            latents, grad_mixed, neighbours.T, send_list, cluster.reshape(1, ROWS), w_send, w_recv, w_edge, w_self,
            w_agg, w_node, w_pool_in, w_pool_out, edge_gain.reshape(1, W), node_gain.reshape(1, W))])
        return pl.pallas_call(
            pass_on,
            out_shape=tuple(jax.ShapeDtypeStruct(r.shape, r.dtype) for r in results),
            in_specs=[pl.BlockSpec(memory_space=pltpu.VMEM)] * 4,
            out_specs=tuple([pl.BlockSpec(memory_space=pltpu.VMEM)] * 4),
            compiler_params=pltpu.CompilerParams(vmem_limit_bytes=8 * 1024 * 1024),
        )(*results)

    rows = P(("gx", "gy", "gz"), None)
    in_specs = (rows, rows, rows, rows, P(("gx", "gy", "gz"))) + (P(),) * 10
    out_specs = (rows, rows, P(), P())
    return jax.shard_map(step, mesh=mesh, in_specs=in_specs, out_specs=out_specs, check_vma=False)
```

```python
import functools

import jax
import jax.numpy as jnp
from jax import lax
from jax.experimental import pallas as pl
from jax.experimental.pallas import tpu as pltpu
from jax.sharding import PartitionSpec as P

EPS = 1e-05
W = 128
ROWS = 1024
NEIGH = 16
TILE = 64
PAIRS = ROWS // W
GHOSTS = 512
CLUSTERS = 256
SLOTS = 192
CHUNK = 256
STEPS = TILE * NEIGH // CHUNK
NODE = 256
GAIN_ROWS = 16
F32 = jnp.float32
BF16 = jnp.bfloat16
MESH = pl.DeviceIdType.MESH


def mm(a, b):
    return lax.dot_general(a, b, (((1,), (0,)), ((), ())), preferred_element_type=F32)


def nt(a, b):
    return lax.dot_general(a, b, (((1,), (1,)), ((), ())), preferred_element_type=F32)


def sigmoid(v):
    return 0.5 * jnp.tanh(0.5 * v) + 0.5


def mean0(v):
    return jnp.sum(v, axis=0, keepdims=True) * (1.0 / W)


def norm_centred(centred):
    inv = lax.rsqrt(mean0(centred * centred) + EPS)
    return centred * inv, inv


def half_silu(h):
    t = jnp.tanh(h)
    up = 1.0 + t
    act = h * up
    return act, up + act * (1.0 - t)


def narrow_half_silu(h):
    h = h.astype(BF16)
    t = jnp.tanh(h)
    one = jnp.ones((), BF16)
    up = one + t
    act = h * up
    return act, up + act * (one - t)


def rows_of(row):
    return jnp.concatenate([jnp.broadcast_to(row, (16, row.shape[1])).astype(BF16)] * (W // 16), axis=0)


def centred_pair(w):
    w_t = jnp.transpose(w.astype(F32))
    centred = w_t - mean0(w_t)
    high = centred.astype(BF16)
    return jnp.concatenate([high, (centred - high.astype(F32)).astype(BF16)], axis=1)


def twice(v):
    return jnp.concatenate([v, v], axis=0)


def one_hot(row, ids):
    wide = jnp.broadcast_to(row, (16, W)).astype(BF16)
    same = jnp.concatenate([wide] * (ids.shape[0] // 16), axis=0) == ids
    return jnp.where(same, jnp.ones((), BF16), jnp.zeros((), BF16))


def low_half():
    return lax.broadcasted_iota(jnp.int32, (W, W), 1) < TILE


def swap(v):
    return pltpu.roll(v, TILE, 1)


def spread_halves(block, low):
    other = swap(block)
    return jnp.where(low, block, other), jnp.where(low, other, block)


def column_of(row):
    return jnp.transpose(jnp.broadcast_to(row, (W, W)))


def kernel(sizes, *refs):
    far, near, in_sems = refs[:15], refs[-16:-1], refs[-1]
    (lat, gm, nb, send, clus, w_send, w_recv, w_edge, w_self, w_agg, w_node, w_pin, w_pout, egain, ngain) = near
    mixed_o, grad_o, mats_o, gains_o = refs[15:19]
    (sbuf, ghost, ret, backbuf, pg, pf, early, early_in, early_mid, early_out, late, late_in, late_mid, late_out,
     lat_t, gm_t, oh_send, oh_clus, tab, tab_sh, gtab, gtab_sh, recv_t, wsa_t, we_c, wn_c,
     oh_all, act_all, slope_all, norm_all, inv_all, sum_t, agg_t, an_t, nslope_t, nn_t, ninv_t, fine_t, gfine_t,
     gy_t, gpn_t, gc_t, grecv_t, gz_tmp, gp_tmp, gp_own, gp_ghost, dw_edge, sums) = refs[19:68]
    (halo_s, halo_r, ret_s, ret_r, pg_s, pg_r, pf_s, pf_r,
     e1s, e1r, e2s, e2r, e3s, e3r, l1s, l1r, l2s, l2r, l3s, l3r) = refs[68:-16]
    n_x, n_y, n_z = sizes
    n_a, n_b = n_x * n_z, n_y
    c_rows = 4 * W // n_a
    gx, gy, gz = lax.axis_index("gx"), lax.axis_index("gy"), lax.axis_index("gz")
    x_up = (lax.rem(gx + 1, n_x), gy, gz)
    x_low = (lax.rem(gx + n_x - 1, n_x), gy, gz)
    y_up = (gx, lax.rem(gy + 1, n_y), gz)
    y_low = (gx, lax.rem(gy + n_y - 1, n_y), gz)
    rank_a = ((gx // 2) * 2 + lax.rem(gy, 2)) * n_z + gz
    rank_b = lax.rem(gx, 2) * (n_y // 2) + gy // 2

    def z_peer(k):
        return lax.rem(gz + k, n_z)

    def a_peer(k):
        return lax.rem(rank_a + k, n_a)

    def a_dev(r):
        yc = r // n_z
        return ((yc // 2) * 2 + lax.rem(gx, 2), (gy // 2) * 2 + lax.rem(yc, 2), lax.rem(r, n_z))

    def b_peer(k):
        return lax.rem(rank_b + k, n_b)

    def b_dev(r):
        return ((gx // 2) * 2 + r // (n_y // 2), lax.rem(r, n_y // 2) * 2 + lax.rem(gy, 2), gz)

    def remote(src, dst, s, r, dev):
        return pltpu.make_async_remote_copy(
            src_ref=src, dst_ref=dst, send_sem=s, recv_sem=r, device_id=dev, device_id_type=MESH
        )

    def drain(ref, sem):
        pltpu.make_async_copy(ref, ref, sem).wait()

    loads = [pltpu.make_async_copy(a, b, in_sems.at[i]) for i, (a, b) in enumerate(zip(far, near))]
    for i in (3, 0, 1, 4, *range(5, 15), 2):
        loads[i].start()

    barrier = pltpu.get_barrier_semaphore()
    for dev in (x_up, x_low, y_up, y_low):
        pl.semaphore_signal(barrier, inc=1, device_id=dev, device_id_type=MESH)

    def greet_a(k, c):
        pl.semaphore_signal(barrier, inc=1, device_id=a_dev(a_peer(k)), device_id_type=MESH)
        return c

    def greet_b(k, c):
        pl.semaphore_signal(barrier, inc=1, device_id=b_dev(b_peer(k)), device_id_type=MESH)
        return c

    lax.fori_loop(1, n_a, greet_a, 0)
    lax.fori_loop(1, n_b, greet_b, 0)

    lane_row = lax.broadcasted_iota(jnp.int32, (TILE, W), 1)
    loads[3].wait()
    send_f = send[...].astype(F32)
    for q in range(4):
        col = jnp.transpose(jnp.broadcast_to(send_f[q : q + 1, :], (W, TILE))).astype(jnp.int32)
        for b in range(PAIRS):
            hot = jnp.where(col == lane_row + b * W, 1.0, 0.0).astype(BF16)
            oh_send[q * TILE : (q + 1) * TILE, b * W : (b + 1) * W] = hot
    loads[0].wait()
    cells = mm(oh_send[...], lat[...]).astype(BF16)
    for slot, q in enumerate((2, 3, 0, 1, 1, 3, 0, 2)):
        sbuf[slot * TILE : (slot + 1) * TILE, :] = cells[q * TILE : (q + 1) * TILE, :]
    pl.semaphore_wait(barrier, 4 + n_a - 1 + n_b - 1)
    halo_to = (x_up, x_low, y_up, y_low)
    halo = [
        remote(sbuf.at[pl.ds(q * W, W)], ghost.at[pl.ds(q * W, W)], halo_s.at[q], halo_r.at[q], halo_to[q])
        for q in range(4)
    ]
    for q in (2, 3, 0, 1):
        halo[q].start()

    eye = jnp.where(
        lax.broadcasted_iota(jnp.int32, (W, W), 0) == lax.broadcasted_iota(jnp.int32, (W, W), 1), 1.0, 0.0
    ).astype(BF16)
    loads[1].wait()
    loads[4].wait()
    gm_t[...] = nt(eye, gm[...]).astype(BF16)
    cl_id = lax.broadcasted_iota(jnp.int32, (CLUSTERS, W), 0).astype(F32).astype(BF16)
    clus_f = clus[...].astype(F32)
    for b in range(PAIRS):
        oh_clus[:, b * W : (b + 1) * W] = one_hot(clus_f[:, b * W : (b + 1) * W], cl_id)

    def pool_send(buf, sems_s, sems_r):
        def go(k, c):
            to = (gx, gy, z_peer(k))
            remote(buf.at[gz], buf.at[gz], sems_s.at[k], sems_r.at[gz], to).start()
            return c

        lax.fori_loop(1, n_z, go, 0)

    def pool_wait(buf, sems_s, sems_r):
        def go(k, c):
            src = lax.rem(gz + n_z - k, n_z)
            remote(buf.at[gz], buf.at[src], sems_s.at[k], sems_r.at[src], (gx, gy, z_peer(k))).wait_recv()
            return c

        lax.fori_loop(1, n_z, go, 0)

    def pool_done(buf, sems_s, sems_r):
        def go(k, c):
            remote(buf.at[gz], buf.at[gz], sems_s.at[k], sems_r.at[gz], (gx, gy, z_peer(k))).wait_send()
            return c

        lax.fori_loop(1, n_z, go, 0)

    pg[gz] = nt(gm_t[...], oh_clus[...]).astype(BF16)
    pool_send(pg, pg_s, pg_r)

    lat_t[...] = nt(eye, lat[...]).astype(BF16)
    for i in (*range(5, 15), 2):
        loads[i].wait()
    wsend_t = (jnp.transpose(w_send[...].astype(F32)) * 0.5).astype(BF16)
    wrecv_t = (jnp.transpose(w_recv[...].astype(F32)) * 0.5).astype(BF16)
    we_c[...] = centred_pair(w_edge[...])
    wn_c[...] = centred_pair(w_node[...])
    wsa_t[:, :W] = (jnp.transpose(w_self[...].astype(F32)) * 0.5).astype(BF16)
    wsa_t[:, W:] = (jnp.transpose(w_agg[...].astype(F32)) * 0.5).astype(BF16)
    w_edge_h = (w_edge[...].astype(F32) * 0.5).astype(BF16)
    w_node_h = (w_node[...].astype(F32) * 0.5).astype(BF16)
    tab[...] = mm(wsend_t, lat_t[...]).astype(BF16)
    lat_roll = jnp.concatenate([lat[TILE:, :], lat[:TILE, :]], axis=0)
    tab_sh[...] = nt(wsend_t, lat_roll).astype(BF16)
    recv_t[...] = mm(wrecv_t, lat_t[...]).astype(BF16).astype(F32)
    eg = column_of(egain[...])
    ng = column_of(ngain[...])

    def ghost_tables(first):
        part = slice(first, first + 2 * W)
        own = ghost[part, :]
        gtab[:, part] = nt(wsend_t, own).astype(BF16)
        gtab_sh[:, part] = nt(wsend_t, jnp.concatenate([own[TILE:, :], own[:TILE, :]], axis=0)).astype(BF16)

    def forward(u, carry):
        low = low_half()
        slot_id = lax.broadcasted_iota(jnp.int32, (SLOTS, W), 0).astype(F32).astype(BF16)
        at = pl.multiple_of(u * W, W)
        at_g = pl.multiple_of(lax.rem(u, GHOSTS // W) * W, W)
        picks = nb[:, pl.ds(at, W)]
        low8 = low[:8, :]
        first, second = picks[:8, :], picks[8:, :]
        picks_of = (jnp.where(low8, first, swap(second)), jnp.where(low8, swap(first), second))
        recv_of = spread_halves(recv_t[:, pl.ds(at, W)], low)
        sums_of = []
        for half in range(2):
            t = 2 * u + half
            chosen = picks_of[half]
            local = jnp.where(chosen >= ROWS, (chosen & (TILE - 1)) + 2 * TILE, (chosen - t * TILE) & (ROWS - 1))
            local = local.astype(F32)
            own, far = (tab, gtab) if half == 0 else (tab_sh, gtab_sh)
            window = jnp.concatenate([own[:, pl.ds(at, W)], far[:, pl.ds(at_g, TILE)]], axis=1)
            total = None
            for q in range(STEPS):
                lanes = slice(q * CHUNK, (q + 1) * CHUNK)
                hot = jnp.concatenate([one_hot(local[c : c + 1, :], slot_id) for c in (2 * q, 2 * q + 1)], axis=1)
                oh_all[t, :, lanes] = hot
                act_b, slope = narrow_half_silu(mm(window, hot) + jnp.concatenate([recv_of[half]] * 2, axis=1))
                act_all[t, :, lanes] = act_b
                slope_all[t, :, lanes] = slope
                normed, inv = norm_centred(mm(we_c[...], twice(act_b)))
                norm_all[t, :, lanes] = normed.astype(BF16)
                inv_all[t, :, lanes] = inv
                part = normed[:, :W] + normed[:, W:]
                total = part if total is None else total + part
            sums_of.append(total + swap(total))
        total = jnp.where(low, sums_of[0], sums_of[1])
        sum_t[:, pl.ds(at, W)] = total
        agg_t[:, pl.ds(at, W)] = (total * eg).astype(BF16)
        return carry

    halo[2].wait()
    halo[3].wait()
    ghost_tables(2 * W)
    lax.fori_loop(0, PAIRS // 4, lambda k, c: forward(k * 4 + 3, forward(k * 4 + 2, c)), 0)
    halo[0].wait()
    halo[1].wait()
    ghost_tables(0)
    lax.fori_loop(0, PAIRS // 4, lambda k, c: forward(k * 4 + 1, forward(k * 4, c)), 0)

    def node_forward(u, carry):
        at = pl.multiple_of(u * NODE, NODE)
        lat_b = lat_t[:, pl.ds(at, NODE)]
        an, slope = half_silu(mm(wsa_t[...], jnp.concatenate([lat_b, agg_t[:, pl.ds(at, NODE)]], axis=0)))
        an_b = an.astype(BF16)
        an_t[:, pl.ds(at, NODE)] = an_b
        nslope_t[:, pl.ds(at, NODE)] = slope
        nn, ninv = norm_centred(mm(wn_c[...], twice(an_b)))
        nn_t[:, pl.ds(at, NODE)] = nn
        ninv_t[:, pl.ds(at, NODE)] = ninv
        fine_t[:, pl.ds(at, NODE)] = (lat_b.astype(F32) + nn * widen(ng)).astype(BF16)
        return carry

    def widen(v):
        return jnp.concatenate([v] * (NODE // W), axis=1)

    lax.fori_loop(0, ROWS // NODE // 2, lambda k, c: node_forward(2 * k + 1, node_forward(2 * k, c)), 0)

    pf[gz] = nt(fine_t[...], oh_clus[...]).astype(BF16)
    pool_send(pf, pf_s, pf_r)
    wpin_t = jnp.transpose(w_pin[...].astype(F32)).astype(BF16)
    wpout_t = jnp.transpose(w_pout[...].astype(F32)).astype(BF16)
    pool_wait(pg, pg_s, pg_r)
    gd = pg[0].astype(F32)
    for k in range(1, n_z):
        gd = gd + pg[k].astype(F32)
    gd_b = gd.astype(BF16)
    gac = mm(w_pout[...], gd_b)
    pool_wait(pf, pf_s, pf_r)
    pooled = pf[0].astype(F32)
    for k in range(1, n_z):
        pooled = pooled + pf[k].astype(F32)
    pooled_b = pooled.astype(BF16)
    pc = mm(wpin_t, pooled_b)
    s = sigmoid(pc)
    ac = pc * s
    ac_b = ac.astype(BF16)
    delta_b = mm(wpout_t, ac_b).astype(BF16)
    gpc_b = (gac * (s + ac * (1.0 - s))).astype(BF16)
    gpool_b = mm(w_pin[...], gpc_b).astype(BF16)
    both = jnp.concatenate([delta_b, gpool_b], axis=0)
    dw_pin = nt(pooled_b, gpc_b) * (1.0 / n_z)
    dw_pout = nt(ac_b, gd_b) * (1.0 / n_z)

    sums[...] = jnp.zeros_like(sums)

    def node_back(u, carry):
        at = pl.multiple_of(u * NODE, NODE)
        added = mm(both, oh_clus[:, pl.ds(at, NODE)])
        mixed = fine_t[:, pl.ds(at, NODE)].astype(F32) + added[:W, :]
        for b in range(NODE // W):
            mixed_o[pl.ds(at + b * W, W), :] = jnp.transpose(mixed[:, b * W : (b + 1) * W]).astype(BF16)
        gf = gm_t[:, pl.ds(at, NODE)].astype(F32) + added[W:, :]
        gfine_t[:, pl.ds(at, NODE)] = gf
        nn = nn_t[:, pl.ds(at, NODE)]
        sums[1] += narrow(gf * nn)
        gn = gf * widen(ng)
        gy_b = ((gn - mean0(gn) - nn * mean0(gn * nn)) * ninv_t[:, pl.ds(at, NODE)]).astype(BF16)
        gy_t[:, pl.ds(at, NODE)] = gy_b
        gpn_b = (mm(w_node_h, gy_b) * nslope_t[:, pl.ds(at, NODE)]).astype(BF16)
        gpn_t[:, pl.ds(at, NODE)] = gpn_b
        ga = mm(w_agg[...], gpn_b)
        sums[0] += narrow(ga * sum_t[:, pl.ds(at, NODE)])
        g = ga * widen(eg)
        gc_t[:, pl.ds(at, NODE)] = g - mean0(g)
        return carry

    def narrow(v):
        total = v[:, :W]
        for b in range(1, NODE // W):
            total = total + v[:, b * W : (b + 1) * W]
        return total

    lax.fori_loop(0, ROWS // NODE // 2, lambda k, c: node_back(2 * k + 1, node_back(2 * k, c)), 0)

    def put(buf, index, mat, width):
        per = W // c_rows
        buf[index * per : (index + 1) * per, :c_rows, :] = mat.reshape(per, c_rows, W).astype(BF16)

    def reduce_out(buf, into, s, r):
        into[rank_a] = buf[rank_a]

        def go(k, c):
            to = a_peer(k)
            remote(buf.at[to], into.at[rank_a], s, r, a_dev(to)).start()
            return c

        lax.fori_loop(1, n_a, go, 0)

    def reduce_mid(buf, into, mid, s, r, s2, r2):
        drain(into.at[pl.ds(0, n_a - 1)], r)
        total = into[0].astype(F32)
        for k in range(1, n_a):
            total = total + into[k].astype(F32)
        mid[rank_b] = total.astype(BF16)

        def go(k, c):
            remote(mid.at[rank_b], mid.at[rank_b], s2, r2, b_dev(b_peer(k))).start()
            return c

        lax.fori_loop(1, n_b, go, 0)

    def gather_out(mid, out, s2, r2, s3, r3):
        drain(mid.at[pl.ds(0, n_b - 1)], r2)
        total = mid[0].astype(F32)
        for k in range(1, n_b):
            total = total + mid[k].astype(F32)
        out[rank_a] = total.astype(BF16)

        def go(k, c):
            remote(out.at[rank_a], out.at[rank_a], s3, r3, a_dev(a_peer(k))).start()
            return c

        lax.fori_loop(1, n_a, go, 0)

    def finish(buf, mid, out, s, s2, s3, r3):
        drain(out.at[pl.ds(0, n_a - 1)], r3)
        drain(buf.at[pl.ds(0, n_a - 1)], s)
        drain(mid.at[pl.ds(0, n_b - 1)], s2)
        drain(out.at[pl.ds(0, n_a - 1)], s3)

    def row_sums(v):
        hi = v.astype(BF16)
        lo = (v - hi.astype(F32)).astype(BF16)
        ones = jnp.ones((GAIN_ROWS, W), BF16)
        return nt(ones, hi) + nt(ones, lo)

    dw_sa = nt(jnp.concatenate([lat_t[...], agg_t[...]], axis=0), gpn_t[...])
    put(early, 0, dw_sa[:W, :], c_rows)
    put(early, 1, dw_sa[W:, :], c_rows)
    put(early, 2, nt(an_t[...], gy_t[...]), c_rows)
    put(early, 3, dw_pin, c_rows)
    which = lax.broadcasted_iota(jnp.int32, (GAIN_ROWS, W), 0)
    gain_rows = jnp.where(which == 0, row_sums(sums[0]), row_sums(sums[1])).astype(BF16)
    for k in range(n_a):
        early[k, c_rows:, :] = gain_rows
    reduce_out(early, early_in, e1s, e1r)

    gp_own[...] = jnp.zeros_like(gp_own)
    gp_ghost[...] = jnp.zeros_like(gp_ghost)
    dw_edge[...] = jnp.zeros_like(dw_edge)

    def backward(u, carry):
        low = low_half()
        at = pl.multiple_of(u * W, W)
        at_g = pl.multiple_of(lax.rem(u, GHOSTS // W) * W, W)
        gc_of = spread_halves(gc_t[:, pl.ds(at, W)], low)
        back_of = []
        for half in range(2):
            t = 2 * u + half
            gc = jnp.concatenate([gc_of[half].astype(BF16)] * 2, axis=1)
            total = None
            for q in range(STEPS):
                lanes = slice(q * CHUNK, (q + 1) * CHUNK)
                normed = norm_all[t, :, lanes]
                shared = rows_of(mean0((gc * normed).astype(F32)))
                gz_b = (gc - normed * shared) * rows_of(inv_all[t, :, lanes])
                gz_tmp[half, :, lanes] = gz_b
                gpre_b = mm(w_edge_h, gz_b).astype(BF16) * slope_all[t, :, lanes]
                gp_tmp[half, :, lanes] = gpre_b
                gpre = gpre_b.astype(F32)
                part = gpre[:, :W] + gpre[:, W:]
                total = part if total is None else total + part
            dw_edge[...] += nt(act_all[t], gz_tmp[half])
            window = nt(oh_all[t], gp_tmp[half])
            gp_own[pl.ds(at + half * TILE, W), :] += window[:W, :]
            gp_ghost[pl.ds(at_g + half * TILE, TILE), :] += window[W:, :]
            back_of.append(total + swap(total))
        grecv_t[:, pl.ds(at, W)] = jnp.where(low, back_of[0], back_of[1]).astype(BF16)
        return carry

    back_to = (x_low, x_up, y_low, y_up)
    back = [
        remote(backbuf.at[pl.ds(q * W, W)], ret.at[pl.ds(q * W, W)], ret_s.at[q], ret_r.at[q], back_to[q])
        for q in range(4)
    ]
    lax.fori_loop(0, PAIRS // 4, lambda k, c: backward(k * 4 + 1, backward(k * 4, c)), 0)
    backbuf[: 2 * W, :] = gp_ghost[: 2 * W, :].astype(BF16)
    back[0].start()
    back[1].start()

    def backward_near(k, c):
        @pl.when(k == 1)
        def _():
            reduce_mid(early, early_in, early_mid, e1s, e1r, e2s, e2r)

        return backward(k * 4 + 3, backward(k * 4 + 2, c))

    lax.fori_loop(0, PAIRS // 4, backward_near, 0)
    backbuf[2 * W :, :] = gp_ghost[2 * W :, :].astype(BF16)
    back[2].start()
    back[3].start()

    gp_own[:TILE, :] += gp_own[ROWS:, :]
    own_b = gp_own[:ROWS, :].astype(BF16)
    ghost_t = nt(eye, ghost[...]).astype(BF16)
    put(late, 0, mm(lat_t[...], own_b) + mm(ghost_t, backbuf[...]), c_rows)
    put(late, 1, nt(lat_t[...], grecv_t[...]), c_rows)
    put(late, 2, dw_edge[...], c_rows)
    put(late, 3, dw_pout, c_rows)
    reduce_out(late, late_in, l1s, l1r)

    gfine_t[...] += (
        mm(w_self[...], gpn_t[...]) + mm(w_recv[...], grecv_t[...]) + nt(w_send[...], own_b)
    )
    for c in back:
        c.wait()
    side_a = jnp.concatenate([ret[q * TILE : (q + 1) * TILE, :] for q in (2, 3, 0, 1)], axis=0)
    side_b = jnp.concatenate([ret[q * TILE : (q + 1) * TILE, :] for q in (6, 4, 7, 5)], axis=0)
    ret_t = (nt(w_send[...], side_a) + nt(w_send[...], side_b)).astype(BF16)
    gfine_t[...] += mm(ret_t, oh_send[...])
    gather_out(early_mid, early_out, e2s, e2r, e3s, e3r)
    reduce_mid(late, late_in, late_mid, l1s, l1r, l2s, l2r)
    for b in range(PAIRS):
        grad_o[b * W : (b + 1) * W, :] = jnp.transpose(gfine_t[:, b * W : (b + 1) * W])

    def emit(out, index, place):
        per = W // c_rows
        mat = out[index * per : (index + 1) * per, :c_rows, :].astype(F32).reshape(W, W)
        mats_o[place] = mat * lax.rsqrt(jnp.mean(mat * mat, keepdims=True) + 1e-06)

    finish(early, early_mid, early_out, e1s, e2s, e3s, e3r)
    for index, place in enumerate((3, 4, 5, 6)):
        emit(early_out, index, place)
    scale = float(ROWS * n_x * n_y * n_z) ** (-0.5)
    gains_o[...] = early_out[0, c_rows : c_rows + 2, :].astype(F32) * scale
    pool_done(pg, pg_s, pg_r)
    pool_done(pf, pf_s, pf_r)
    gather_out(late_mid, late_out, l2s, l2r, l3s, l3r)
    finish(late, late_mid, late_out, l1s, l2s, l3s, l3r)
    for index, place in enumerate((0, 1, 2, 7)):
        emit(late_out, index, place)


def pass_on(*refs):
    sems = refs[-1]
    copies = [pltpu.make_async_copy(a, b, sems.at[i]) for i, (a, b) in enumerate(zip(refs[:4], refs[4:8]))]
    for c in copies:
        c.start()
    for c in copies:
        c.wait()


def solution(mesh):
    sizes = tuple(mesh.shape[name] for name in ("gx", "gy", "gz"))
    n_a, n_b, n_z = sizes[0] * sizes[2], sizes[1], sizes[2]
    c_rows = 4 * W // n_a
    tiles = ROWS // TILE
    edges = TILE * NEIGH
    v = pltpu.VMEM
    dma = pltpu.SemaphoreType.DMA

    def reduce_bufs(rows):
        return [v((n_a, rows, W), BF16), v((n_a, rows, W), BF16), v((n_b, rows, W), BF16), v((n_a, rows, W), BF16)]

    scratch = [
        v((GHOSTS, W), BF16),
        v((GHOSTS, W), BF16),
        v((GHOSTS, W), BF16),
        v((GHOSTS, W), BF16),
        v((n_z, W, CLUSTERS), BF16),
        v((n_z, W, CLUSTERS), BF16),
        *reduce_bufs(c_rows + GAIN_ROWS),
        *reduce_bufs(c_rows),
        v((W, ROWS), BF16),
        v((W, ROWS), BF16),
        v((4 * TILE, ROWS), BF16),
        v((CLUSTERS, ROWS), BF16),
        v((W, ROWS), BF16),
        v((W, ROWS), BF16),
        v((W, GHOSTS), BF16),
        v((W, GHOSTS), BF16),
        v((W, ROWS), F32),
        v((W, 2 * W), BF16),
        v((W, 2 * W), BF16),
        v((W, 2 * W), BF16),
        v((tiles, SLOTS, edges), BF16),
        v((tiles, W, edges), BF16),
        v((tiles, W, edges), BF16),
        v((tiles, W, edges), BF16),
        v((tiles, 1, edges), F32),
        v((W, ROWS), F32),
        v((W, ROWS), BF16),
        v((W, ROWS), BF16),
        v((W, ROWS), F32),
        v((W, ROWS), F32),
        v((1, ROWS), F32),
        v((W, ROWS), BF16),
        v((W, ROWS), F32),
        v((W, ROWS), BF16),
        v((W, ROWS), BF16),
        v((W, ROWS), F32),
        v((W, ROWS), BF16),
        v((2, W, edges), BF16),
        v((2, W, edges), BF16),
        v((ROWS + TILE, W), F32),
        v((GHOSTS, W), F32),
        v((W, W), F32),
        v((2, W, W), F32),
        dma((4,)), dma((4,)), dma((4,)), dma((4,)),
        dma((n_z,)), dma((n_z,)), dma((n_z,)), dma((n_z,)),
        *[dma for _ in range(12)],
        v((ROWS, W), BF16), v((ROWS, W), BF16), v((NEIGH, ROWS), jnp.int32), v((4, TILE), jnp.int32),
        v((1, ROWS), jnp.int32), *[v((W, W), BF16) for _ in range(8)], v((1, W), F32), v((1, W), F32),
        dma((15,)),
    ]

    def step(latents, grad_mixed, neighbours, send_list, cluster, w_send, w_recv, w_edge, edge_gain, w_self, w_agg,
             w_node, node_gain, w_pool_in, w_pool_out):
        results = pl.pallas_call(
            functools.partial(kernel, sizes),
            out_shape=(
                jax.ShapeDtypeStruct((ROWS, W), BF16),
                jax.ShapeDtypeStruct((ROWS, W), F32),
                jax.ShapeDtypeStruct((8, W, W), F32),
                jax.ShapeDtypeStruct((2, W), F32),
            ),
            in_specs=[pl.BlockSpec(memory_space=pltpu.HBM)] * 15,
            out_specs=tuple([pl.BlockSpec(memory_space=pltpu.VMEM)] * 4),
            scratch_shapes=scratch,
            compiler_params=pltpu.CompilerParams(
                collective_id=0, has_side_effects=True, vmem_limit_bytes=44 * 1024 * 1024
            ),
        )(*[pltpu.with_memory_space_constraint(x, pltpu.HBM) for x in (
            latents, grad_mixed, neighbours.T, send_list, cluster.reshape(1, ROWS), w_send, w_recv, w_edge, w_self,
            w_agg, w_node, w_pool_in, w_pool_out, edge_gain.reshape(1, W), node_gain.reshape(1, W))])
        return pl.pallas_call(
            pass_on,
            out_shape=tuple(jax.ShapeDtypeStruct(r.shape, r.dtype) for r in results),
            in_specs=[pl.BlockSpec(memory_space=pltpu.VMEM)] * 4,
            out_specs=tuple([pl.BlockSpec(memory_space=pltpu.HBM)] * 4),
            scratch_shapes=[pltpu.SemaphoreType.DMA((4,))],
            compiler_params=pltpu.CompilerParams(vmem_limit_bytes=8 * 1024 * 1024),
        )(*results)

    rows = P(("gx", "gy", "gz"), None)
    in_specs = (rows, rows, rows, rows, P(("gx", "gy", "gz"))) + (P(),) * 10
    out_specs = (rows, rows, P(), P())
    return jax.shard_map(step, mesh=mesh, in_specs=in_specs, out_specs=out_specs, check_vma=False)
```

```python
import functools

import jax
import jax.numpy as jnp
from jax import lax
from jax.experimental import pallas as pl
from jax.experimental.pallas import tpu as pltpu
from jax.sharding import PartitionSpec as P

EPS = 1e-05
W = 128
ROWS = 1024
NEIGH = 16
TILE = 64
PAIRS = ROWS // W
GHOSTS = 512
CLUSTERS = 256
SLOTS = 192
CHUNK = 256
STEPS = TILE * NEIGH // CHUNK
NODE = 256
GAIN_ROWS = 16
F32 = jnp.float32
BF16 = jnp.bfloat16
MESH = pl.DeviceIdType.MESH


def mm(a, b):
    return lax.dot_general(a, b, (((1,), (0,)), ((), ())), preferred_element_type=F32)


def nt(a, b):
    return lax.dot_general(a, b, (((1,), (1,)), ((), ())), preferred_element_type=F32)


def sigmoid(v):
    return 0.5 * jnp.tanh(0.5 * v) + 0.5


def mean0(v):
    return jnp.sum(v, axis=0, keepdims=True) * (1.0 / W)


def norm_centred(centred):
    inv = lax.rsqrt(mean0(centred * centred) + EPS)
    return centred * inv, inv


def half_silu(h):
    t = jnp.tanh(h)
    up = 1.0 + t
    act = h * up
    return act, up + act * (1.0 - t)


def narrow_half_silu(h):
    h = h.astype(BF16)
    t = jnp.tanh(h)
    one = jnp.ones((), BF16)
    up = one + t
    act = h * up
    return act, up + act * (one - t)


def rows_of(row):
    return jnp.concatenate([jnp.broadcast_to(row, (16, row.shape[1])).astype(BF16)] * (W // 16), axis=0)


def centred_pair(w):
    w_t = jnp.transpose(w.astype(F32))
    centred = w_t - mean0(w_t)
    high = centred.astype(BF16)
    return jnp.concatenate([high, (centred - high.astype(F32)).astype(BF16)], axis=1)


def beside(parts):
    return jnp.concatenate(parts, axis=1)


def twice(v):
    return jnp.concatenate([v, v], axis=0)


def one_hot(row, ids):
    wide = jnp.broadcast_to(row, (16, W)).astype(BF16)
    same = jnp.concatenate([wide] * (ids.shape[0] // 16), axis=0) == ids
    return jnp.where(same, jnp.ones((), BF16), jnp.zeros((), BF16))


def low_half():
    return lax.broadcasted_iota(jnp.int32, (W, W), 1) < TILE


def swap(v):
    return pltpu.roll(v, TILE, 1)


def spread_halves(block, low):
    other = swap(block)
    return jnp.where(low, block, other), jnp.where(low, other, block)


def column_of(row):
    return jnp.transpose(jnp.broadcast_to(row, (W, W)))


def kernel(sizes, *refs):
    far, near, in_sems = refs[:15], refs[-16:-1], refs[-1]
    (lat, gm, nb, send, clus, w_send, w_recv, w_edge, w_self, w_agg, w_node, w_pin, w_pout, egain, ngain) = near
    mixed_o, grad_o, mats_o, gains_o = refs[15:19]
    (sbuf, ghost, ret, backbuf, pg, pf, early, early_in, early_mid, early_out, late, late_in, late_mid, late_out,
     lat_t, gm_t, oh_send, oh_clus, tab, tab_sh, gtab, gtab_sh, recv_t, wsa_t, we_c, wn_c, delta,
     oh_all, act_all, slope_all, norm_all, inv_all, sum_t, agg_t, an_t, nslope_t, nn_t, ninv_t, fine_t, gfine_t,
     gy_t, gpn_t, gc_t, grecv_t, gp_own, gp_ghost, dw_edge, sums) = refs[19:67]
    (halo_s, halo_r, ret_s, ret_r, pg_s, pg_r, pf_s, pf_r,
     e1s, e1r, e2s, e2r, e3s, e3r, l1s, l1r, l2s, l2r, l3s, l3r) = refs[67:-16]
    loads = [pltpu.make_async_copy(a, b, in_sems.at[i]) for i, (a, b) in enumerate(zip(far, near))]
    for i in (3, 0, 1, 4, *range(5, 15), 2):
        loads[i].start()

    n_x, n_y, n_z = sizes
    n_a, n_b = n_x * n_z, n_y
    c_rows = 4 * W // n_a
    gx, gy, gz = lax.axis_index("gx"), lax.axis_index("gy"), lax.axis_index("gz")
    x_up = (lax.rem(gx + 1, n_x), gy, gz)
    x_low = (lax.rem(gx + n_x - 1, n_x), gy, gz)
    y_up = (gx, lax.rem(gy + 1, n_y), gz)
    y_low = (gx, lax.rem(gy + n_y - 1, n_y), gz)
    y_now, z_high = lax.div(gx, 2), lax.rem(gx, 2)
    z_low, core = lax.div(gy, 2), lax.rem(gy, 2)
    n_yc, n_zl = n_x // 2, n_y // 2
    z_now = z_high * n_zl + z_low
    rank_a, rank_b = (y_now * 2 + core) * n_z + gz, z_now

    def hops(step, n):
        return min(step, n - step)

    ys = [lax.rem(y_now + d, n_yc) for d in range(n_yc)]
    cs = [core, 1 - core]
    xs = [lax.rem(gz + d, n_z) for d in range(n_z)]
    order = sorted(
        [(d, e, f) for d in range(n_yc) for e in range(2) for f in range(n_z)][1:],
        key=lambda o: (-hops(o[0], n_yc) - hops(o[2], n_z), o),
    )
    plane = [
        ((ys[d] * 2 + cs[e]) * n_z + xs[f], (ys[d] * 2 + z_high, z_low * 2 + cs[e], xs[f])) for d, e, f in order
    ]
    zs = [lax.rem(z_now + d, n_b) for d in sorted(range(1, n_b), key=lambda d: (-hops(d, n_b), d))]
    column = [(z, (y_now * 2 + lax.div(z, n_zl), lax.rem(z, n_zl) * 2 + core, gz)) for z in zs]
    row = [(xs[d], (gx, gy, xs[d])) for d in sorted(range(1, n_z), key=lambda d: (-hops(d, n_z), d))]

    def remote(src, dst, s, r, dev):
        return pltpu.make_async_remote_copy(
            src_ref=src, dst_ref=dst, send_sem=s, recv_sem=r, device_id=dev, device_id_type=MESH
        )

    def drain(ref, sem):
        pltpu.make_async_copy(ref, ref, sem).wait()

    barrier = pltpu.get_barrier_semaphore()
    for dev in (x_up, x_low, y_up, y_low, *[d for _, d in plane], *[d for _, d in column]):
        pl.semaphore_signal(barrier, inc=1, device_id=dev, device_id_type=MESH)

    lane_row = lax.broadcasted_iota(jnp.int32, (TILE, W), 1)
    loads[3].wait()
    send_f = send[...].astype(F32)
    for q in range(4):
        col = jnp.transpose(jnp.broadcast_to(send_f[q : q + 1, :], (W, TILE))).astype(jnp.int32)
        for b in range(PAIRS):
            hot = jnp.where(col == lane_row + b * W, 1.0, 0.0).astype(BF16)
            oh_send[q * TILE : (q + 1) * TILE, b * W : (b + 1) * W] = hot
    loads[0].wait()
    cells = mm(oh_send[...], lat[...]).astype(BF16)
    for slot, q in enumerate((2, 3, 0, 1, 1, 3, 0, 2)):
        sbuf[slot * TILE : (slot + 1) * TILE, :] = cells[q * TILE : (q + 1) * TILE, :]
    pl.semaphore_wait(barrier, 4 + n_a - 1 + n_b - 1)
    halo_to = (x_up, x_low, y_up, y_low)
    halo = [
        remote(sbuf.at[pl.ds(q * W, W)], ghost.at[pl.ds(q * W, W)], halo_s.at[q], halo_r.at[q], halo_to[q])
        for q in range(4)
    ]
    for q in (2, 3, 0, 1):
        halo[q].start()

    eye = jnp.where(
        lax.broadcasted_iota(jnp.int32, (W, W), 0) == lax.broadcasted_iota(jnp.int32, (W, W), 1), 1.0, 0.0
    ).astype(BF16)
    loads[1].wait()
    loads[4].wait()
    gm_t[...] = nt(eye, gm[...]).astype(BF16)
    cl_id = lax.broadcasted_iota(jnp.int32, (CLUSTERS, W), 0).astype(F32).astype(BF16)
    clus_f = clus[...].astype(F32)
    for b in range(PAIRS):
        oh_clus[:, b * W : (b + 1) * W] = one_hot(clus_f[:, b * W : (b + 1) * W], cl_id)

    def pool_send(buf, s, r):
        for _, dev in row:
            remote(buf.at[gz], buf.at[gz], s, r, dev).start()

    def pool_wait(buf, r):
        drain(buf.at[pl.ds(0, n_z - 1)], r)

    pg[gz] = nt(gm_t[...], oh_clus[...]).astype(BF16)
    pool_send(pg, pg_s, pg_r)

    lat_t[...] = nt(eye, lat[...]).astype(BF16)
    for i in (*range(5, 15), 2):
        loads[i].wait()
    wsend_t = (jnp.transpose(w_send[...].astype(F32)) * 0.5).astype(BF16)
    wrecv_t = (jnp.transpose(w_recv[...].astype(F32)) * 0.5).astype(BF16)
    we_c[...] = centred_pair(w_edge[...])
    wn_c[...] = centred_pair(w_node[...])
    wsa_t[:, :W] = (jnp.transpose(w_self[...].astype(F32)) * 0.5).astype(BF16)
    wsa_t[:, W:] = (jnp.transpose(w_agg[...].astype(F32)) * 0.5).astype(BF16)
    w_edge_h = (w_edge[...].astype(F32) * 0.5).astype(BF16)
    w_node_h = (w_node[...].astype(F32) * 0.5).astype(BF16)
    tab[...] = mm(wsend_t, lat_t[...]).astype(BF16)
    lat_roll = jnp.concatenate([lat[TILE:, :], lat[:TILE, :]], axis=0)
    tab_sh[...] = nt(wsend_t, lat_roll).astype(BF16)
    recv_t[...] = mm(wrecv_t, lat_t[...]).astype(BF16).astype(F32)
    eg = column_of(egain[...])
    ng = column_of(ngain[...])

    def ghost_tables(first):
        part = slice(first, first + 2 * W)
        own = ghost[part, :]
        gtab[:, part] = nt(wsend_t, own).astype(BF16)
        gtab_sh[:, part] = nt(wsend_t, jnp.concatenate([own[TILE:, :], own[:TILE, :]], axis=0)).astype(BF16)

    def forward(u, carry):
        low = low_half()
        slot_id = lax.broadcasted_iota(jnp.int32, (SLOTS, W), 0).astype(F32).astype(BF16)
        at = pl.multiple_of(u * W, W)
        at_g = pl.multiple_of(lax.rem(u, GHOSTS // W) * W, W)
        picks = nb[:, pl.ds(at, W)]
        low8 = low[:8, :]
        first, second = picks[:8, :], picks[8:, :]
        picks_of = (jnp.where(low8, first, swap(second)), jnp.where(low8, swap(first), second))
        recv_of = spread_halves(recv_t[:, pl.ds(at, W)], low)
        sums_of = []
        for half in range(2):
            t = 2 * u + half
            chosen = picks_of[half]
            local = jnp.where(chosen >= ROWS, (chosen & (TILE - 1)) + 2 * TILE, (chosen - t * TILE) & (ROWS - 1))
            local = local.astype(F32)
            own, far = (tab, gtab) if half == 0 else (tab_sh, gtab_sh)
            window = jnp.concatenate([own[:, pl.ds(at, W)], far[:, pl.ds(at_g, TILE)]], axis=1)
            total = None
            for q in range(STEPS):
                lanes = slice(q * CHUNK, (q + 1) * CHUNK)
                hot = jnp.concatenate([one_hot(local[c : c + 1, :], slot_id) for c in (2 * q, 2 * q + 1)], axis=1)
                oh_all[t, :, lanes] = hot
                act_b, slope = narrow_half_silu(mm(window, hot) + jnp.concatenate([recv_of[half]] * 2, axis=1))
                act_all[t, :, lanes] = act_b
                slope_all[t, :, lanes] = slope
                normed, inv = norm_centred(mm(we_c[...], twice(act_b)))
                norm_all[t, :, lanes] = normed.astype(BF16)
                inv_all[t, :, lanes] = inv
                part = normed[:, :W] + normed[:, W:]
                total = part if total is None else total + part
            sums_of.append(total + swap(total))
        total = jnp.where(low, sums_of[0], sums_of[1])
        sum_t[:, pl.ds(at, W)] = total
        agg_t[:, pl.ds(at, W)] = (total * eg).astype(BF16)
        return carry

    halo[2].wait()
    halo[3].wait()
    ghost_tables(2 * W)
    lax.fori_loop(0, PAIRS // 4, lambda k, c: forward(k * 4 + 3, forward(k * 4 + 2, c)), 0)
    halo[0].wait()
    halo[1].wait()
    ghost_tables(0)
    lax.fori_loop(0, PAIRS // 4, lambda k, c: forward(k * 4 + 1, forward(k * 4, c)), 0)

    def node_forward(u, carry):
        at = pl.multiple_of(u * NODE, NODE)
        lat_b = lat_t[:, pl.ds(at, NODE)]
        an, slope = half_silu(mm(wsa_t[...], jnp.concatenate([lat_b, agg_t[:, pl.ds(at, NODE)]], axis=0)))
        an_b = an.astype(BF16)
        an_t[:, pl.ds(at, NODE)] = an_b
        nslope_t[:, pl.ds(at, NODE)] = slope
        nn, ninv = norm_centred(mm(wn_c[...], twice(an_b)))
        nn_t[:, pl.ds(at, NODE)] = nn
        ninv_t[:, pl.ds(at, NODE)] = ninv
        fine_t[:, pl.ds(at, NODE)] = (lat_b.astype(F32) + nn * widen(ng)).astype(BF16)
        return carry

    def widen(v):
        return jnp.concatenate([v] * (NODE // W), axis=1)

    lax.fori_loop(0, ROWS // NODE // 2, lambda k, c: node_forward(2 * k + 1, node_forward(2 * k, c)), 0)

    pf[gz] = nt(fine_t[...], oh_clus[...]).astype(BF16)
    pool_send(pf, pf_s, pf_r)
    wpin_t = jnp.transpose(w_pin[...].astype(F32)).astype(BF16)
    wpout_t = jnp.transpose(w_pout[...].astype(F32)).astype(BF16)
    pool_wait(pg, pg_r)
    gd = pg[0].astype(F32)
    for k in range(1, n_z):
        gd = gd + pg[k].astype(F32)
    gd_b = gd.astype(BF16)
    gac = mm(w_pout[...], gd_b)
    pool_wait(pf, pf_r)
    pooled = pf[0].astype(F32)
    for k in range(1, n_z):
        pooled = pooled + pf[k].astype(F32)
    pooled_b = pooled.astype(BF16)
    pc = mm(wpin_t, pooled_b)
    s = sigmoid(pc)
    ac = pc * s
    ac_b = ac.astype(BF16)
    delta_b = mm(wpout_t, ac_b).astype(BF16)
    gpc_b = (gac * (s + ac * (1.0 - s))).astype(BF16)
    gpool_b = mm(w_pin[...], gpc_b).astype(BF16)
    delta[...] = delta_b
    dw_pin = nt(pooled_b, gpc_b) * (1.0 / n_z)
    dw_pout = nt(ac_b, gd_b) * (1.0 / n_z)

    sums[...] = jnp.zeros_like(sums)

    def node_back(u, carry):
        at = pl.multiple_of(u * NODE, NODE)
        gf = gm_t[:, pl.ds(at, NODE)].astype(F32) + mm(gpool_b, oh_clus[:, pl.ds(at, NODE)])
        gfine_t[:, pl.ds(at, NODE)] = gf
        nn = nn_t[:, pl.ds(at, NODE)]
        sums[1] += narrow(gf * nn)
        gn = gf * widen(ng)
        gy_b = ((gn - mean0(gn) - nn * mean0(gn * nn)) * ninv_t[:, pl.ds(at, NODE)]).astype(BF16)
        gy_t[:, pl.ds(at, NODE)] = gy_b
        gpn_b = (mm(w_node_h, gy_b) * nslope_t[:, pl.ds(at, NODE)]).astype(BF16)
        gpn_t[:, pl.ds(at, NODE)] = gpn_b
        ga = mm(w_agg[...], gpn_b)
        sums[0] += narrow(ga * sum_t[:, pl.ds(at, NODE)])
        g = ga * widen(eg)
        gc_t[:, pl.ds(at, NODE)] = g - mean0(g)
        return carry

    def narrow(v):
        total = v[:, :W]
        for b in range(1, NODE // W):
            total = total + v[:, b * W : (b + 1) * W]
        return total

    lax.fori_loop(0, ROWS // NODE // 2, lambda k, c: node_back(2 * k + 1, node_back(2 * k, c)), 0)

    def put(buf, index, mat, width):
        per = W // c_rows
        buf[index * per : (index + 1) * per, :c_rows, :] = mat.reshape(per, c_rows, W).astype(BF16)

    def reduce_out(buf, into, s, r):
        into[rank_a] = buf[rank_a]

        for to, dev in plane:
            remote(buf.at[to], into.at[rank_a], s, r, dev).start()

    def reduce_mid(buf, into, mid, s, r, s2, r2):
        drain(into.at[pl.ds(0, n_a - 1)], r)
        total = into[0].astype(F32)
        for k in range(1, n_a):
            total = total + into[k].astype(F32)
        mid[rank_b] = total.astype(BF16)
        for _, dev in column:
            remote(mid.at[rank_b], mid.at[rank_b], s2, r2, dev).start()

    def gather_out(mid, out, s2, r2, s3, r3):
        drain(mid.at[pl.ds(0, n_b - 1)], r2)
        total = mid[0].astype(F32)
        for k in range(1, n_b):
            total = total + mid[k].astype(F32)
        out[rank_a] = total.astype(BF16)
        for _, dev in plane:
            remote(out.at[rank_a], out.at[rank_a], s3, r3, dev).start()

    def finish(buf, mid, out, s, s2, s3, r3):
        drain(out.at[pl.ds(0, n_a - 1)], r3)
        drain(buf.at[pl.ds(0, n_a - 1)], s)
        drain(mid.at[pl.ds(0, n_b - 1)], s2)
        drain(out.at[pl.ds(0, n_a - 1)], s3)

    def row_sums(v):
        hi = v.astype(BF16)
        lo = (v - hi.astype(F32)).astype(BF16)
        ones = jnp.ones((GAIN_ROWS, W), BF16)
        return nt(ones, hi) + nt(ones, lo)

    dw_sa = nt(jnp.concatenate([lat_t[...], agg_t[...]], axis=0), gpn_t[...])
    put(early, 0, dw_sa[:W, :], c_rows)
    put(early, 1, dw_sa[W:, :], c_rows)
    put(early, 2, nt(an_t[...], gy_t[...]), c_rows)
    put(early, 3, dw_pin, c_rows)
    which = lax.broadcasted_iota(jnp.int32, (GAIN_ROWS, W), 0)
    gain_rows = jnp.where(which == 0, row_sums(sums[0]), row_sums(sums[1])).astype(BF16)
    for k in range(n_a):
        early[k, c_rows:, :] = gain_rows
    reduce_out(early, early_in, e1s, e1r)

    gp_own[...] = jnp.zeros_like(gp_own)
    gp_ghost[...] = jnp.zeros_like(gp_ghost)
    dw_edge[...] = jnp.zeros_like(dw_edge)

    def backward(u, carry):
        low = low_half()
        at = pl.multiple_of(u * W, W)
        at_g = pl.multiple_of(lax.rem(u, GHOSTS // W) * W, W)
        gc_of = spread_halves(gc_t[:, pl.ds(at, W)], low)
        back_of = []
        for half in range(2):
            t = 2 * u + half
            gzs, gps = [], []
            gc = jnp.concatenate([gc_of[half].astype(BF16)] * 2, axis=1)
            total = None
            for q in range(STEPS):
                lanes = slice(q * CHUNK, (q + 1) * CHUNK)
                normed = norm_all[t, :, lanes]
                shared = rows_of(mean0((gc * normed).astype(F32)))
                gz_b = (gc - normed * shared) * rows_of(inv_all[t, :, lanes])
                gzs.append(gz_b)
                gpre_b = mm(w_edge_h, gz_b).astype(BF16) * slope_all[t, :, lanes]
                gps.append(gpre_b)
                gpre = gpre_b.astype(F32)
                part = gpre[:, :W] + gpre[:, W:]
                total = part if total is None else total + part
            dw_edge[...] += nt(act_all[t], beside(gzs))
            window = nt(oh_all[t], beside(gps))
            gp_own[pl.ds(at + half * TILE, W), :] += window[:W, :]
            gp_ghost[pl.ds(at_g + half * TILE, TILE), :] += window[W:, :]
            back_of.append(total + swap(total))
        grecv_t[:, pl.ds(at, W)] = jnp.where(low, back_of[0], back_of[1]).astype(BF16)
        return carry

    back_to = (x_low, x_up, y_low, y_up)
    back = [
        remote(backbuf.at[pl.ds(q * W, W)], ret.at[pl.ds(q * W, W)], ret_s.at[q], ret_r.at[q], back_to[q])
        for q in range(4)
    ]
    lax.fori_loop(0, PAIRS // 4, lambda k, c: backward(k * 4 + 1, backward(k * 4, c)), 0)
    backbuf[: 2 * W, :] = gp_ghost[: 2 * W, :].astype(BF16)
    back[0].start()
    back[1].start()

    def backward_near(k, c):
        @pl.when(k == 1)
        def _():
            reduce_mid(early, early_in, early_mid, e1s, e1r, e2s, e2r)

        return backward(k * 4 + 3, backward(k * 4 + 2, c))

    lax.fori_loop(0, PAIRS // 4, backward_near, 0)
    backbuf[2 * W :, :] = gp_ghost[2 * W :, :].astype(BF16)
    back[2].start()
    back[3].start()

    gp_own[:TILE, :] += gp_own[ROWS:, :]
    own_b = gp_own[:ROWS, :].astype(BF16)
    ghost_t = nt(eye, ghost[...]).astype(BF16)
    put(late, 0, mm(lat_t[...], own_b) + mm(ghost_t, backbuf[...]), c_rows)
    put(late, 1, nt(lat_t[...], grecv_t[...]), c_rows)
    put(late, 2, dw_edge[...], c_rows)
    put(late, 3, dw_pout, c_rows)
    reduce_out(late, late_in, l1s, l1r)

    gfine_t[...] += (
        mm(w_self[...], gpn_t[...]) + mm(w_recv[...], grecv_t[...]) + nt(w_send[...], own_b)
    )
    for c in back:
        c.wait()
    side_a = jnp.concatenate([ret[q * TILE : (q + 1) * TILE, :] for q in (2, 3, 0, 1)], axis=0)
    side_b = jnp.concatenate([ret[q * TILE : (q + 1) * TILE, :] for q in (6, 4, 7, 5)], axis=0)
    ret_t = (nt(w_send[...], side_a) + nt(w_send[...], side_b)).astype(BF16)
    gfine_t[...] += mm(ret_t, oh_send[...])
    gather_out(early_mid, early_out, e2s, e2r, e3s, e3r)
    mixed = fine_t[...].astype(F32) + mm(delta[...], oh_clus[...])
    for b in range(PAIRS):
        mixed_o[b * W : (b + 1) * W, :] = jnp.transpose(mixed[:, b * W : (b + 1) * W]).astype(BF16)
    reduce_mid(late, late_in, late_mid, l1s, l1r, l2s, l2r)
    for b in range(PAIRS):
        grad_o[b * W : (b + 1) * W, :] = jnp.transpose(gfine_t[:, b * W : (b + 1) * W])

    def emit(out, index, place):
        per = W // c_rows
        mat = out[index * per : (index + 1) * per, :c_rows, :].astype(F32).reshape(W, W)
        mats_o[place] = mat * lax.rsqrt(jnp.mean(mat * mat, keepdims=True) + 1e-06)

    finish(early, early_mid, early_out, e1s, e2s, e3s, e3r)
    for index, place in enumerate((3, 4, 5, 6)):
        emit(early_out, index, place)
    scale = float(ROWS * n_x * n_y * n_z) ** (-0.5)
    gains_o[...] = early_out[0, c_rows : c_rows + 2, :].astype(F32) * scale
    pool_wait(pg, pg_s)
    pool_wait(pf, pf_s)
    gather_out(late_mid, late_out, l2s, l2r, l3s, l3r)
    finish(late, late_mid, late_out, l1s, l2s, l3s, l3r)
    for index, place in enumerate((0, 1, 2, 7)):
        emit(late_out, index, place)


def pass_on(*refs):
    sems = refs[-1]
    copies = [pltpu.make_async_copy(a, b, sems.at[i]) for i, (a, b) in enumerate(zip(refs[:4], refs[4:8]))]
    for c in copies:
        c.start()
    for c in copies:
        c.wait()


def solution(mesh):
    sizes = tuple(mesh.shape[name] for name in ("gx", "gy", "gz"))
    n_a, n_b, n_z = sizes[0] * sizes[2], sizes[1], sizes[2]
    c_rows = 4 * W // n_a
    tiles = ROWS // TILE
    edges = TILE * NEIGH
    v = pltpu.VMEM
    dma = pltpu.SemaphoreType.DMA

    def reduce_bufs(rows):
        return [v((n_a, rows, W), BF16), v((n_a, rows, W), BF16), v((n_b, rows, W), BF16), v((n_a, rows, W), BF16)]

    scratch = [
        v((GHOSTS, W), BF16),
        v((GHOSTS, W), BF16),
        v((GHOSTS, W), BF16),
        v((GHOSTS, W), BF16),
        v((n_z, W, CLUSTERS), BF16),
        v((n_z, W, CLUSTERS), BF16),
        *reduce_bufs(c_rows + GAIN_ROWS),
        *reduce_bufs(c_rows),
        v((W, ROWS), BF16),
        v((W, ROWS), BF16),
        v((4 * TILE, ROWS), BF16),
        v((CLUSTERS, ROWS), BF16),
        v((W, ROWS), BF16),
        v((W, ROWS), BF16),
        v((W, GHOSTS), BF16),
        v((W, GHOSTS), BF16),
        v((W, ROWS), F32),
        v((W, 2 * W), BF16),
        v((W, 2 * W), BF16),
        v((W, 2 * W), BF16),
        v((W, CLUSTERS), BF16),
        v((tiles, SLOTS, edges), BF16),
        v((tiles, W, edges), BF16),
        v((tiles, W, edges), BF16),
        v((tiles, W, edges), BF16),
        v((tiles, 1, edges), F32),
        v((W, ROWS), F32),
        v((W, ROWS), BF16),
        v((W, ROWS), BF16),
        v((W, ROWS), F32),
        v((W, ROWS), F32),
        v((1, ROWS), F32),
        v((W, ROWS), BF16),
        v((W, ROWS), F32),
        v((W, ROWS), BF16),
        v((W, ROWS), BF16),
        v((W, ROWS), F32),
        v((W, ROWS), BF16),
        v((ROWS + TILE, W), F32),
        v((GHOSTS, W), F32),
        v((W, W), F32),
        v((2, W, W), F32),
        dma((4,)), dma((4,)), dma((4,)), dma((4,)),
        *[dma for _ in range(16)],
        v((ROWS, W), BF16), v((ROWS, W), BF16), v((NEIGH, ROWS), jnp.int32), v((4, TILE), jnp.int32),
        v((1, ROWS), jnp.int32), *[v((W, W), BF16) for _ in range(8)], v((1, W), F32), v((1, W), F32),
        dma((15,)),
    ]

    def step(latents, grad_mixed, neighbours, send_list, cluster, w_send, w_recv, w_edge, edge_gain, w_self, w_agg,
             w_node, node_gain, w_pool_in, w_pool_out):
        results = pl.pallas_call(
            functools.partial(kernel, sizes),
            out_shape=(
                jax.ShapeDtypeStruct((ROWS, W), BF16),
                jax.ShapeDtypeStruct((ROWS, W), F32),
                jax.ShapeDtypeStruct((8, W, W), F32),
                jax.ShapeDtypeStruct((2, W), F32),
            ),
            in_specs=[pl.BlockSpec(memory_space=pltpu.HBM)] * 15,
            out_specs=tuple([pl.BlockSpec(memory_space=pltpu.VMEM)] * 4),
            scratch_shapes=scratch,
            compiler_params=pltpu.CompilerParams(
                collective_id=0, has_side_effects=True, vmem_limit_bytes=44 * 1024 * 1024
            ),
        )(*[pltpu.with_memory_space_constraint(x, pltpu.HBM) for x in (
            latents, grad_mixed, neighbours.T, send_list, cluster.reshape(1, ROWS), w_send, w_recv, w_edge, w_self,
            w_agg, w_node, w_pool_in, w_pool_out, edge_gain.reshape(1, W), node_gain.reshape(1, W))])
        return pl.pallas_call(
            pass_on,
            out_shape=tuple(jax.ShapeDtypeStruct(r.shape, r.dtype) for r in results),
            in_specs=[pl.BlockSpec(memory_space=pltpu.VMEM)] * 4,
            out_specs=tuple([pl.BlockSpec(memory_space=pltpu.HBM)] * 4),
            scratch_shapes=[pltpu.SemaphoreType.DMA((4,))],
            compiler_params=pltpu.CompilerParams(vmem_limit_bytes=8 * 1024 * 1024),
        )(*results)

    rows = P(("gx", "gy", "gz"), None)
    in_specs = (rows, rows, rows, rows, P(("gx", "gy", "gz"))) + (P(),) * 10
    out_specs = (rows, rows, P(), P())
    return jax.shard_map(step, mesh=mesh, in_specs=in_specs, out_specs=out_specs, check_vma=False)
```

```python
import functools

import jax
import jax.numpy as jnp
from jax import lax
from jax.experimental import pallas as pl
from jax.experimental.pallas import tpu as pltpu
from jax.sharding import PartitionSpec as P

EPS = 1e-05
W = 128
ROWS = 1024
NEIGH = 16
TILE = 64
PAIRS = ROWS // W
GHOSTS = 512
CLUSTERS = 256
SLOTS = 192
CHUNK = 256
STEPS = TILE * NEIGH // CHUNK
NODE = 256
GAIN_ROWS = 16
F32 = jnp.float32
BF16 = jnp.bfloat16
MESH = pl.DeviceIdType.MESH


def mm(a, b):
    return lax.dot_general(a, b, (((1,), (0,)), ((), ())), preferred_element_type=F32)


def nt(a, b):
    return lax.dot_general(a, b, (((1,), (1,)), ((), ())), preferred_element_type=F32)


def sigmoid(v):
    return 0.5 * jnp.tanh(0.5 * v) + 0.5


def mean0(v):
    return jnp.sum(v, axis=0, keepdims=True) * (1.0 / W)


def norm_centred(centred):
    inv = lax.rsqrt(mean0(centred * centred) + EPS)
    return centred * inv, inv


def half_silu(h):
    t = jnp.tanh(h)
    up = 1.0 + t
    act = h * up
    return act, up + act * (1.0 - t)


def narrow_half_silu(h):
    h = h.astype(BF16)
    t = jnp.tanh(h)
    one = jnp.ones((), BF16)
    return h * (one + t), t


def rows_of(row):
    return jnp.concatenate([jnp.broadcast_to(row, (16, row.shape[1])).astype(BF16)] * (W // 16), axis=0)


def centred_pair(w):
    w_t = jnp.transpose(w.astype(F32))
    centred = w_t - mean0(w_t)
    high = centred.astype(BF16)
    return jnp.concatenate([high, (centred - high.astype(F32)).astype(BF16)], axis=1)


def beside(parts):
    return jnp.concatenate(parts, axis=1)


def beside(parts):
    return jnp.concatenate(parts, axis=1)


def twice(v):
    return jnp.concatenate([v, v], axis=0)


def one_hot(row, ids):
    wide = jnp.broadcast_to(row, (16, W)).astype(BF16)
    same = jnp.concatenate([wide] * (ids.shape[0] // 16), axis=0) == ids
    return jnp.where(same, jnp.ones((), BF16), jnp.zeros((), BF16))


def low_half():
    return lax.broadcasted_iota(jnp.int32, (W, W), 1) < TILE


def swap(v):
    return pltpu.roll(v, TILE, 1)


def spread_halves(block, low):
    other = swap(block)
    return jnp.where(low, block, other), jnp.where(low, other, block)


def column_of(row):
    return jnp.transpose(jnp.broadcast_to(row, (W, W)))


def kernel(sizes, *refs):
    far, near, in_sems = refs[:15], refs[-16:-1], refs[-1]
    (lat, gm, nb, send, clus, w_send, w_recv, w_edge, w_self, w_agg, w_node, w_pin, w_pout, egain, ngain) = near
    mixed_o, grad_o, mats_o, gains_o = refs[15:19]
    (sbuf, ghost, ret, backbuf, pg, pf, early, early_in, early_mid, early_out, late, late_in, late_mid, late_out,
     lat_t, gm_t, oh_send, oh_clus, tab, tab_sh, gtab, gtab_sh, recv_t, wsa_t, we_c, wn_c, delta, ghost_t,
     oh_all, act_cols, act_all, slope_all, norm_all, inv_all, sum_t, agg_t, an_t, nslope_t, nn_t, ninv_t, fine_t, gfine_t,
     gy_t, gpn_t, gc_t, grecv_t, gp_own, gp_ghost, dw_edge, sums) = refs[19:69]
    (halo_s, halo_r, ret_s, ret_r, pg_s, pg_r, pf_s, pf_r,
     e1s, e1r, e2s, e2r, e3s, e3r, l1s, l1r, l2s, l2r, l3s, l3r) = refs[69:-16]
    loads = [pltpu.make_async_copy(a, b, in_sems.at[i]) for i, (a, b) in enumerate(zip(far, near))]
    for i in (3, 0, 1, 4, *range(5, 15), 2):
        loads[i].start()

    n_x, n_y, n_z = sizes
    n_a, n_b = n_x * n_z, n_y
    c_rows = 4 * W // n_a
    gx, gy, gz = lax.axis_index("gx"), lax.axis_index("gy"), lax.axis_index("gz")
    x_up = (lax.rem(gx + 1, n_x), gy, gz)
    x_low = (lax.rem(gx + n_x - 1, n_x), gy, gz)
    y_up = (gx, lax.rem(gy + 1, n_y), gz)
    y_low = (gx, lax.rem(gy + n_y - 1, n_y), gz)
    y_now, z_high = lax.div(gx, 2), lax.rem(gx, 2)
    z_low, core = lax.div(gy, 2), lax.rem(gy, 2)
    n_yc, n_zl = n_x // 2, n_y // 2
    z_now = z_high * n_zl + z_low
    rank_a, rank_b = (y_now * 2 + core) * n_z + gz, z_now

    def hops(step, n):
        return min(step, n - step)

    ys = [lax.rem(y_now + d, n_yc) for d in range(n_yc)]
    cs = [core, 1 - core]
    xs = [lax.rem(gz + d, n_z) for d in range(n_z)]
    order = sorted(
        [(d, e, f) for d in range(n_yc) for e in range(2) for f in range(n_z)][1:],
        key=lambda o: (-hops(o[0], n_yc) - hops(o[2], n_z), o),
    )
    plane = [
        ((ys[d] * 2 + cs[e]) * n_z + xs[f], (ys[d] * 2 + z_high, z_low * 2 + cs[e], xs[f])) for d, e, f in order
    ]
    zs = [lax.rem(z_now + d, n_b) for d in sorted(range(1, n_b), key=lambda d: (-hops(d, n_b), d))]
    column = [(z, (y_now * 2 + lax.div(z, n_zl), lax.rem(z, n_zl) * 2 + core, gz)) for z in zs]
    row = [(xs[d], (gx, gy, xs[d])) for d in sorted(range(1, n_z), key=lambda d: (-hops(d, n_z), d))]

    def remote(src, dst, s, r, dev):
        return pltpu.make_async_remote_copy(
            src_ref=src, dst_ref=dst, send_sem=s, recv_sem=r, device_id=dev, device_id_type=MESH
        )

    def drain(ref, sem):
        pltpu.make_async_copy(ref, ref, sem).wait()

    barrier = pltpu.get_barrier_semaphore()
    for dev in (x_up, x_low, y_up, y_low, *[d for _, d in plane], *[d for _, d in column]):
        pl.semaphore_signal(barrier, inc=1, device_id=dev, device_id_type=MESH)

    lane_row = lax.broadcasted_iota(jnp.int32, (TILE, W), 1)
    loads[3].wait()
    send_f = send[...].astype(F32)
    for q in range(4):
        col = jnp.transpose(jnp.broadcast_to(send_f[q : q + 1, :], (W, TILE))).astype(jnp.int32)
        for b in range(PAIRS):
            hot = jnp.where(col == lane_row + b * W, 1.0, 0.0).astype(BF16)
            oh_send[q * TILE : (q + 1) * TILE, b * W : (b + 1) * W] = hot
    loads[0].wait()
    cells = mm(oh_send[...], lat[...]).astype(BF16)
    for slot, q in enumerate((2, 3, 0, 1, 1, 3, 0, 2)):
        sbuf[slot * TILE : (slot + 1) * TILE, :] = cells[q * TILE : (q + 1) * TILE, :]
    pl.semaphore_wait(barrier, 4 + n_a - 1 + n_b - 1)
    halo_to = (x_up, x_low, y_up, y_low)
    halo = [
        remote(sbuf.at[pl.ds(q * W, W)], ghost.at[pl.ds(q * W, W)], halo_s.at[q], halo_r.at[q], halo_to[q])
        for q in range(4)
    ]
    for q in (2, 3, 0, 1):
        halo[q].start()

    eye = jnp.where(
        lax.broadcasted_iota(jnp.int32, (W, W), 0) == lax.broadcasted_iota(jnp.int32, (W, W), 1), 1.0, 0.0
    ).astype(BF16)
    loads[1].wait()
    loads[4].wait()
    gm_t[...] = nt(eye, gm[...]).astype(BF16)
    cl_id = lax.broadcasted_iota(jnp.int32, (CLUSTERS, W), 0).astype(F32).astype(BF16)
    clus_f = clus[...].astype(F32)
    for b in range(PAIRS):
        oh_clus[:, b * W : (b + 1) * W] = one_hot(clus_f[:, b * W : (b + 1) * W], cl_id)

    def pool_send(buf, s, r):
        for _, dev in row:
            remote(buf.at[gz], buf.at[gz], s, r, dev).start()

    def pool_wait(buf, r):
        drain(buf.at[pl.ds(0, n_z - 1)], r)

    pg[gz] = nt(gm_t[...], oh_clus[...]).astype(BF16)
    pool_send(pg, pg_s, pg_r)

    lat_t[...] = nt(eye, lat[...]).astype(BF16)
    for i in (*range(5, 15), 2):
        loads[i].wait()
    wsend_t = (jnp.transpose(w_send[...].astype(F32)) * 0.5).astype(BF16)
    wrecv_t = (jnp.transpose(w_recv[...].astype(F32)) * 0.5).astype(BF16)
    we_c[...] = centred_pair(w_edge[...])
    wn_c[...] = centred_pair(w_node[...])
    wsa_t[:, :W] = (jnp.transpose(w_self[...].astype(F32)) * 0.5).astype(BF16)
    wsa_t[:, W:] = (jnp.transpose(w_agg[...].astype(F32)) * 0.5).astype(BF16)
    w_edge_h = (w_edge[...].astype(F32) * 0.5).astype(BF16)
    w_node_h = (w_node[...].astype(F32) * 0.5).astype(BF16)
    tab[...] = mm(wsend_t, lat_t[...]).astype(BF16)
    lat_roll = jnp.concatenate([lat[TILE:, :], lat[:TILE, :]], axis=0)
    tab_sh[...] = nt(wsend_t, lat_roll).astype(BF16)
    recv_t[...] = mm(wrecv_t, lat_t[...]).astype(BF16).astype(F32)
    eg = column_of(egain[...])
    ng = column_of(ngain[...])

    def ghost_tables(first):
        part = slice(first, first + 2 * W)
        own = ghost[part, :]
        gtab[:, part] = nt(wsend_t, own).astype(BF16)
        gtab_sh[:, part] = nt(wsend_t, jnp.concatenate([own[TILE:, :], own[:TILE, :]], axis=0)).astype(BF16)

    def pick_tables(u, carry):
        low8 = low_half()[:8, :]
        slot_id = lax.broadcasted_iota(jnp.int32, (SLOTS, W), 0).astype(F32).astype(BF16)
        picks = nb[:, pl.ds(pl.multiple_of(u * W, W), W)]
        first, second = picks[:8, :], picks[8:, :]
        picks_of = (jnp.where(low8, first, swap(second)), jnp.where(low8, swap(first), second))
        for half in range(2):
            t = 2 * u + half
            chosen = picks_of[half]
            local = jnp.where(chosen >= ROWS, (chosen & (TILE - 1)) + 2 * TILE, (chosen - t * TILE) & (ROWS - 1))
            local = local.astype(F32)
            for q in range(STEPS):
                for c in (2 * q, 2 * q + 1):
                    oh_all[t, c] = one_hot(local[c : c + 1, :], slot_id)
        return carry

    lax.fori_loop(0, PAIRS, pick_tables, 0)

    def forward(u, carry):
        low = low_half()
        at = pl.multiple_of(u * W, W)
        at_g = pl.multiple_of(lax.rem(u, GHOSTS // W) * W, W)
        recv_of = spread_halves(recv_t[:, pl.ds(at, W)], low)
        sums_of = []
        for half in range(2):
            t = 2 * u + half
            own, far = (tab, gtab) if half == 0 else (tab_sh, gtab_sh)
            window = jnp.concatenate([own[:, pl.ds(at, W)], far[:, pl.ds(at_g, TILE)]], axis=1)
            total = None
            for q in range(STEPS):
                lanes = slice(q * CHUNK, (q + 1) * CHUNK)
                act_b, bend = narrow_half_silu(mm(window, beside([oh_all[t, 2 * q], oh_all[t, 2 * q + 1]])) + jnp.concatenate([recv_of[half]] * 2, axis=1))
                act_all[t, :, lanes] = act_b
                slope_all[t, :, lanes] = bend
                normed, inv = norm_centred(mm(we_c[...], twice(act_b)))
                norm_all[t, :, lanes] = normed.astype(BF16)
                inv_all[t, :, lanes] = inv
                part = normed[:, :W] + normed[:, W:]
                total = part if total is None else total + part
            sums_of.append(total + swap(total))
        total = jnp.where(low, sums_of[0], sums_of[1])
        sum_t[:, pl.ds(at, W)] = total
        agg_t[:, pl.ds(at, W)] = (total * eg).astype(BF16)
        return carry

    halo[2].wait()
    halo[3].wait()
    ghost_tables(2 * W)
    lax.fori_loop(0, PAIRS // 4, lambda k, c: forward(k * 4 + 3, forward(k * 4 + 2, c)), 0)
    halo[0].wait()
    halo[1].wait()
    ghost_tables(0)
    lax.fori_loop(0, PAIRS // 4, lambda k, c: forward(k * 4 + 1, forward(k * 4, c)), 0)

    def node_forward(u, carry):
        at = u * NODE
        lat_b = lat_t[:, pl.ds(at, NODE)]
        an, slope = half_silu(mm(wsa_t[...], jnp.concatenate([lat_b, agg_t[:, pl.ds(at, NODE)]], axis=0)))
        an_b = an.astype(BF16)
        an_t[:, pl.ds(at, NODE)] = an_b
        nslope_t[:, pl.ds(at, NODE)] = slope
        nn, ninv = norm_centred(mm(wn_c[...], twice(an_b)))
        nn_t[:, pl.ds(at, NODE)] = nn
        ninv_t[:, pl.ds(at, NODE)] = ninv
        fine_t[:, pl.ds(at, NODE)] = (lat_b.astype(F32) + nn * widen(ng)).astype(BF16)
        return carry

    def widen(v):
        return jnp.concatenate([v] * (NODE // W), axis=1)

    for k in range(ROWS // NODE):
        node_forward(k, 0)

    pf[gz] = nt(fine_t[...], oh_clus[...]).astype(BF16)
    pool_send(pf, pf_s, pf_r)
    ghost_t[...] = nt(eye, ghost[...]).astype(BF16)

    def prepare(u, carry):
        one = jnp.ones((), BF16)
        for half in range(2):
            t = 2 * u + half
            for q in range(STEPS):
                lanes = slice(q * CHUNK, (q + 1) * CHUNK)
                bend, act = slope_all[t, :, lanes], act_all[t, :, lanes]
                slope_all[t, :, lanes] = (one + bend) + act * (one - bend)
                for i in range(CHUNK // W):
                    act_cols[t, 2 * q + i] = act[:, i * W : (i + 1) * W]
        return carry

    lax.fori_loop(0, PAIRS, prepare, 0)
    wpin_t = jnp.transpose(w_pin[...].astype(F32)).astype(BF16)
    wpout_t = jnp.transpose(w_pout[...].astype(F32)).astype(BF16)
    pool_wait(pg, pg_r)
    gd = pg[0].astype(F32)
    for k in range(1, n_z):
        gd = gd + pg[k].astype(F32)
    gd_b = gd.astype(BF16)
    gac = mm(w_pout[...], gd_b)
    pool_wait(pf, pf_r)
    pooled = pf[0].astype(F32)
    for k in range(1, n_z):
        pooled = pooled + pf[k].astype(F32)
    pooled_b = pooled.astype(BF16)
    pc = mm(wpin_t, pooled_b)
    s = sigmoid(pc)
    ac = pc * s
    ac_b = ac.astype(BF16)
    delta_b = mm(wpout_t, ac_b).astype(BF16)
    gpc_b = (gac * (s + ac * (1.0 - s))).astype(BF16)
    gpool_b = mm(w_pin[...], gpc_b).astype(BF16)
    delta[...] = delta_b
    dw_pin = nt(pooled_b, gpc_b) * (1.0 / n_z)
    dw_pout = nt(ac_b, gd_b) * (1.0 / n_z)

    sums[...] = jnp.zeros_like(sums)

    def node_back(u, carry):
        at = u * NODE
        gf = gm_t[:, pl.ds(at, NODE)].astype(F32) + mm(gpool_b, oh_clus[:, pl.ds(at, NODE)])
        gfine_t[:, pl.ds(at, NODE)] = gf
        nn = nn_t[:, pl.ds(at, NODE)]
        sums[1] += narrow(gf * nn)
        gn = gf * widen(ng)
        gy_b = ((gn - mean0(gn) - nn * mean0(gn * nn)) * ninv_t[:, pl.ds(at, NODE)]).astype(BF16)
        gy_t[:, pl.ds(at, NODE)] = gy_b
        gpn_b = (mm(w_node_h, gy_b) * nslope_t[:, pl.ds(at, NODE)]).astype(BF16)
        gpn_t[:, pl.ds(at, NODE)] = gpn_b
        ga = mm(w_agg[...], gpn_b)
        sums[0] += narrow(ga * sum_t[:, pl.ds(at, NODE)])
        g = ga * widen(eg)
        gc_t[:, pl.ds(at, NODE)] = g - mean0(g)
        return carry

    def narrow(v):
        total = v[:, :W]
        for b in range(1, NODE // W):
            total = total + v[:, b * W : (b + 1) * W]
        return total

    for k in range(ROWS // NODE):
        node_back(k, 0)

    def put(buf, index, mat, width):
        per = W // c_rows
        buf[index * per : (index + 1) * per, :c_rows, :] = mat.reshape(per, c_rows, W).astype(BF16)

    def reduce_out(buf, into, s, r):
        into[rank_a] = buf[rank_a]

        for to, dev in plane:
            remote(buf.at[to], into.at[rank_a], s, r, dev).start()

    def reduce_mid(buf, into, mid, s, r, s2, r2):
        drain(into.at[pl.ds(0, n_a - 1)], r)
        total = into[0].astype(F32)
        for k in range(1, n_a):
            total = total + into[k].astype(F32)
        mid[rank_b] = total.astype(BF16)
        for _, dev in column:
            remote(mid.at[rank_b], mid.at[rank_b], s2, r2, dev).start()

    def gather_out(mid, out, s2, r2, s3, r3):
        drain(mid.at[pl.ds(0, n_b - 1)], r2)
        total = mid[0].astype(F32)
        for k in range(1, n_b):
            total = total + mid[k].astype(F32)
        out[rank_a] = total.astype(BF16)
        for _, dev in plane:
            remote(out.at[rank_a], out.at[rank_a], s3, r3, dev).start()

    def finish(buf, mid, out, s, s2, s3, r3):
        drain(out.at[pl.ds(0, n_a - 1)], r3)
        drain(buf.at[pl.ds(0, n_a - 1)], s)
        drain(mid.at[pl.ds(0, n_b - 1)], s2)
        drain(out.at[pl.ds(0, n_a - 1)], s3)

    def row_sums(v):
        hi = v.astype(BF16)
        lo = (v - hi.astype(F32)).astype(BF16)
        ones = jnp.ones((GAIN_ROWS, W), BF16)
        return nt(ones, hi) + nt(ones, lo)

    dw_sa = nt(jnp.concatenate([lat_t[...], agg_t[...]], axis=0), gpn_t[...])
    put(early, 0, dw_sa[:W, :], c_rows)
    put(early, 1, dw_sa[W:, :], c_rows)
    put(early, 2, nt(an_t[...], gy_t[...]), c_rows)
    put(early, 3, dw_pin, c_rows)
    which = lax.broadcasted_iota(jnp.int32, (GAIN_ROWS, W), 0)
    gain_rows = jnp.where(which == 0, row_sums(sums[0]), row_sums(sums[1])).astype(BF16)
    for k in range(n_a):
        early[k, c_rows:, :] = gain_rows
    reduce_out(early, early_in, e1s, e1r)

    gp_own[...] = jnp.zeros_like(gp_own)
    gp_ghost[...] = jnp.zeros_like(gp_ghost)
    dw_edge[...] = jnp.zeros_like(dw_edge)

    def backward(u, carry):
        low = low_half()
        at = pl.multiple_of(u * W, W)
        at_g = pl.multiple_of(lax.rem(u, GHOSTS // W) * W, W)
        gc_of = spread_halves(gc_t[:, pl.ds(at, W)], low)
        back_of = []
        for half in range(2):
            t = 2 * u + half
            gzs, gps = [], []
            gc = jnp.concatenate([gc_of[half].astype(BF16)] * 2, axis=1)
            total = None
            for q in range(STEPS):
                lanes = slice(q * CHUNK, (q + 1) * CHUNK)
                normed = norm_all[t, :, lanes]
                shared = rows_of(mean0((gc * normed).astype(F32)))
                gz_b = (gc - normed * shared) * rows_of(inv_all[t, :, lanes])
                gzs.append(gz_b)
                gpre_b = mm(w_edge_h, gz_b).astype(BF16) * slope_all[t, :, lanes]
                gps.append(gpre_b)
                gpre = gpre_b.astype(F32)
                part = gpre[:, :W] + gpre[:, W:]
                total = part if total is None else total + part
            dw_edge[...] += nt(beside([act_cols[t, c] for c in range(2 * STEPS)]), beside(gzs))
            window = nt(beside([oh_all[t, c] for c in range(2 * STEPS)]), beside(gps))
            gp_own[pl.ds(at + half * TILE, W), :] += window[:W, :]
            gp_ghost[pl.ds(at_g + half * TILE, TILE), :] += window[W:, :]
            back_of.append(total + swap(total))
        grecv_t[:, pl.ds(at, W)] = jnp.where(low, back_of[0], back_of[1]).astype(BF16)
        return carry

    back_to = (x_low, x_up, y_low, y_up)
    back = [
        remote(backbuf.at[pl.ds(q * W, W)], ret.at[pl.ds(q * W, W)], ret_s.at[q], ret_r.at[q], back_to[q])
        for q in range(4)
    ]
    lax.fori_loop(0, PAIRS // 4, lambda k, c: backward(k * 4 + 1, backward(k * 4, c)), 0)
    backbuf[: 2 * W, :] = gp_ghost[: 2 * W, :].astype(BF16)
    back[0].start()
    back[1].start()

    def backward_near(k, c):
        return backward(k * 4 + 3, backward(k * 4 + 2, c))

    lax.fori_loop(0, PAIRS // 4, backward_near, 0)
    backbuf[2 * W :, :] = gp_ghost[2 * W :, :].astype(BF16)
    back[2].start()
    back[3].start()

    gp_own[:TILE, :] += gp_own[ROWS:, :]
    own_b = gp_own[:ROWS, :].astype(BF16)
    put(late, 0, mm(lat_t[...], own_b) + mm(ghost_t[...], backbuf[...]), c_rows)
    put(late, 1, nt(lat_t[...], grecv_t[...]), c_rows)
    put(late, 2, dw_edge[...], c_rows)
    put(late, 3, dw_pout, c_rows)
    reduce_out(late, late_in, l1s, l1r)
    reduce_mid(early, early_in, early_mid, e1s, e1r, e2s, e2r)

    gfine_t[...] += (
        mm(w_self[...], gpn_t[...]) + mm(w_recv[...], grecv_t[...]) + nt(w_send[...], own_b)
    )
    for c in back:
        c.wait()
    side_a = jnp.concatenate([ret[q * TILE : (q + 1) * TILE, :] for q in (2, 3, 0, 1)], axis=0)
    side_b = jnp.concatenate([ret[q * TILE : (q + 1) * TILE, :] for q in (6, 4, 7, 5)], axis=0)
    ret_t = (nt(w_send[...], side_a) + nt(w_send[...], side_b)).astype(BF16)
    gfine_t[...] += mm(ret_t, oh_send[...])
    mixed = fine_t[...].astype(F32) + mm(delta[...], oh_clus[...])
    for b in range(PAIRS):
        mixed_o[b * W : (b + 1) * W, :] = jnp.transpose(mixed[:, b * W : (b + 1) * W]).astype(BF16)
    reduce_mid(late, late_in, late_mid, l1s, l1r, l2s, l2r)
    gather_out(early_mid, early_out, e2s, e2r, e3s, e3r)
    for b in range(PAIRS):
        grad_o[b * W : (b + 1) * W, :] = jnp.transpose(gfine_t[:, b * W : (b + 1) * W])

    def emit(out, index, place):
        per = W // c_rows
        mat = out[index * per : (index + 1) * per, :c_rows, :].astype(F32).reshape(W, W)
        mats_o[place] = mat * lax.rsqrt(jnp.mean(mat * mat, keepdims=True) + 1e-06)

    finish(early, early_mid, early_out, e1s, e2s, e3s, e3r)
    for index, place in enumerate((3, 4, 5, 6)):
        emit(early_out, index, place)
    scale = float(ROWS * n_x * n_y * n_z) ** (-0.5)
    gains_o[...] = early_out[0, c_rows : c_rows + 2, :].astype(F32) * scale
    pool_wait(pg, pg_s)
    pool_wait(pf, pf_s)
    gather_out(late_mid, late_out, l2s, l2r, l3s, l3r)
    finish(late, late_mid, late_out, l1s, l2s, l3s, l3r)
    for index, place in enumerate((0, 1, 2, 7)):
        emit(late_out, index, place)


def pass_on(*refs):
    sems = refs[-1]
    copies = [pltpu.make_async_copy(a, b, sems.at[i]) for i, (a, b) in enumerate(zip(refs[:4], refs[4:8]))]
    for c in copies:
        c.start()
    for c in copies:
        c.wait()


def solution(mesh):
    sizes = tuple(mesh.shape[name] for name in ("gx", "gy", "gz"))
    n_a, n_b, n_z = sizes[0] * sizes[2], sizes[1], sizes[2]
    c_rows = 4 * W // n_a
    tiles = ROWS // TILE
    edges = TILE * NEIGH
    v = pltpu.VMEM
    dma = pltpu.SemaphoreType.DMA

    def reduce_bufs(rows):
        return [v((n_a, rows, W), BF16), v((n_a, rows, W), BF16), v((n_b, rows, W), BF16), v((n_a, rows, W), BF16)]

    scratch = [
        v((GHOSTS, W), BF16),
        v((GHOSTS, W), BF16),
        v((GHOSTS, W), BF16),
        v((GHOSTS, W), BF16),
        v((n_z, W, CLUSTERS), BF16),
        v((n_z, W, CLUSTERS), BF16),
        *reduce_bufs(c_rows + GAIN_ROWS),
        *reduce_bufs(c_rows),
        v((W, ROWS), BF16),
        v((W, ROWS), BF16),
        v((4 * TILE, ROWS), BF16),
        v((CLUSTERS, ROWS), BF16),
        v((W, ROWS), BF16),
        v((W, ROWS), BF16),
        v((W, GHOSTS), BF16),
        v((W, GHOSTS), BF16),
        v((W, ROWS), F32),
        v((W, 2 * W), BF16),
        v((W, 2 * W), BF16),
        v((W, 2 * W), BF16),
        v((W, CLUSTERS), BF16),
        v((W, GHOSTS), BF16),
        v((tiles, edges // W, SLOTS, W), BF16),
        v((tiles, edges // W, W, W), BF16),
        v((tiles, W, edges), BF16),
        v((tiles, W, edges), BF16),
        v((tiles, W, edges), BF16),
        v((tiles, 1, edges), F32),
        v((W, ROWS), F32),
        v((W, ROWS), BF16),
        v((W, ROWS), BF16),
        v((W, ROWS), F32),
        v((W, ROWS), F32),
        v((1, ROWS), F32),
        v((W, ROWS), BF16),
        v((W, ROWS), F32),
        v((W, ROWS), BF16),
        v((W, ROWS), BF16),
        v((W, ROWS), F32),
        v((W, ROWS), BF16),
        v((ROWS + TILE, W), F32),
        v((GHOSTS, W), F32),
        v((W, W), F32),
        v((2, W, W), F32),
        dma((4,)), dma((4,)), dma((4,)), dma((4,)),
        *[dma for _ in range(16)],
        v((ROWS, W), BF16), v((ROWS, W), BF16), v((NEIGH, ROWS), jnp.int32), v((4, TILE), jnp.int32),
        v((1, ROWS), jnp.int32), *[v((W, W), BF16) for _ in range(8)], v((1, W), F32), v((1, W), F32),
        dma((15,)),
    ]

    def step(latents, grad_mixed, neighbours, send_list, cluster, w_send, w_recv, w_edge, edge_gain, w_self, w_agg,
             w_node, node_gain, w_pool_in, w_pool_out):
        results = pl.pallas_call(
            functools.partial(kernel, sizes),
            out_shape=(
                jax.ShapeDtypeStruct((ROWS, W), BF16),
                jax.ShapeDtypeStruct((ROWS, W), F32),
                jax.ShapeDtypeStruct((8, W, W), F32),
                jax.ShapeDtypeStruct((2, W), F32),
            ),
            in_specs=[pl.BlockSpec(memory_space=pltpu.HBM)] * 15,
            out_specs=tuple([pl.BlockSpec(memory_space=pltpu.VMEM)] * 4),
            scratch_shapes=scratch,
            compiler_params=pltpu.CompilerParams(
                collective_id=0, has_side_effects=True, vmem_limit_bytes=44 * 1024 * 1024
            ),
        )(*[pltpu.with_memory_space_constraint(x, pltpu.HBM) for x in (
            latents, grad_mixed, neighbours.T, send_list, cluster.reshape(1, ROWS), w_send, w_recv, w_edge, w_self,
            w_agg, w_node, w_pool_in, w_pool_out, edge_gain.reshape(1, W), node_gain.reshape(1, W))])
        return pl.pallas_call(
            pass_on,
            out_shape=tuple(jax.ShapeDtypeStruct(r.shape, r.dtype) for r in results),
            in_specs=[pl.BlockSpec(memory_space=pltpu.VMEM)] * 4,
            out_specs=tuple([pl.BlockSpec(memory_space=pltpu.HBM)] * 4),
            scratch_shapes=[pltpu.SemaphoreType.DMA((4,))],
            compiler_params=pltpu.CompilerParams(vmem_limit_bytes=8 * 1024 * 1024),
        )(*results)

    rows = P(("gx", "gy", "gz"), None)
    in_specs = (rows, rows, rows, rows, P(("gx", "gy", "gz"))) + (P(),) * 10
    out_specs = (rows, rows, P(), P())
    return jax.shard_map(step, mesh=mesh, in_specs=in_specs, out_specs=out_specs, check_vma=False)
```

```python
import functools

import jax
import jax.numpy as jnp
from jax import lax
from jax.experimental import pallas as pl
from jax.experimental.pallas import tpu as pltpu
from jax.sharding import PartitionSpec as P

EPS = 1e-05
W = 128
ROWS = 1024
NEIGH = 16
TILE = 64
PAIRS = ROWS // W
GHOSTS = 512
CLUSTERS = 256
SLOTS = 192
CHUNK = 256
STEPS = TILE * NEIGH // CHUNK
NODE = 256
GAIN_ROWS = 16
F32 = jnp.float32
BF16 = jnp.bfloat16
MESH = pl.DeviceIdType.MESH


def mm(a, b):
    return lax.dot_general(a, b, (((1,), (0,)), ((), ())), preferred_element_type=F32)


def nt(a, b):
    return lax.dot_general(a, b, (((1,), (1,)), ((), ())), preferred_element_type=F32)


def sigmoid(v):
    return 0.5 * jnp.tanh(0.5 * v) + 0.5


def mean0(v):
    return jnp.sum(v, axis=0, keepdims=True) * (1.0 / W)


def norm_centred(centred):
    inv = lax.rsqrt(mean0(centred * centred) + EPS)
    return centred * inv, inv


def half_silu(h):
    t = jnp.tanh(h)
    up = 1.0 + t
    act = h * up
    return act, up + act * (1.0 - t)


def narrow_half_silu(h):
    h = h.astype(BF16)
    t = jnp.tanh(h)
    one = jnp.ones((), BF16)
    return h * (one + t), t


def rows_of(row):
    return jnp.concatenate([jnp.broadcast_to(row, (16, row.shape[1])).astype(BF16)] * (W // 16), axis=0)


def centred_pair(w):
    w_t = jnp.transpose(w.astype(F32))
    centred = w_t - mean0(w_t)
    high = centred.astype(BF16)
    return jnp.concatenate([high, (centred - high.astype(F32)).astype(BF16)], axis=1)


def beside(parts):
    return jnp.concatenate(parts, axis=1)


def beside(parts):
    return jnp.concatenate(parts, axis=1)


def twice(v):
    return jnp.concatenate([v, v], axis=0)


def one_hot(row, ids):
    wide = jnp.broadcast_to(row, (16, W)).astype(BF16)
    same = jnp.concatenate([wide] * (ids.shape[0] // 16), axis=0) == ids
    return jnp.where(same, jnp.ones((), BF16), jnp.zeros((), BF16))


def low_half():
    return lax.broadcasted_iota(jnp.int32, (W, W), 1) < TILE


def swap(v):
    return pltpu.roll(v, TILE, 1)


def spread_halves(block, low):
    other = swap(block)
    return jnp.where(low, block, other), jnp.where(low, other, block)


def column_of(row):
    return jnp.transpose(jnp.broadcast_to(row, (W, W)))


def kernel(sizes, *refs):
    far, near, in_sems = refs[:15], refs[-16:-1], refs[-1]
    (lat, gm, nb, send, clus, w_send, w_recv, w_edge, w_self, w_agg, w_node, w_pin, w_pout, egain, ngain) = near
    mixed_o, grad_o, mats_o, gains_o = refs[15:19]
    (sbuf, ghost, ret, backbuf, pg, pf, early, early_in, early_mid, early_out, late, late_in, late_mid, late_out,
     lat_t, gm_t, oh_send, oh_clus, tab, tab_sh, gtab, gtab_sh, recv_t, wsa_t, we_c, wn_c, delta, ghost_t,
     oh_all, act_cols, act_all, slope_all, norm_all, inv_all, sum_t, agg_t, an_t, nslope_t, nn_t, ninv_t, fine_t, gfine_t,
     gy_t, gpn_t, gc_t, grecv_t, gp_own, gp_ghost, dw_edge, sums) = refs[19:69]
    (halo_s, halo_r, ret_s, ret_r, pg_s, pg_r, pf_s, pf_r,
     e1s, e1r, e2s, e2r, e3s, e3r, l1s, l1r, l2s, l2r, l3s, l3r) = refs[69:-16]
    loads = [pltpu.make_async_copy(a, b, in_sems.at[i]) for i, (a, b) in enumerate(zip(far, near))]
    for i in (3, 0, 1, 4, *range(5, 15), 2):
        loads[i].start()

    n_x, n_y, n_z = sizes
    n_a, n_b = n_x * n_z, n_y
    c_rows = 4 * W // n_a
    gx, gy, gz = lax.axis_index("gx"), lax.axis_index("gy"), lax.axis_index("gz")
    x_up = (lax.rem(gx + 1, n_x), gy, gz)
    x_low = (lax.rem(gx + n_x - 1, n_x), gy, gz)
    y_up = (gx, lax.rem(gy + 1, n_y), gz)
    y_low = (gx, lax.rem(gy + n_y - 1, n_y), gz)
    y_now, z_high = lax.div(gx, 2), lax.rem(gx, 2)
    z_low, core = lax.div(gy, 2), lax.rem(gy, 2)
    n_yc, n_zl = n_x // 2, n_y // 2
    z_now = z_high * n_zl + z_low
    rank_a, rank_b = (y_now * 2 + core) * n_z + gz, z_now

    def hops(step, n):
        return min(step, n - step)

    ys = [lax.rem(y_now + d, n_yc) for d in range(n_yc)]
    cs = [core, 1 - core]
    xs = [lax.rem(gz + d, n_z) for d in range(n_z)]
    order = sorted(
        [(d, e, f) for d in range(n_yc) for e in range(2) for f in range(n_z)][1:],
        key=lambda o: (-hops(o[0], n_yc) - hops(o[2], n_z), o),
    )
    plane = [
        ((ys[d] * 2 + cs[e]) * n_z + xs[f], (ys[d] * 2 + z_high, z_low * 2 + cs[e], xs[f])) for d, e, f in order
    ]
    zs = [lax.rem(z_now + d, n_b) for d in sorted(range(1, n_b), key=lambda d: (-hops(d, n_b), d))]
    column = [(z, (y_now * 2 + lax.div(z, n_zl), lax.rem(z, n_zl) * 2 + core, gz)) for z in zs]
    row = [(xs[d], (gx, gy, xs[d])) for d in sorted(range(1, n_z), key=lambda d: (-hops(d, n_z), d))]

    def remote(src, dst, s, r, dev):
        return pltpu.make_async_remote_copy(
            src_ref=src, dst_ref=dst, send_sem=s, recv_sem=r, device_id=dev, device_id_type=MESH
        )

    def drain(ref, sem):
        pltpu.make_async_copy(ref, ref, sem).wait()

    barrier = pltpu.get_barrier_semaphore()
    for dev in (x_up, x_low, y_up, y_low, *[d for _, d in plane], *[d for _, d in column]):
        pl.semaphore_signal(barrier, inc=1, device_id=dev, device_id_type=MESH)

    lane_row = lax.broadcasted_iota(jnp.int32, (TILE, W), 1)
    loads[3].wait()
    send_f = send[...].astype(F32)
    for q in range(4):
        col = jnp.transpose(jnp.broadcast_to(send_f[q : q + 1, :], (W, TILE))).astype(jnp.int32)
        for b in range(PAIRS):
            hot = jnp.where(col == lane_row + b * W, 1.0, 0.0).astype(BF16)
            oh_send[q * TILE : (q + 1) * TILE, b * W : (b + 1) * W] = hot
    loads[0].wait()
    cells = mm(oh_send[...], lat[...]).astype(BF16)
    for slot, q in enumerate((2, 3, 0, 1, 1, 3, 0, 2)):
        sbuf[slot * TILE : (slot + 1) * TILE, :] = cells[q * TILE : (q + 1) * TILE, :]
    pl.semaphore_wait(barrier, 4 + n_a - 1 + n_b - 1)
    halo_to = (x_up, x_low, y_up, y_low)
    halo = [
        remote(sbuf.at[pl.ds(q * W, W)], ghost.at[pl.ds(q * W, W)], halo_s.at[q], halo_r.at[q], halo_to[q])
        for q in range(4)
    ]
    for q in (2, 3, 0, 1):
        halo[q].start()

    eye = jnp.where(
        lax.broadcasted_iota(jnp.int32, (W, W), 0) == lax.broadcasted_iota(jnp.int32, (W, W), 1), 1.0, 0.0
    ).astype(BF16)
    loads[1].wait()
    loads[4].wait()
    gm_t[...] = nt(eye, gm[...]).astype(BF16)
    cl_id = lax.broadcasted_iota(jnp.int32, (CLUSTERS, W), 0).astype(F32).astype(BF16)
    clus_f = clus[...].astype(F32)
    for b in range(PAIRS):
        oh_clus[:, b * W : (b + 1) * W] = one_hot(clus_f[:, b * W : (b + 1) * W], cl_id)

    def pool_send(buf, s, r):
        for _, dev in row:
            remote(buf.at[gz], buf.at[gz], s, r, dev).start()

    def pool_wait(buf, r):
        drain(buf.at[pl.ds(0, n_z - 1)], r)

    pg[gz] = nt(gm_t[...], oh_clus[...]).astype(BF16)
    pool_send(pg, pg_s, pg_r)

    lat_t[...] = nt(eye, lat[...]).astype(BF16)
    for i in (*range(5, 15), 2):
        loads[i].wait()
    wsend_t = (jnp.transpose(w_send[...].astype(F32)) * 0.5).astype(BF16)
    wrecv_t = (jnp.transpose(w_recv[...].astype(F32)) * 0.5).astype(BF16)
    we_c[...] = centred_pair(w_edge[...])
    wn_c[...] = centred_pair(w_node[...])
    wsa_t[:, :W] = (jnp.transpose(w_self[...].astype(F32)) * 0.5).astype(BF16)
    wsa_t[:, W:] = (jnp.transpose(w_agg[...].astype(F32)) * 0.5).astype(BF16)
    w_edge_h = (w_edge[...].astype(F32) * 0.5).astype(BF16)
    w_node_h = (w_node[...].astype(F32) * 0.5).astype(BF16)
    tab[...] = mm(wsend_t, lat_t[...]).astype(BF16)
    lat_roll = jnp.concatenate([lat[TILE:, :], lat[:TILE, :]], axis=0)
    tab_sh[...] = nt(wsend_t, lat_roll).astype(BF16)
    recv_t[...] = mm(wrecv_t, lat_t[...]).astype(BF16).astype(F32)
    eg = column_of(egain[...])
    ng = column_of(ngain[...])

    def ghost_tables(first):
        part = slice(first, first + 2 * W)
        own = ghost[part, :]
        gtab[:, part] = nt(wsend_t, own).astype(BF16)
        gtab_sh[:, part] = nt(wsend_t, jnp.concatenate([own[TILE:, :], own[:TILE, :]], axis=0)).astype(BF16)

    def pick_tables(u, carry):
        low8 = low_half()[:8, :]
        slot_id = lax.broadcasted_iota(jnp.int32, (SLOTS, W), 0).astype(F32).astype(BF16)
        picks = nb[:, pl.ds(pl.multiple_of(u * W, W), W)]
        first, second = picks[:8, :], picks[8:, :]
        picks_of = (jnp.where(low8, first, swap(second)), jnp.where(low8, swap(first), second))
        for half in range(2):
            t = 2 * u + half
            chosen = picks_of[half]
            local = jnp.where(chosen >= ROWS, (chosen & (TILE - 1)) + 2 * TILE, (chosen - t * TILE) & (ROWS - 1))
            local = local.astype(F32)
            for q in range(STEPS):
                for c in (2 * q, 2 * q + 1):
                    oh_all[t, c] = one_hot(local[c : c + 1, :], slot_id)
        return carry

    lax.fori_loop(0, PAIRS, pick_tables, 0)

    def forward(u, carry):
        low = low_half()
        at = u * W if isinstance(u, int) else pl.multiple_of(u * W, W)
        at_g = u % (GHOSTS // W) * W if isinstance(u, int) else pl.multiple_of(lax.rem(u, GHOSTS // W) * W, W)
        recv_of = spread_halves(recv_t[:, pl.ds(at, W)], low)
        sums_of = []
        for half in range(2):
            t = 2 * u + half
            own, far = (tab, gtab) if half == 0 else (tab_sh, gtab_sh)
            window = jnp.concatenate([own[:, pl.ds(at, W)], far[:, pl.ds(at_g, TILE)]], axis=1)
            total = None
            for q in range(STEPS):
                lanes = slice(q * CHUNK, (q + 1) * CHUNK)
                act_b, bend = narrow_half_silu(mm(window, beside([oh_all[t, 2 * q], oh_all[t, 2 * q + 1]])) + jnp.concatenate([recv_of[half]] * 2, axis=1))
                act_all[t, :, lanes] = act_b
                slope_all[t, :, lanes] = bend
                normed, inv = norm_centred(mm(we_c[...], twice(act_b)))
                norm_all[t, :, lanes] = normed.astype(BF16)
                inv_all[t, :, lanes] = inv
                part = normed[:, :W] + normed[:, W:]
                total = part if total is None else total + part
            sums_of.append(total + swap(total))
        total = jnp.where(low, sums_of[0], sums_of[1])
        sum_t[:, pl.ds(at, W)] = total
        agg_t[:, pl.ds(at, W)] = (total * eg).astype(BF16)
        return carry

    halo[2].wait()
    halo[3].wait()
    ghost_tables(2 * W)
    for u in (2, 3, 6, 7):
        forward(u, 0)
    halo[0].wait()
    halo[1].wait()
    ghost_tables(0)
    for u in (0, 1, 4, 5):
        forward(u, 0)

    def node_forward(u, carry):
        at = u * NODE
        lat_b = lat_t[:, pl.ds(at, NODE)]
        an, slope = half_silu(mm(wsa_t[...], jnp.concatenate([lat_b, agg_t[:, pl.ds(at, NODE)]], axis=0)))
        an_b = an.astype(BF16)
        an_t[:, pl.ds(at, NODE)] = an_b
        nslope_t[:, pl.ds(at, NODE)] = slope
        nn, ninv = norm_centred(mm(wn_c[...], twice(an_b)))
        nn_t[:, pl.ds(at, NODE)] = nn
        ninv_t[:, pl.ds(at, NODE)] = ninv
        fine_t[:, pl.ds(at, NODE)] = (lat_b.astype(F32) + nn * widen(ng)).astype(BF16)
        return carry

    def widen(v):
        return jnp.concatenate([v] * (NODE // W), axis=1)

    for k in range(ROWS // NODE):
        node_forward(k, 0)

    pf[gz] = nt(fine_t[...], oh_clus[...]).astype(BF16)
    pool_send(pf, pf_s, pf_r)
    ghost_t[...] = nt(eye, ghost[...]).astype(BF16)

    def prepare(u, carry):
        one = jnp.ones((), BF16)
        for half in range(2):
            t = 2 * u + half
            for q in range(STEPS):
                lanes = slice(q * CHUNK, (q + 1) * CHUNK)
                bend, act = slope_all[t, :, lanes], act_all[t, :, lanes]
                slope_all[t, :, lanes] = (one + bend) + act * (one - bend)
                for i in range(CHUNK // W):
                    act_cols[t, 2 * q + i] = act[:, i * W : (i + 1) * W]
        return carry

    lax.fori_loop(0, PAIRS, prepare, 0)
    wpin_t = jnp.transpose(w_pin[...].astype(F32)).astype(BF16)
    wpout_t = jnp.transpose(w_pout[...].astype(F32)).astype(BF16)
    pool_wait(pg, pg_r)
    gd = pg[0].astype(F32)
    for k in range(1, n_z):
        gd = gd + pg[k].astype(F32)
    gd_b = gd.astype(BF16)
    gac = mm(w_pout[...], gd_b)
    pool_wait(pf, pf_r)
    pooled = pf[0].astype(F32)
    for k in range(1, n_z):
        pooled = pooled + pf[k].astype(F32)
    pooled_b = pooled.astype(BF16)
    pc = mm(wpin_t, pooled_b)
    s = sigmoid(pc)
    ac = pc * s
    ac_b = ac.astype(BF16)
    delta_b = mm(wpout_t, ac_b).astype(BF16)
    gpc_b = (gac * (s + ac * (1.0 - s))).astype(BF16)
    gpool_b = mm(w_pin[...], gpc_b).astype(BF16)
    delta[...] = delta_b
    dw_pin = nt(pooled_b, gpc_b) * (1.0 / n_z)
    dw_pout = nt(ac_b, gd_b) * (1.0 / n_z)

    sums[...] = jnp.zeros_like(sums)

    def node_back(u, carry):
        at = u * NODE
        gf = gm_t[:, pl.ds(at, NODE)].astype(F32) + mm(gpool_b, oh_clus[:, pl.ds(at, NODE)])
        gfine_t[:, pl.ds(at, NODE)] = gf
        nn = nn_t[:, pl.ds(at, NODE)]
        sums[1] += narrow(gf * nn)
        gn = gf * widen(ng)
        gy_b = ((gn - mean0(gn) - nn * mean0(gn * nn)) * ninv_t[:, pl.ds(at, NODE)]).astype(BF16)
        gy_t[:, pl.ds(at, NODE)] = gy_b
        gpn_b = (mm(w_node_h, gy_b) * nslope_t[:, pl.ds(at, NODE)]).astype(BF16)
        gpn_t[:, pl.ds(at, NODE)] = gpn_b
        ga = mm(w_agg[...], gpn_b)
        sums[0] += narrow(ga * sum_t[:, pl.ds(at, NODE)])
        g = ga * widen(eg)
        gc_t[:, pl.ds(at, NODE)] = g - mean0(g)
        return carry

    def narrow(v):
        total = v[:, :W]
        for b in range(1, NODE // W):
            total = total + v[:, b * W : (b + 1) * W]
        return total

    for k in range(ROWS // NODE):
        node_back(k, 0)

    def put(buf, index, mat, width):
        per = W // c_rows
        buf[index * per : (index + 1) * per, :c_rows, :] = mat.reshape(per, c_rows, W).astype(BF16)

    def reduce_out(buf, into, s, r):
        into[rank_a] = buf[rank_a]

        for to, dev in plane:
            remote(buf.at[to], into.at[rank_a], s, r, dev).start()

    def reduce_mid(buf, into, mid, s, r, s2, r2):
        drain(into.at[pl.ds(0, n_a - 1)], r)
        total = into[0].astype(F32)
        for k in range(1, n_a):
            total = total + into[k].astype(F32)
        mid[rank_b] = total.astype(BF16)
        for _, dev in column:
            remote(mid.at[rank_b], mid.at[rank_b], s2, r2, dev).start()

    def gather_out(mid, out, s2, r2, s3, r3):
        drain(mid.at[pl.ds(0, n_b - 1)], r2)
        total = mid[0].astype(F32)
        for k in range(1, n_b):
            total = total + mid[k].astype(F32)
        out[rank_a] = total.astype(BF16)
        for _, dev in plane:
            remote(out.at[rank_a], out.at[rank_a], s3, r3, dev).start()

    def finish(buf, mid, out, s, s2, s3, r3):
        drain(out.at[pl.ds(0, n_a - 1)], r3)
        drain(buf.at[pl.ds(0, n_a - 1)], s)
        drain(mid.at[pl.ds(0, n_b - 1)], s2)
        drain(out.at[pl.ds(0, n_a - 1)], s3)

    def row_sums(v):
        hi = v.astype(BF16)
        lo = (v - hi.astype(F32)).astype(BF16)
        ones = jnp.ones((GAIN_ROWS, W), BF16)
        return nt(ones, hi) + nt(ones, lo)

    dw_sa = nt(jnp.concatenate([lat_t[...], agg_t[...]], axis=0), gpn_t[...])
    put(early, 0, dw_sa[:W, :], c_rows)
    put(early, 1, dw_sa[W:, :], c_rows)
    put(early, 2, nt(an_t[...], gy_t[...]), c_rows)
    put(early, 3, dw_pin, c_rows)
    which = lax.broadcasted_iota(jnp.int32, (GAIN_ROWS, W), 0)
    gain_rows = jnp.where(which == 0, row_sums(sums[0]), row_sums(sums[1])).astype(BF16)
    for k in range(n_a):
        early[k, c_rows:, :] = gain_rows
    reduce_out(early, early_in, e1s, e1r)

    gp_own[...] = jnp.zeros_like(gp_own)
    gp_ghost[...] = jnp.zeros_like(gp_ghost)
    dw_edge[...] = jnp.zeros_like(dw_edge)

    def backward(u, carry):
        low = low_half()
        at = u * W if isinstance(u, int) else pl.multiple_of(u * W, W)
        at_g = u % (GHOSTS // W) * W if isinstance(u, int) else pl.multiple_of(lax.rem(u, GHOSTS // W) * W, W)
        gc_of = spread_halves(gc_t[:, pl.ds(at, W)], low)
        back_of = []
        for half in range(2):
            t = 2 * u + half
            gzs, gps = [], []
            gc = jnp.concatenate([gc_of[half].astype(BF16)] * 2, axis=1)
            total = None
            for q in range(STEPS):
                lanes = slice(q * CHUNK, (q + 1) * CHUNK)
                normed = norm_all[t, :, lanes]
                shared = rows_of(mean0((gc * normed).astype(F32)))
                gz_b = (gc - normed * shared) * rows_of(inv_all[t, :, lanes])
                gzs.append(gz_b)
                gpre_b = mm(w_edge_h, gz_b).astype(BF16) * slope_all[t, :, lanes]
                gps.append(gpre_b)
                gpre = gpre_b.astype(F32)
                part = gpre[:, :W] + gpre[:, W:]
                total = part if total is None else total + part
            dw_edge[...] += nt(beside([act_cols[t, c] for c in range(2 * STEPS)]), beside(gzs))
            window = nt(beside([oh_all[t, c] for c in range(2 * STEPS)]), beside(gps))
            gp_own[pl.ds(at + half * TILE, W), :] += window[:W, :]
            gp_ghost[pl.ds(at_g + half * TILE, TILE), :] += window[W:, :]
            back_of.append(total + swap(total))
        grecv_t[:, pl.ds(at, W)] = jnp.where(low, back_of[0], back_of[1]).astype(BF16)
        return carry

    back_to = (x_low, x_up, y_low, y_up)
    back = [
        remote(backbuf.at[pl.ds(q * W, W)], ret.at[pl.ds(q * W, W)], ret_s.at[q], ret_r.at[q], back_to[q])
        for q in range(4)
    ]
    for u in (0, 1, 4, 5):
        backward(u, 0)
    backbuf[: 2 * W, :] = gp_ghost[: 2 * W, :].astype(BF16)
    back[0].start()
    back[1].start()

    def backward_near(k, c):
        return backward(k * 4 + 3, backward(k * 4 + 2, c))

    for u in (2, 3, 6, 7):
        backward(u, 0)
    backbuf[2 * W :, :] = gp_ghost[2 * W :, :].astype(BF16)
    back[2].start()
    back[3].start()

    gp_own[:TILE, :] += gp_own[ROWS:, :]
    own_b = gp_own[:ROWS, :].astype(BF16)
    put(late, 0, mm(lat_t[...], own_b) + mm(ghost_t[...], backbuf[...]), c_rows)
    put(late, 1, nt(lat_t[...], grecv_t[...]), c_rows)
    put(late, 2, dw_edge[...], c_rows)
    put(late, 3, dw_pout, c_rows)
    reduce_out(late, late_in, l1s, l1r)
    reduce_mid(early, early_in, early_mid, e1s, e1r, e2s, e2r)

    gfine_t[...] += (
        mm(w_self[...], gpn_t[...]) + mm(w_recv[...], grecv_t[...]) + nt(w_send[...], own_b)
    )
    for c in back:
        c.wait()
    side_a = jnp.concatenate([ret[q * TILE : (q + 1) * TILE, :] for q in (2, 3, 0, 1)], axis=0)
    side_b = jnp.concatenate([ret[q * TILE : (q + 1) * TILE, :] for q in (6, 4, 7, 5)], axis=0)
    ret_t = (nt(w_send[...], side_a) + nt(w_send[...], side_b)).astype(BF16)
    gfine_t[...] += mm(ret_t, oh_send[...])
    mixed = fine_t[...].astype(F32) + mm(delta[...], oh_clus[...])
    for b in range(PAIRS):
        mixed_o[b * W : (b + 1) * W, :] = jnp.transpose(mixed[:, b * W : (b + 1) * W]).astype(BF16)
    reduce_mid(late, late_in, late_mid, l1s, l1r, l2s, l2r)
    gather_out(early_mid, early_out, e2s, e2r, e3s, e3r)
    for b in range(PAIRS):
        grad_o[b * W : (b + 1) * W, :] = jnp.transpose(gfine_t[:, b * W : (b + 1) * W])

    def emit(out, index, place):
        per = W // c_rows
        mat = out[index * per : (index + 1) * per, :c_rows, :].astype(F32).reshape(W, W)
        mats_o[place] = mat * lax.rsqrt(jnp.mean(mat * mat, keepdims=True) + 1e-06)

    finish(early, early_mid, early_out, e1s, e2s, e3s, e3r)
    for index, place in enumerate((3, 4, 5, 6)):
        emit(early_out, index, place)
    scale = float(ROWS * n_x * n_y * n_z) ** (-0.5)
    gains_o[...] = early_out[0, c_rows : c_rows + 2, :].astype(F32) * scale
    pool_wait(pg, pg_s)
    pool_wait(pf, pf_s)
    gather_out(late_mid, late_out, l2s, l2r, l3s, l3r)
    finish(late, late_mid, late_out, l1s, l2s, l3s, l3r)
    for index, place in enumerate((0, 1, 2, 7)):
        emit(late_out, index, place)


def pass_on(*refs):
    sems = refs[-1]
    copies = [pltpu.make_async_copy(a, b, sems.at[i]) for i, (a, b) in enumerate(zip(refs[:4], refs[4:8]))]
    for c in copies:
        c.start()
    for c in copies:
        c.wait()


def solution(mesh):
    sizes = tuple(mesh.shape[name] for name in ("gx", "gy", "gz"))
    n_a, n_b, n_z = sizes[0] * sizes[2], sizes[1], sizes[2]
    c_rows = 4 * W // n_a
    tiles = ROWS // TILE
    edges = TILE * NEIGH
    v = pltpu.VMEM
    dma = pltpu.SemaphoreType.DMA

    def reduce_bufs(rows):
        return [v((n_a, rows, W), BF16), v((n_a, rows, W), BF16), v((n_b, rows, W), BF16), v((n_a, rows, W), BF16)]

    scratch = [
        v((GHOSTS, W), BF16),
        v((GHOSTS, W), BF16),
        v((GHOSTS, W), BF16),
        v((GHOSTS, W), BF16),
        v((n_z, W, CLUSTERS), BF16),
        v((n_z, W, CLUSTERS), BF16),
        *reduce_bufs(c_rows + GAIN_ROWS),
        *reduce_bufs(c_rows),
        v((W, ROWS), BF16),
        v((W, ROWS), BF16),
        v((4 * TILE, ROWS), BF16),
        v((CLUSTERS, ROWS), BF16),
        v((W, ROWS), BF16),
        v((W, ROWS), BF16),
        v((W, GHOSTS), BF16),
        v((W, GHOSTS), BF16),
        v((W, ROWS), F32),
        v((W, 2 * W), BF16),
        v((W, 2 * W), BF16),
        v((W, 2 * W), BF16),
        v((W, CLUSTERS), BF16),
        v((W, GHOSTS), BF16),
        v((tiles, edges // W, SLOTS, W), BF16),
        v((tiles, edges // W, W, W), BF16),
        v((tiles, W, edges), BF16),
        v((tiles, W, edges), BF16),
        v((tiles, W, edges), BF16),
        v((tiles, 1, edges), F32),
        v((W, ROWS), F32),
        v((W, ROWS), BF16),
        v((W, ROWS), BF16),
        v((W, ROWS), F32),
        v((W, ROWS), F32),
        v((1, ROWS), F32),
        v((W, ROWS), BF16),
        v((W, ROWS), F32),
        v((W, ROWS), BF16),
        v((W, ROWS), BF16),
        v((W, ROWS), F32),
        v((W, ROWS), BF16),
        v((ROWS + TILE, W), F32),
        v((GHOSTS, W), F32),
        v((W, W), F32),
        v((2, W, W), F32),
        dma((4,)), dma((4,)), dma((4,)), dma((4,)),
        *[dma for _ in range(16)],
        v((ROWS, W), BF16), v((ROWS, W), BF16), v((NEIGH, ROWS), jnp.int32), v((4, TILE), jnp.int32),
        v((1, ROWS), jnp.int32), *[v((W, W), BF16) for _ in range(8)], v((1, W), F32), v((1, W), F32),
        dma((15,)),
    ]

    def step(latents, grad_mixed, neighbours, send_list, cluster, w_send, w_recv, w_edge, edge_gain, w_self, w_agg,
             w_node, node_gain, w_pool_in, w_pool_out):
        results = pl.pallas_call(
            functools.partial(kernel, sizes),
            out_shape=(
                jax.ShapeDtypeStruct((ROWS, W), BF16),
                jax.ShapeDtypeStruct((ROWS, W), F32),
                jax.ShapeDtypeStruct((8, W, W), F32),
                jax.ShapeDtypeStruct((2, W), F32),
            ),
            in_specs=[pl.BlockSpec(memory_space=pltpu.HBM)] * 15,
            out_specs=tuple([pl.BlockSpec(memory_space=pltpu.VMEM)] * 4),
            scratch_shapes=scratch,
            compiler_params=pltpu.CompilerParams(
                collective_id=0, has_side_effects=True, vmem_limit_bytes=44 * 1024 * 1024
            ),
        )(*[pltpu.with_memory_space_constraint(x, pltpu.HBM) for x in (
            latents, grad_mixed, neighbours.T, send_list, cluster.reshape(1, ROWS), w_send, w_recv, w_edge, w_self,
            w_agg, w_node, w_pool_in, w_pool_out, edge_gain.reshape(1, W), node_gain.reshape(1, W))])
        return pl.pallas_call(
            pass_on,
            out_shape=tuple(jax.ShapeDtypeStruct(r.shape, r.dtype) for r in results),
            in_specs=[pl.BlockSpec(memory_space=pltpu.VMEM)] * 4,
            out_specs=tuple([pl.BlockSpec(memory_space=pltpu.HBM)] * 4),
            scratch_shapes=[pltpu.SemaphoreType.DMA((4,))],
            compiler_params=pltpu.CompilerParams(vmem_limit_bytes=8 * 1024 * 1024),
        )(*results)

    rows = P(("gx", "gy", "gz"), None)
    in_specs = (rows, rows, rows, rows, P(("gx", "gy", "gz"))) + (P(),) * 10
    out_specs = (rows, rows, P(), P())
    return jax.shard_map(step, mesh=mesh, in_specs=in_specs, out_specs=out_specs, check_vma=False)
```

```python
import functools

import jax
import jax.numpy as jnp
from jax import lax
from jax.experimental import pallas as pl
from jax.experimental.pallas import tpu as pltpu
from jax.sharding import PartitionSpec as P

EPS = 1e-05
W = 128
ROWS = 1024
NEIGH = 16
TILE = 64
PAIRS = ROWS // W
GHOSTS = 512
CLUSTERS = 256
SLOTS = 192
CHUNK = 256
STEPS = TILE * NEIGH // CHUNK
NODE = 256
GAIN_ROWS = 8
F32 = jnp.float32
BF16 = jnp.bfloat16
MESH = pl.DeviceIdType.MESH


def mm(a, b):
    return lax.dot_general(a, b, (((1,), (0,)), ((), ())), preferred_element_type=F32)


def nt(a, b):
    return lax.dot_general(a, b, (((1,), (1,)), ((), ())), preferred_element_type=F32)


def sigmoid(v):
    return 0.5 * jnp.tanh(0.5 * v) + 0.5


def mean0(v):
    return jnp.sum(v, axis=0, keepdims=True) * (1.0 / W)


def norm_centred(centred):
    inv = lax.rsqrt(mean0(centred * centred) + EPS)
    return centred * inv, inv


def half_silu(h):
    t = jnp.tanh(h)
    up = 1.0 + t
    act = h * up
    return act, up + act * (1.0 - t)


def narrow_half_silu(h):
    h = h.astype(BF16)
    t = jnp.tanh(h)
    one = jnp.ones((), BF16)
    return h * (one + t), t


def rows_of(row):
    return jnp.concatenate([jnp.broadcast_to(row, (16, row.shape[1])).astype(BF16)] * (W // 16), axis=0)


def centred_pair(w):
    w_t = jnp.transpose(w.astype(F32))
    centred = w_t - mean0(w_t)
    high = centred.astype(BF16)
    return jnp.concatenate([high, (centred - high.astype(F32)).astype(BF16)], axis=1)


def beside(parts):
    return jnp.concatenate(parts, axis=1)


def beside(parts):
    return jnp.concatenate(parts, axis=1)


def twice(v):
    return jnp.concatenate([v, v], axis=0)


def one_hot(row, ids):
    wide = jnp.broadcast_to(row, (16, W)).astype(BF16)
    same = jnp.concatenate([wide] * (ids.shape[0] // 16), axis=0) == ids
    return jnp.where(same, jnp.ones((), BF16), jnp.zeros((), BF16))


def low_half():
    return lax.broadcasted_iota(jnp.int32, (W, W), 1) < TILE


def swap(v):
    return pltpu.roll(v, TILE, 1)


def spread_halves(block, low):
    other = swap(block)
    return jnp.where(low, block, other), jnp.where(low, other, block)


def column_of(row):
    return jnp.transpose(jnp.broadcast_to(row, (W, W)))


def kernel(sizes, *refs):
    far, near, in_sems = refs[:15], refs[-16:-1], refs[-1]
    (lat, gm, nb, send, clus, w_send, w_recv, w_edge, w_self, w_agg, w_node, w_pin, w_pout, egain, ngain) = near
    mixed_o, grad_o, mats_o, gains_o = refs[15:19]
    (sbuf, ghost, ret, backbuf, pg, pf, early, early_in, early_mid, early_out, late, late_in, late_mid, late_out,
     lat_t, gm_t, oh_send, oh_clus, tab, tab_sh, gtab, gtab_sh, recv_t, wsa_t, we_c, wn_c, delta, ghost_t,
     oh_all, act_cols, act_all, slope_all, norm_all, inv_all, sum_t, agg_t, an_t, nslope_t, nn_t, ninv_t, fine_t, gfine_t,
     gy_t, gpn_t, gc_t, grecv_t, gp_own, gp_ghost, dw_edge, sums) = refs[19:69]
    (halo_s, halo_r, ret_s, ret_r, pg_s, pg_r, pf_s, pf_r,
     e1s, e1r, e2s, e2r, e3s, e3r, l1s, l1r, l2s, l2r, l3s, l3r) = refs[69:-16]
    loads = [pltpu.make_async_copy(a, b, in_sems.at[i]) for i, (a, b) in enumerate(zip(far, near))]
    for i in (3, 0, 1, 4, *range(5, 15), 2):
        loads[i].start()

    n_x, n_y, n_z = sizes
    n_a, n_b = n_x * n_z, n_y
    c_rows = 4 * W // n_a
    gx, gy, gz = lax.axis_index("gx"), lax.axis_index("gy"), lax.axis_index("gz")
    x_up = (lax.rem(gx + 1, n_x), gy, gz)
    x_low = (lax.rem(gx + n_x - 1, n_x), gy, gz)
    y_up = (gx, lax.rem(gy + 1, n_y), gz)
    y_low = (gx, lax.rem(gy + n_y - 1, n_y), gz)
    y_now, z_high = lax.div(gx, 2), lax.rem(gx, 2)
    z_low, core = lax.div(gy, 2), lax.rem(gy, 2)
    n_yc, n_zl = n_x // 2, n_y // 2
    z_now = z_high * n_zl + z_low
    rank_a, rank_b = (y_now * 2 + core) * n_z + gz, z_now

    def hops(step, n):
        return min(step, n - step)

    ys = [lax.rem(y_now + d, n_yc) for d in range(n_yc)]
    cs = [core, 1 - core]
    xs = [lax.rem(gz + d, n_z) for d in range(n_z)]
    order = sorted(
        [(d, e, f) for d in range(n_yc) for e in range(2) for f in range(n_z)][1:],
        key=lambda o: (-hops(o[0], n_yc) - hops(o[2], n_z), o),
    )
    plane = [
        ((ys[d] * 2 + cs[e]) * n_z + xs[f], (ys[d] * 2 + z_high, z_low * 2 + cs[e], xs[f])) for d, e, f in order
    ]
    zs = [lax.rem(z_now + d, n_b) for d in sorted(range(1, n_b), key=lambda d: (-hops(d, n_b), d))]
    column = [(z, (y_now * 2 + lax.div(z, n_zl), lax.rem(z, n_zl) * 2 + core, gz)) for z in zs]
    row = [(xs[d], (gx, gy, xs[d])) for d in sorted(range(1, n_z), key=lambda d: (-hops(d, n_z), d))]

    def remote(src, dst, s, r, dev):
        return pltpu.make_async_remote_copy(
            src_ref=src, dst_ref=dst, send_sem=s, recv_sem=r, device_id=dev, device_id_type=MESH
        )

    def drain(ref, sem):
        pltpu.make_async_copy(ref, ref, sem).wait()

    barrier = pltpu.get_barrier_semaphore()
    for dev in (x_up, x_low, y_up, y_low, *[d for _, d in plane], *[d for _, d in column]):
        pl.semaphore_signal(barrier, inc=1, device_id=dev, device_id_type=MESH)

    lane_row = lax.broadcasted_iota(jnp.int32, (TILE, W), 1)
    loads[3].wait()
    send_f = send[...].astype(F32)
    for q in range(4):
        col = jnp.transpose(jnp.broadcast_to(send_f[q : q + 1, :], (W, TILE))).astype(jnp.int32)
        for b in range(PAIRS):
            hot = jnp.where(col == lane_row + b * W, 1.0, 0.0).astype(BF16)
            oh_send[q * TILE : (q + 1) * TILE, b * W : (b + 1) * W] = hot
    loads[0].wait()
    cells = mm(oh_send[...], lat[...]).astype(BF16)
    for slot, q in enumerate((2, 3, 0, 1, 1, 3, 0, 2)):
        sbuf[slot * TILE : (slot + 1) * TILE, :] = cells[q * TILE : (q + 1) * TILE, :]
    pl.semaphore_wait(barrier, 4 + n_a - 1 + n_b - 1)
    halo_to = (x_up, x_low, y_up, y_low)
    halo = [
        remote(sbuf.at[pl.ds(q * W, W)], ghost.at[pl.ds(q * W, W)], halo_s.at[q], halo_r.at[q], halo_to[q])
        for q in range(4)
    ]
    for c in halo:
        c.start()

    eye = jnp.where(
        lax.broadcasted_iota(jnp.int32, (W, W), 0) == lax.broadcasted_iota(jnp.int32, (W, W), 1), 1.0, 0.0
    ).astype(BF16)
    loads[1].wait()
    loads[4].wait()
    gm_t[...] = nt(eye, gm[...]).astype(BF16)
    cl_id = lax.broadcasted_iota(jnp.int32, (CLUSTERS, W), 0).astype(F32).astype(BF16)
    clus_f = clus[...].astype(F32)
    for b in range(PAIRS):
        oh_clus[:, b * W : (b + 1) * W] = one_hot(clus_f[:, b * W : (b + 1) * W], cl_id)

    def pool_send(buf, s, r):
        for _, dev in row:
            remote(buf.at[gz], buf.at[gz], s, r, dev).start()

    def pool_wait(buf, r):
        drain(buf.at[pl.ds(0, n_z - 1)], r)

    pg[gz] = nt(gm_t[...], oh_clus[...]).astype(BF16)
    pool_send(pg, pg_s, pg_r)

    lat_t[...] = nt(eye, lat[...]).astype(BF16)
    for i in (*range(5, 15), 2):
        loads[i].wait()
    wsend_t = (jnp.transpose(w_send[...].astype(F32)) * 0.5).astype(BF16)
    wrecv_t = (jnp.transpose(w_recv[...].astype(F32)) * 0.5).astype(BF16)
    we_c[...] = centred_pair(w_edge[...])
    wn_c[...] = centred_pair(w_node[...])
    wsa_t[:, :W] = (jnp.transpose(w_self[...].astype(F32)) * 0.5).astype(BF16)
    wsa_t[:, W:] = (jnp.transpose(w_agg[...].astype(F32)) * 0.5).astype(BF16)
    w_edge_h = (w_edge[...].astype(F32) * 0.5).astype(BF16)
    w_node_h = (w_node[...].astype(F32) * 0.5).astype(BF16)
    tab[...] = mm(wsend_t, lat_t[...]).astype(BF16)
    lat_roll = jnp.concatenate([lat[TILE:, :], lat[:TILE, :]], axis=0)
    tab_sh[...] = nt(wsend_t, lat_roll).astype(BF16)
    recv_t[...] = mm(wrecv_t, lat_t[...]).astype(BF16).astype(F32)
    eg = column_of(egain[...])
    ng = column_of(ngain[...])

    def ghost_tables(first):
        part = slice(first, first + 2 * W)
        own = ghost[part, :]
        gtab[:, part] = nt(wsend_t, own).astype(BF16)
        gtab_sh[:, part] = nt(wsend_t, jnp.concatenate([own[TILE:, :], own[:TILE, :]], axis=0)).astype(BF16)

    def pick_tables(u, carry):
        low8 = low_half()[:8, :]
        slot_id = lax.broadcasted_iota(jnp.int32, (SLOTS, W), 0).astype(F32).astype(BF16)
        picks = nb[:, pl.ds(pl.multiple_of(u * W, W), W)]
        first, second = picks[:8, :], picks[8:, :]
        picks_of = (jnp.where(low8, first, swap(second)), jnp.where(low8, swap(first), second))
        for half in range(2):
            t = 2 * u + half
            chosen = picks_of[half]
            local = jnp.where(chosen >= ROWS, (chosen & (TILE - 1)) + 2 * TILE, (chosen - t * TILE) & (ROWS - 1))
            local = local.astype(F32)
            for q in range(STEPS):
                for c in (2 * q, 2 * q + 1):
                    oh_all[t, c] = one_hot(local[c : c + 1, :], slot_id)
        return carry

    lax.fori_loop(0, PAIRS, pick_tables, 0)

    def forward(u, carry):
        low = low_half()
        at = u * W if isinstance(u, int) else pl.multiple_of(u * W, W)
        at_g = u % (GHOSTS // W) * W if isinstance(u, int) else pl.multiple_of(lax.rem(u, GHOSTS // W) * W, W)
        recv_of = spread_halves(recv_t[:, pl.ds(at, W)], low)
        sums_of = []
        for half in range(2):
            t = 2 * u + half
            own, far = (tab, gtab) if half == 0 else (tab_sh, gtab_sh)
            window = jnp.concatenate([own[:, pl.ds(at, W)], far[:, pl.ds(at_g, TILE)]], axis=1)
            total = None
            for q in range(STEPS):
                lanes = slice(q * CHUNK, (q + 1) * CHUNK)
                act_b, bend = narrow_half_silu(mm(window, beside([oh_all[t, 2 * q], oh_all[t, 2 * q + 1]])) + jnp.concatenate([recv_of[half]] * 2, axis=1))
                act_all[t, :, lanes] = act_b
                slope_all[t, :, lanes] = bend
                normed, inv = norm_centred(mm(we_c[...], twice(act_b)))
                norm_all[t, :, lanes] = normed.astype(BF16)
                inv_all[t, :, lanes] = inv
                part = normed[:, :W] + normed[:, W:]
                total = part if total is None else total + part
            sums_of.append(total + swap(total))
        total = jnp.where(low, sums_of[0], sums_of[1])
        sum_t[:, pl.ds(at, W)] = total
        agg_t[:, pl.ds(at, W)] = (total * eg).astype(BF16)
        return carry

    def node_forward(u, carry):
        at = u * NODE
        lat_b = lat_t[:, pl.ds(at, NODE)]
        an, slope = half_silu(mm(wsa_t[...], jnp.concatenate([lat_b, agg_t[:, pl.ds(at, NODE)]], axis=0)))
        an_b = an.astype(BF16)
        an_t[:, pl.ds(at, NODE)] = an_b
        nslope_t[:, pl.ds(at, NODE)] = slope
        nn, ninv = norm_centred(mm(wn_c[...], twice(an_b)))
        nn_t[:, pl.ds(at, NODE)] = nn
        ninv_t[:, pl.ds(at, NODE)] = ninv
        fine_t[:, pl.ds(at, NODE)] = (lat_b.astype(F32) + nn * widen(ng)).astype(BF16)
        return carry

    def widen(v):
        return jnp.concatenate([v] * (NODE // W), axis=1)

    halo[2].wait()
    halo[3].wait()
    ghost_tables(2 * W)
    for u in (2, 3, 6, 7):
        forward(u, 0)
    for k in (1, 3):
        node_forward(k, 0)
    halo[0].wait()
    halo[1].wait()
    ghost_tables(0)
    for u in (0, 1, 4, 5):
        forward(u, 0)

    for k in (0, 2):
        node_forward(k, 0)

    pf[gz] = nt(fine_t[...], oh_clus[...]).astype(BF16)
    pool_send(pf, pf_s, pf_r)
    ghost_t[...] = nt(eye, ghost[...]).astype(BF16)

    def prepare(u, carry):
        one = jnp.ones((), BF16)
        for half in range(2):
            t = 2 * u + half
            for q in range(STEPS):
                lanes = slice(q * CHUNK, (q + 1) * CHUNK)
                bend, act = slope_all[t, :, lanes], act_all[t, :, lanes]
                slope_all[t, :, lanes] = (one + bend) + act * (one - bend)
                for i in range(CHUNK // W):
                    act_cols[t, 2 * q + i] = act[:, i * W : (i + 1) * W]
        return carry

    lax.fori_loop(0, PAIRS, prepare, 0)
    wpin_t = jnp.transpose(w_pin[...].astype(F32)).astype(BF16)
    wpout_t = jnp.transpose(w_pout[...].astype(F32)).astype(BF16)
    pool_wait(pg, pg_r)
    gd = pg[0].astype(F32)
    for k in range(1, n_z):
        gd = gd + pg[k].astype(F32)
    gd_b = gd.astype(BF16)
    gac = mm(w_pout[...], gd_b)
    pool_wait(pf, pf_r)
    pooled = pf[0].astype(F32)
    for k in range(1, n_z):
        pooled = pooled + pf[k].astype(F32)
    pooled_b = pooled.astype(BF16)
    pc = mm(wpin_t, pooled_b)
    s = sigmoid(pc)
    ac = pc * s
    ac_b = ac.astype(BF16)
    delta_b = mm(wpout_t, ac_b).astype(BF16)
    gpc_b = (gac * (s + ac * (1.0 - s))).astype(BF16)
    gpool_b = mm(w_pin[...], gpc_b).astype(BF16)
    delta[...] = delta_b
    dw_pin = nt(pooled_b, gpc_b) * (1.0 / n_z)
    dw_pout = nt(ac_b, gd_b) * (1.0 / n_z)

    sums[...] = jnp.zeros_like(sums)

    def node_back(u, carry):
        at = u * NODE
        gf = gm_t[:, pl.ds(at, NODE)].astype(F32) + mm(gpool_b, oh_clus[:, pl.ds(at, NODE)])
        gfine_t[:, pl.ds(at, NODE)] = gf
        nn = nn_t[:, pl.ds(at, NODE)]
        sums[1] += narrow(gf * nn)
        gn = gf * widen(ng)
        gy_b = ((gn - mean0(gn) - nn * mean0(gn * nn)) * ninv_t[:, pl.ds(at, NODE)]).astype(BF16)
        gy_t[:, pl.ds(at, NODE)] = gy_b
        gpn_b = (mm(w_node_h, gy_b) * nslope_t[:, pl.ds(at, NODE)]).astype(BF16)
        gpn_t[:, pl.ds(at, NODE)] = gpn_b
        ga = mm(w_agg[...], gpn_b)
        sums[0] += narrow(ga * sum_t[:, pl.ds(at, NODE)])
        g = ga * widen(eg)
        gc_t[:, pl.ds(at, NODE)] = g - mean0(g)
        return carry

    def narrow(v):
        total = v[:, :W]
        for b in range(1, NODE // W):
            total = total + v[:, b * W : (b + 1) * W]
        return total

    for k in range(ROWS // NODE):
        node_back(k, 0)

    def put(buf, index, mat, width):
        per = W // c_rows
        buf[index * per : (index + 1) * per, :c_rows, :] = mat.reshape(per, c_rows, W).astype(BF16)

    def reduce_out(buf, into, s, r):
        into[rank_a] = buf[rank_a]

        for to, dev in plane:
            remote(buf.at[to], into.at[rank_a], s, r, dev).start()

    def reduce_mid(buf, into, mid, s, r, s2, r2):
        drain(into.at[pl.ds(0, n_a - 1)], r)
        total = into[0].astype(F32)
        for k in range(1, n_a):
            total = total + into[k].astype(F32)
        mid[rank_b] = total.astype(BF16)
        for _, dev in column:
            remote(mid.at[rank_b], mid.at[rank_b], s2, r2, dev).start()

    def gather_out(mid, out, s2, r2, s3, r3):
        drain(mid.at[pl.ds(0, n_b - 1)], r2)
        total = mid[0].astype(F32)
        for k in range(1, n_b):
            total = total + mid[k].astype(F32)
        out[rank_a] = total.astype(BF16)
        for _, dev in plane:
            remote(out.at[rank_a], out.at[rank_a], s3, r3, dev).start()

    def finish(buf, mid, out, s, s2, s3, r3):
        drain(out.at[pl.ds(0, n_a - 1)], r3)
        drain(buf.at[pl.ds(0, n_a - 1)], s)
        drain(mid.at[pl.ds(0, n_b - 1)], s2)
        drain(out.at[pl.ds(0, n_a - 1)], s3)

    def row_sums(v):
        hi = v.astype(BF16)
        lo = (v - hi.astype(F32)).astype(BF16)
        ones = jnp.ones((GAIN_ROWS, W), BF16)
        return nt(ones, hi) + nt(ones, lo)

    dw_sa = nt(jnp.concatenate([lat_t[...], agg_t[...]], axis=0), gpn_t[...])
    put(early, 0, dw_sa[:W, :], c_rows)
    put(early, 1, dw_sa[W:, :], c_rows)
    put(early, 2, nt(an_t[...], gy_t[...]), c_rows)
    put(early, 3, dw_pin, c_rows)
    which = lax.broadcasted_iota(jnp.int32, (GAIN_ROWS, W), 0)
    gain_rows = jnp.where(which == 0, row_sums(sums[0]), row_sums(sums[1])).astype(BF16)
    for k in range(n_a):
        early[k, c_rows:, :] = gain_rows
    reduce_out(early, early_in, e1s, e1r)

    gp_own[...] = jnp.zeros_like(gp_own)
    gp_ghost[...] = jnp.zeros_like(gp_ghost)
    dw_edge[...] = jnp.zeros_like(dw_edge)

    def backward(u, carry):
        low = low_half()
        at = u * W if isinstance(u, int) else pl.multiple_of(u * W, W)
        at_g = u % (GHOSTS // W) * W if isinstance(u, int) else pl.multiple_of(lax.rem(u, GHOSTS // W) * W, W)
        gc_of = spread_halves(gc_t[:, pl.ds(at, W)], low)
        back_of = []
        for half in range(2):
            t = 2 * u + half
            gzs, gps = [], []
            gc = jnp.concatenate([gc_of[half].astype(BF16)] * 2, axis=1)
            total = None
            for q in range(STEPS):
                lanes = slice(q * CHUNK, (q + 1) * CHUNK)
                normed = norm_all[t, :, lanes]
                shared = rows_of(mean0((gc * normed).astype(F32)))
                gz_b = (gc - normed * shared) * rows_of(inv_all[t, :, lanes])
                gzs.append(gz_b)
                gpre_b = mm(w_edge_h, gz_b).astype(BF16) * slope_all[t, :, lanes]
                gps.append(gpre_b)
                gpre = gpre_b.astype(F32)
                part = gpre[:, :W] + gpre[:, W:]
                total = part if total is None else total + part
            dw_edge[...] += nt(beside([act_cols[t, c] for c in range(2 * STEPS)]), beside(gzs))
            window = nt(beside([oh_all[t, c] for c in range(2 * STEPS)]), beside(gps))
            gp_own[pl.ds(at + half * TILE, W), :] += window[:W, :]
            gp_ghost[pl.ds(at_g + half * TILE, TILE), :] += window[W:, :]
            back_of.append(total + swap(total))
        grecv_t[:, pl.ds(at, W)] = jnp.where(low, back_of[0], back_of[1]).astype(BF16)
        return carry

    back_to = (x_low, x_up, y_low, y_up)
    back = [
        remote(backbuf.at[pl.ds(q * W, W)], ret.at[pl.ds(q * W, W)], ret_s.at[q], ret_r.at[q], back_to[q])
        for q in range(4)
    ]
    for u in (0, 1, 4, 5):
        backward(u, 0)
    backbuf[: 2 * W, :] = gp_ghost[: 2 * W, :].astype(BF16)
    back[0].start()
    back[1].start()

    def backward_near(k, c):
        return backward(k * 4 + 3, backward(k * 4 + 2, c))

    for u in (2, 3, 6, 7):
        backward(u, 0)
    backbuf[2 * W :, :] = gp_ghost[2 * W :, :].astype(BF16)
    back[2].start()
    back[3].start()

    gp_own[:TILE, :] += gp_own[ROWS:, :]
    own_b = gp_own[:ROWS, :].astype(BF16)
    put(late, 0, mm(lat_t[...], own_b) + mm(ghost_t[...], backbuf[...]), c_rows)
    put(late, 1, nt(lat_t[...], grecv_t[...]), c_rows)
    put(late, 2, dw_edge[...], c_rows)
    put(late, 3, dw_pout, c_rows)
    reduce_out(late, late_in, l1s, l1r)

    gfine_t[...] += (
        mm(w_self[...], gpn_t[...]) + mm(w_recv[...], grecv_t[...]) + nt(w_send[...], own_b)
    )
    reduce_mid(early, early_in, early_mid, e1s, e1r, e2s, e2r)
    for c in back:
        c.wait()
    side_a = jnp.concatenate([ret[q * TILE : (q + 1) * TILE, :] for q in (2, 3, 0, 1)], axis=0)
    side_b = jnp.concatenate([ret[q * TILE : (q + 1) * TILE, :] for q in (6, 4, 7, 5)], axis=0)
    ret_t = (nt(w_send[...], side_a) + nt(w_send[...], side_b)).astype(BF16)
    gfine_t[...] += mm(ret_t, oh_send[...])
    mixed = fine_t[...].astype(F32) + mm(delta[...], oh_clus[...])
    for b in range(PAIRS):
        mixed_o[b * W : (b + 1) * W, :] = jnp.transpose(mixed[:, b * W : (b + 1) * W]).astype(BF16)
    reduce_mid(late, late_in, late_mid, l1s, l1r, l2s, l2r)
    gather_out(early_mid, early_out, e2s, e2r, e3s, e3r)
    for b in range(PAIRS):
        grad_o[b * W : (b + 1) * W, :] = jnp.transpose(gfine_t[:, b * W : (b + 1) * W])

    def emit(out, index, place):
        per = W // c_rows
        mat = out[index * per : (index + 1) * per, :c_rows, :].astype(F32).reshape(W, W)
        mats_o[place] = mat * lax.rsqrt(jnp.mean(mat * mat, keepdims=True) + 1e-06)

    finish(early, early_mid, early_out, e1s, e2s, e3s, e3r)
    for index, place in enumerate((3, 4, 5, 6)):
        emit(early_out, index, place)
    scale = float(ROWS * n_x * n_y * n_z) ** (-0.5)
    gains_o[...] = early_out[0, c_rows : c_rows + 2, :].astype(F32) * scale
    pool_wait(pg, pg_s)
    pool_wait(pf, pf_s)
    gather_out(late_mid, late_out, l2s, l2r, l3s, l3r)
    finish(late, late_mid, late_out, l1s, l2s, l3s, l3r)
    for index, place in enumerate((0, 1, 2, 7)):
        emit(late_out, index, place)


def pass_on(*refs):
    sems = refs[-1]
    copies = [pltpu.make_async_copy(a, b, sems.at[i]) for i, (a, b) in enumerate(zip(refs[:4], refs[4:8]))]
    for c in copies:
        c.start()
    for c in copies:
        c.wait()


def solution(mesh):
    sizes = tuple(mesh.shape[name] for name in ("gx", "gy", "gz"))
    n_a, n_b, n_z = sizes[0] * sizes[2], sizes[1], sizes[2]
    c_rows = 4 * W // n_a
    tiles = ROWS // TILE
    edges = TILE * NEIGH
    v = pltpu.VMEM
    dma = pltpu.SemaphoreType.DMA

    def reduce_bufs(rows):
        return [v((n_a, rows, W), BF16), v((n_a, rows, W), BF16), v((n_b, rows, W), BF16), v((n_a, rows, W), BF16)]

    scratch = [
        v((GHOSTS, W), BF16),
        v((GHOSTS, W), BF16),
        v((GHOSTS, W), BF16),
        v((GHOSTS, W), BF16),
        v((n_z, W, CLUSTERS), BF16),
        v((n_z, W, CLUSTERS), BF16),
        *reduce_bufs(c_rows + GAIN_ROWS),
        *reduce_bufs(c_rows),
        v((W, ROWS), BF16),
        v((W, ROWS), BF16),
        v((4 * TILE, ROWS), BF16),
        v((CLUSTERS, ROWS), BF16),
        v((W, ROWS), BF16),
        v((W, ROWS), BF16),
        v((W, GHOSTS), BF16),
        v((W, GHOSTS), BF16),
        v((W, ROWS), F32),
        v((W, 2 * W), BF16),
        v((W, 2 * W), BF16),
        v((W, 2 * W), BF16),
        v((W, CLUSTERS), BF16),
        v((W, GHOSTS), BF16),
        v((tiles, edges // W, SLOTS, W), BF16),
        v((tiles, edges // W, W, W), BF16),
        v((tiles, W, edges), BF16),
        v((tiles, W, edges), BF16),
        v((tiles, W, edges), BF16),
        v((tiles, 1, edges), F32),
        v((W, ROWS), F32),
        v((W, ROWS), BF16),
        v((W, ROWS), BF16),
        v((W, ROWS), F32),
        v((W, ROWS), F32),
        v((1, ROWS), F32),
        v((W, ROWS), BF16),
        v((W, ROWS), F32),
        v((W, ROWS), BF16),
        v((W, ROWS), BF16),
        v((W, ROWS), F32),
        v((W, ROWS), BF16),
        v((ROWS + TILE, W), F32),
        v((GHOSTS, W), F32),
        v((W, W), F32),
        v((2, W, W), F32),
        dma((4,)), dma((4,)), dma((4,)), dma((4,)),
        *[dma for _ in range(16)],
        v((ROWS, W), BF16), v((ROWS, W), BF16), v((NEIGH, ROWS), jnp.int32), v((4, TILE), jnp.int32),
        v((1, ROWS), jnp.int32), *[v((W, W), BF16) for _ in range(8)], v((1, W), F32), v((1, W), F32),
        dma((15,)),
    ]

    def step(latents, grad_mixed, neighbours, send_list, cluster, w_send, w_recv, w_edge, edge_gain, w_self, w_agg,
             w_node, node_gain, w_pool_in, w_pool_out):
        results = pl.pallas_call(
            functools.partial(kernel, sizes),
            out_shape=(
                jax.ShapeDtypeStruct((ROWS, W), BF16),
                jax.ShapeDtypeStruct((ROWS, W), F32),
                jax.ShapeDtypeStruct((8, W, W), F32),
                jax.ShapeDtypeStruct((2, W), F32),
            ),
            in_specs=[pl.BlockSpec(memory_space=pltpu.HBM)] * 15,
            out_specs=tuple([pl.BlockSpec(memory_space=pltpu.VMEM)] * 4),
            scratch_shapes=scratch,
            compiler_params=pltpu.CompilerParams(
                collective_id=0, has_side_effects=True, vmem_limit_bytes=44 * 1024 * 1024
            ),
        )(*[pltpu.with_memory_space_constraint(x, pltpu.HBM) for x in (
            latents, grad_mixed, neighbours.T, send_list, cluster.reshape(1, ROWS), w_send, w_recv, w_edge, w_self,
            w_agg, w_node, w_pool_in, w_pool_out, edge_gain.reshape(1, W), node_gain.reshape(1, W))])
        return pl.pallas_call(
            pass_on,
            out_shape=tuple(jax.ShapeDtypeStruct(r.shape, r.dtype) for r in results),
            in_specs=[pl.BlockSpec(memory_space=pltpu.VMEM)] * 4,
            out_specs=tuple([pl.BlockSpec(memory_space=pltpu.HBM)] * 4),
            scratch_shapes=[pltpu.SemaphoreType.DMA((4,))],
            compiler_params=pltpu.CompilerParams(vmem_limit_bytes=8 * 1024 * 1024),
        )(*results)

    rows = P(("gx", "gy", "gz"), None)
    in_specs = (rows, rows, rows, rows, P(("gx", "gy", "gz"))) + (P(),) * 10
    out_specs = (rows, rows, P(), P())
    return jax.shard_map(step, mesh=mesh, in_specs=in_specs, out_specs=out_specs, check_vma=False)
```

```python
import functools

import jax
import jax.numpy as jnp
from jax import lax
from jax.experimental import pallas as pl
from jax.experimental.pallas import tpu as pltpu
from jax.sharding import PartitionSpec as P

EPS = 1e-05
W = 128
ROWS = 1024
NEIGH = 16
TILE = 64
PAIRS = ROWS // W
GHOSTS = 512
CLUSTERS = 256
SLOTS = 192
CHUNK = 256
STEPS = TILE * NEIGH // CHUNK
NODE = 256
GAIN_ROWS = 8
F32 = jnp.float32
BF16 = jnp.bfloat16
MESH = pl.DeviceIdType.MESH


def mm(a, b):
    return lax.dot_general(a, b, (((1,), (0,)), ((), ())), preferred_element_type=F32)


def nt(a, b):
    return lax.dot_general(a, b, (((1,), (1,)), ((), ())), preferred_element_type=F32)


def sigmoid(v):
    return 0.5 * jnp.tanh(0.5 * v) + 0.5


def mean0(v):
    return jnp.sum(v, axis=0, keepdims=True) * (1.0 / W)


def norm_centred(centred):
    inv = lax.rsqrt(mean0(centred * centred) + EPS)
    return centred * inv, inv


def half_silu(h):
    t = jnp.tanh(h)
    up = 1.0 + t
    act = h * up
    return act, up + act * (1.0 - t)


def narrow_half_silu(h):
    h = h.astype(BF16)
    t = jnp.tanh(h)
    one = jnp.ones((), BF16)
    return h * (one + t), t


def rows_of(row):
    return jnp.concatenate([jnp.broadcast_to(row, (16, row.shape[1])).astype(BF16)] * (W // 16), axis=0)


def centred_pair(w):
    w_t = jnp.transpose(w.astype(F32))
    centred = w_t - mean0(w_t)
    high = centred.astype(BF16)
    return jnp.concatenate([high, (centred - high.astype(F32)).astype(BF16)], axis=1)


def beside(parts):
    return jnp.concatenate(parts, axis=1)


def beside(parts):
    return jnp.concatenate(parts, axis=1)


def twice(v):
    return jnp.concatenate([v, v], axis=0)


def one_hot(row, ids):
    wide = jnp.broadcast_to(row, (16, W)).astype(BF16)
    same = jnp.concatenate([wide] * (ids.shape[0] // 16), axis=0) == ids
    return jnp.where(same, jnp.ones((), BF16), jnp.zeros((), BF16))


def low_half():
    return lax.broadcasted_iota(jnp.int32, (W, W), 1) < TILE


def swap(v):
    return pltpu.roll(v, TILE, 1)


def spread_halves(block, low):
    other = swap(block)
    return jnp.where(low, block, other), jnp.where(low, other, block)


def column_of(row):
    return jnp.transpose(jnp.broadcast_to(row, (W, W)))


def kernel(sizes, *refs):
    far, near, in_sems = refs[:15], refs[-16:-1], refs[-1]
    (lat, gm, nb, send, clus, w_send, w_recv, w_edge, w_self, w_agg, w_node, w_pin, w_pout, egain, ngain) = near
    mixed_o, grad_o, mats_o, gains_o = refs[15:19]
    (sbuf, ghost, ret, backbuf, pg, pf, early, early_in, early_mid, early_out, late, late_in, late_mid, late_out,
     lat_t, gm_t, oh_send, oh_clus, tab, tab_sh, gtab, gtab_sh, recv_t, wsa_t, we_c, wn_c, delta, ghost_t,
     oh_all, act_cols, act_all, slope_all, norm_all, inv_all, sum_t, agg_t, an_t, nslope_t, nn_t, ninv_t, fine_t, gfine_t,
     gy_t, gpn_t, gc_t, grecv_t, gp_own, gp_ghost, dw_edge, sums) = refs[19:69]
    (halo_s, halo_r, ret_s, ret_r, pg_s, pg_r, pf_s, pf_r,
     e1s, e1r, e2s, e2r, e3s, e3r, l1s, l1r, l2s, l2r, l3s, l3r) = refs[69:-16]
    loads = [pltpu.make_async_copy(a, b, in_sems.at[i]) for i, (a, b) in enumerate(zip(far, near))]
    for i in (3, 0, 1, 4, *range(5, 15), 2):
        loads[i].start()

    n_x, n_y, n_z = sizes
    n_a, n_b = n_x * n_z, n_y
    c_rows = 4 * W // n_a
    gx, gy, gz = lax.axis_index("gx"), lax.axis_index("gy"), lax.axis_index("gz")
    x_up = (lax.rem(gx + 1, n_x), gy, gz)
    x_low = (lax.rem(gx + n_x - 1, n_x), gy, gz)
    y_up = (gx, lax.rem(gy + 1, n_y), gz)
    y_low = (gx, lax.rem(gy + n_y - 1, n_y), gz)
    y_now, z_high = lax.div(gx, 2), lax.rem(gx, 2)
    z_low, core = lax.div(gy, 2), lax.rem(gy, 2)
    n_yc, n_zl = n_x // 2, n_y // 2
    z_now = z_high * n_zl + z_low
    rank_a, rank_b = (y_now * 2 + core) * n_z + gz, z_now

    def hops(step, n):
        return min(step, n - step)

    ys = [lax.rem(y_now + d, n_yc) for d in range(n_yc)]
    cs = [core, 1 - core]
    xs = [lax.rem(gz + d, n_z) for d in range(n_z)]
    order = sorted(
        [(d, e, f) for d in range(n_yc) for e in range(2) for f in range(n_z)][1:],
        key=lambda o: (-hops(o[0], n_yc) - hops(o[2], n_z), o),
    )
    plane = [
        ((ys[d] * 2 + cs[e]) * n_z + xs[f], (ys[d] * 2 + z_high, z_low * 2 + cs[e], xs[f])) for d, e, f in order
    ]
    zs = [lax.rem(z_now + d, n_b) for d in sorted(range(1, n_b), key=lambda d: (-hops(d, n_b), d))]
    column = [(z, (y_now * 2 + lax.div(z, n_zl), lax.rem(z, n_zl) * 2 + core, gz)) for z in zs]
    row = [(xs[d], (gx, gy, xs[d])) for d in sorted(range(1, n_z), key=lambda d: (-hops(d, n_z), d))]

    def remote(src, dst, s, r, dev):
        return pltpu.make_async_remote_copy(
            src_ref=src, dst_ref=dst, send_sem=s, recv_sem=r, device_id=dev, device_id_type=MESH
        )

    def drain(ref, sem):
        pltpu.make_async_copy(ref, ref, sem).wait()

    barrier = pltpu.get_barrier_semaphore()
    for dev in (x_up, x_low, y_up, y_low, *[d for _, d in plane], *[d for _, d in column]):
        pl.semaphore_signal(barrier, inc=1, device_id=dev, device_id_type=MESH)

    lane_row = lax.broadcasted_iota(jnp.int32, (TILE, W), 1)
    loads[3].wait()
    send_f = send[...].astype(F32)
    for q in range(4):
        col = jnp.transpose(jnp.broadcast_to(send_f[q : q + 1, :], (W, TILE))).astype(jnp.int32)
        for b in range(PAIRS):
            hot = jnp.where(col == lane_row + b * W, 1.0, 0.0).astype(BF16)
            oh_send[q * TILE : (q + 1) * TILE, b * W : (b + 1) * W] = hot
    loads[0].wait()
    cells = mm(oh_send[...], lat[...]).astype(BF16)
    for slot, q in enumerate((2, 3, 0, 1, 1, 3, 0, 2)):
        sbuf[slot * TILE : (slot + 1) * TILE, :] = cells[q * TILE : (q + 1) * TILE, :]
    pl.semaphore_wait(barrier, 4 + n_a - 1 + n_b - 1)
    halo_to = (x_up, x_low, y_up, y_low)
    halo = [
        remote(sbuf.at[pl.ds(q * W, W)], ghost.at[pl.ds(q * W, W)], halo_s.at[q], halo_r.at[q], halo_to[q])
        for q in range(4)
    ]
    for c in halo:
        c.start()

    eye = jnp.where(
        lax.broadcasted_iota(jnp.int32, (W, W), 0) == lax.broadcasted_iota(jnp.int32, (W, W), 1), 1.0, 0.0
    ).astype(BF16)
    loads[1].wait()
    loads[4].wait()
    gm_t[...] = nt(eye, gm[...]).astype(BF16)
    cl_id = lax.broadcasted_iota(jnp.int32, (CLUSTERS, W), 0).astype(F32).astype(BF16)
    clus_f = clus[...].astype(F32)
    for b in range(PAIRS):
        oh_clus[:, b * W : (b + 1) * W] = one_hot(clus_f[:, b * W : (b + 1) * W], cl_id)

    def pool_send(buf, s, r):
        for _, dev in row:
            remote(buf.at[gz], buf.at[gz], s, r, dev).start()

    def pool_wait(buf, r):
        drain(buf.at[pl.ds(0, n_z - 1)], r)

    pg[gz] = nt(gm_t[...], oh_clus[...]).astype(BF16)
    pool_send(pg, pg_s, pg_r)

    lat_t[...] = nt(eye, lat[...]).astype(BF16)
    for i in (*range(5, 15), 2):
        loads[i].wait()
    wsend_t = (jnp.transpose(w_send[...].astype(F32)) * 0.5).astype(BF16)
    wrecv_t = (jnp.transpose(w_recv[...].astype(F32)) * 0.5).astype(BF16)
    we_c[...] = centred_pair(w_edge[...])
    wn_c[...] = centred_pair(w_node[...])
    wsa_t[:, :W] = (jnp.transpose(w_self[...].astype(F32)) * 0.5).astype(BF16)
    wsa_t[:, W:] = (jnp.transpose(w_agg[...].astype(F32)) * 0.5).astype(BF16)
    w_edge_h = (w_edge[...].astype(F32) * 0.5).astype(BF16)
    w_node_h = (w_node[...].astype(F32) * 0.5).astype(BF16)
    tab[...] = mm(wsend_t, lat_t[...]).astype(BF16)
    lat_roll = jnp.concatenate([lat[TILE:, :], lat[:TILE, :]], axis=0)
    tab_sh[...] = nt(wsend_t, lat_roll).astype(BF16)
    recv_t[...] = mm(wrecv_t, lat_t[...]).astype(BF16).astype(F32)
    eg = column_of(egain[...])
    ng = column_of(ngain[...])

    def ghost_tables(first):
        part = slice(first, first + 2 * W)
        own = ghost[part, :]
        gtab[:, part] = nt(wsend_t, own).astype(BF16)
        gtab_sh[:, part] = nt(wsend_t, jnp.concatenate([own[TILE:, :], own[:TILE, :]], axis=0)).astype(BF16)

    def pick_tables(u, carry):
        low8 = low_half()[:8, :]
        slot_id = lax.broadcasted_iota(jnp.int32, (SLOTS, W), 0).astype(F32).astype(BF16)
        picks = nb[:, pl.ds(pl.multiple_of(u * W, W), W)]
        first, second = picks[:8, :], picks[8:, :]
        picks_of = (jnp.where(low8, first, swap(second)), jnp.where(low8, swap(first), second))
        for half in range(2):
            t = 2 * u + half
            chosen = picks_of[half]
            local = jnp.where(chosen >= ROWS, (chosen & (TILE - 1)) + 2 * TILE, (chosen - t * TILE) & (ROWS - 1))
            local = local.astype(F32)
            for q in range(STEPS):
                for c in (2 * q, 2 * q + 1):
                    oh_all[t, c] = one_hot(local[c : c + 1, :], slot_id)
        return carry

    lax.fori_loop(0, PAIRS, pick_tables, 0)

    def forward(u, carry):
        low = low_half()
        at = u * W if isinstance(u, int) else pl.multiple_of(u * W, W)
        at_g = u % (GHOSTS // W) * W if isinstance(u, int) else pl.multiple_of(lax.rem(u, GHOSTS // W) * W, W)
        recv_of = spread_halves(recv_t[:, pl.ds(at, W)], low)
        sums_of = []
        for half in range(2):
            t = 2 * u + half
            own, far = (tab, gtab) if half == 0 else (tab_sh, gtab_sh)
            window = jnp.concatenate([own[:, pl.ds(at, W)], far[:, pl.ds(at_g, TILE)]], axis=1)
            total = None
            for q in range(STEPS):
                lanes = slice(q * CHUNK, (q + 1) * CHUNK)
                act_b, bend = narrow_half_silu(mm(window, beside([oh_all[t, 2 * q], oh_all[t, 2 * q + 1]])) + jnp.concatenate([recv_of[half]] * 2, axis=1))
                act_all[t, :, lanes] = act_b
                slope_all[t, :, lanes] = bend
                normed, inv = norm_centred(mm(we_c[...], twice(act_b)))
                norm_all[t, :, lanes] = normed.astype(BF16)
                inv_all[t, :, lanes] = inv
                part = normed[:, :W] + normed[:, W:]
                total = part if total is None else total + part
            sums_of.append(total + swap(total))
        total = jnp.where(low, sums_of[0], sums_of[1])
        sum_t[:, pl.ds(at, W)] = total
        agg_t[:, pl.ds(at, W)] = (total * eg).astype(BF16)
        return carry

    def node_forward(u, carry):
        at = u * NODE
        lat_b = lat_t[:, pl.ds(at, NODE)]
        an, slope = half_silu(mm(wsa_t[...], jnp.concatenate([lat_b, agg_t[:, pl.ds(at, NODE)]], axis=0)))
        an_b = an.astype(BF16)
        an_t[:, pl.ds(at, NODE)] = an_b
        nslope_t[:, pl.ds(at, NODE)] = slope
        nn, ninv = norm_centred(mm(wn_c[...], twice(an_b)))
        nn_t[:, pl.ds(at, NODE)] = nn
        ninv_t[:, pl.ds(at, NODE)] = ninv
        fine_t[:, pl.ds(at, NODE)] = (lat_b.astype(F32) + nn * widen(ng)).astype(BF16)
        return carry

    def widen(v):
        return jnp.concatenate([v] * (NODE // W), axis=1)

    halo[2].wait()
    halo[3].wait()
    ghost_tables(2 * W)
    for u in (2, 3, 6, 7):
        forward(u, 0)
    for k in (1, 3):
        node_forward(k, 0)
    for side in (1 - z_high, z_high):
        here = pl.ds(pl.multiple_of(side * W, W), W)
        pltpu.make_async_copy(ghost.at[here], ghost.at[here], halo_r.at[side]).wait()
        own = ghost[here, :]
        gtab[:, here] = nt(wsend_t, own).astype(BF16)
        gtab_sh[:, here] = nt(wsend_t, jnp.concatenate([own[TILE:, :], own[:TILE, :]], axis=0)).astype(BF16)
        forward(side, 0)
        forward(side + 4, 0)
    halo[0].wait_send()
    halo[1].wait_send()

    for k in (0, 2):
        node_forward(k, 0)

    pf[gz] = nt(fine_t[...], oh_clus[...]).astype(BF16)
    pool_send(pf, pf_s, pf_r)
    ghost_t[...] = nt(eye, ghost[...]).astype(BF16)

    def prepare(u, carry):
        one = jnp.ones((), BF16)
        for half in range(2):
            t = 2 * u + half
            for q in range(STEPS):
                lanes = slice(q * CHUNK, (q + 1) * CHUNK)
                bend, act = slope_all[t, :, lanes], act_all[t, :, lanes]
                slope_all[t, :, lanes] = (one + bend) + act * (one - bend)
                for i in range(CHUNK // W):
                    act_cols[t, 2 * q + i] = act[:, i * W : (i + 1) * W]
        return carry

    lax.fori_loop(0, PAIRS, prepare, 0)
    wpin_t = jnp.transpose(w_pin[...].astype(F32)).astype(BF16)
    wpout_t = jnp.transpose(w_pout[...].astype(F32)).astype(BF16)
    pool_wait(pg, pg_r)
    gd = pg[0].astype(F32)
    for k in range(1, n_z):
        gd = gd + pg[k].astype(F32)
    gd_b = gd.astype(BF16)
    gac = mm(w_pout[...], gd_b)
    pool_wait(pf, pf_r)
    pooled = pf[0].astype(F32)
    for k in range(1, n_z):
        pooled = pooled + pf[k].astype(F32)
    pooled_b = pooled.astype(BF16)
    pc = mm(wpin_t, pooled_b)
    s = sigmoid(pc)
    ac = pc * s
    ac_b = ac.astype(BF16)
    delta_b = mm(wpout_t, ac_b).astype(BF16)
    gpc_b = (gac * (s + ac * (1.0 - s))).astype(BF16)
    gpool_b = mm(w_pin[...], gpc_b).astype(BF16)
    delta[...] = delta_b
    dw_pin = nt(pooled_b, gpc_b) * (1.0 / n_z)
    dw_pout = nt(ac_b, gd_b) * (1.0 / n_z)

    sums[...] = jnp.zeros_like(sums)

    def node_back(u, carry):
        at = u * NODE
        gf = gm_t[:, pl.ds(at, NODE)].astype(F32) + mm(gpool_b, oh_clus[:, pl.ds(at, NODE)])
        gfine_t[:, pl.ds(at, NODE)] = gf
        nn = nn_t[:, pl.ds(at, NODE)]
        sums[1] += narrow(gf * nn)
        gn = gf * widen(ng)
        gy_b = ((gn - mean0(gn) - nn * mean0(gn * nn)) * ninv_t[:, pl.ds(at, NODE)]).astype(BF16)
        gy_t[:, pl.ds(at, NODE)] = gy_b
        gpn_b = (mm(w_node_h, gy_b) * nslope_t[:, pl.ds(at, NODE)]).astype(BF16)
        gpn_t[:, pl.ds(at, NODE)] = gpn_b
        ga = mm(w_agg[...], gpn_b)
        sums[0] += narrow(ga * sum_t[:, pl.ds(at, NODE)])
        g = ga * widen(eg)
        gc_t[:, pl.ds(at, NODE)] = g - mean0(g)
        return carry

    def narrow(v):
        total = v[:, :W]
        for b in range(1, NODE // W):
            total = total + v[:, b * W : (b + 1) * W]
        return total

    for k in range(ROWS // NODE):
        node_back(k, 0)

    def put(buf, index, mat, width):
        per = W // c_rows
        buf[index * per : (index + 1) * per, :c_rows, :] = mat.reshape(per, c_rows, W).astype(BF16)

    def reduce_out(buf, into, s, r):
        into[rank_a] = buf[rank_a]

        for to, dev in plane:
            remote(buf.at[to], into.at[rank_a], s, r, dev).start()

    def reduce_mid(buf, into, mid, s, r, s2, r2):
        drain(into.at[pl.ds(0, n_a - 1)], r)
        total = into[0].astype(F32)
        for k in range(1, n_a):
            total = total + into[k].astype(F32)
        mid[rank_b] = total.astype(BF16)
        for _, dev in column:
            remote(mid.at[rank_b], mid.at[rank_b], s2, r2, dev).start()

    def gather_out(mid, out, s2, r2, s3, r3):
        drain(mid.at[pl.ds(0, n_b - 1)], r2)
        total = mid[0].astype(F32)
        for k in range(1, n_b):
            total = total + mid[k].astype(F32)
        out[rank_a] = total.astype(BF16)
        for _, dev in plane:
            remote(out.at[rank_a], out.at[rank_a], s3, r3, dev).start()

    def finish(buf, mid, out, s, s2, s3, r3):
        drain(out.at[pl.ds(0, n_a - 1)], r3)
        drain(buf.at[pl.ds(0, n_a - 1)], s)
        drain(mid.at[pl.ds(0, n_b - 1)], s2)
        drain(out.at[pl.ds(0, n_a - 1)], s3)

    def row_sums(v):
        hi = v.astype(BF16)
        lo = (v - hi.astype(F32)).astype(BF16)
        ones = jnp.ones((GAIN_ROWS, W), BF16)
        return nt(ones, hi) + nt(ones, lo)

    dw_sa = nt(jnp.concatenate([lat_t[...], agg_t[...]], axis=0), gpn_t[...])
    put(early, 0, dw_sa[:W, :], c_rows)
    put(early, 1, dw_sa[W:, :], c_rows)
    put(early, 2, nt(an_t[...], gy_t[...]), c_rows)
    put(early, 3, dw_pin, c_rows)
    which = lax.broadcasted_iota(jnp.int32, (GAIN_ROWS, W), 0)
    gain_rows = jnp.where(which == 0, row_sums(sums[0]), row_sums(sums[1])).astype(BF16)
    for k in range(n_a):
        early[k, c_rows:, :] = gain_rows
    reduce_out(early, early_in, e1s, e1r)

    gp_own[...] = jnp.zeros_like(gp_own)
    gp_ghost[...] = jnp.zeros_like(gp_ghost)
    dw_edge[...] = jnp.zeros_like(dw_edge)

    def backward(u, carry):
        low = low_half()
        at = u * W if isinstance(u, int) else pl.multiple_of(u * W, W)
        at_g = u % (GHOSTS // W) * W if isinstance(u, int) else pl.multiple_of(lax.rem(u, GHOSTS // W) * W, W)
        gc_of = spread_halves(gc_t[:, pl.ds(at, W)], low)
        back_of = []
        for half in range(2):
            t = 2 * u + half
            gzs, gps = [], []
            gc = jnp.concatenate([gc_of[half].astype(BF16)] * 2, axis=1)
            total = None
            for q in range(STEPS):
                lanes = slice(q * CHUNK, (q + 1) * CHUNK)
                normed = norm_all[t, :, lanes]
                shared = rows_of(mean0((gc * normed).astype(F32)))
                gz_b = (gc - normed * shared) * rows_of(inv_all[t, :, lanes])
                gzs.append(gz_b)
                gpre_b = mm(w_edge_h, gz_b).astype(BF16) * slope_all[t, :, lanes]
                gps.append(gpre_b)
                gpre = gpre_b.astype(F32)
                part = gpre[:, :W] + gpre[:, W:]
                total = part if total is None else total + part
            dw_edge[...] += nt(beside([act_cols[t, c] for c in range(2 * STEPS)]), beside(gzs))
            window = nt(beside([oh_all[t, c] for c in range(2 * STEPS)]), beside(gps))
            gp_own[pl.ds(at + half * TILE, W), :] += window[:W, :]
            gp_ghost[pl.ds(at_g + half * TILE, TILE), :] += window[W:, :]
            back_of.append(total + swap(total))
        grecv_t[:, pl.ds(at, W)] = jnp.where(low, back_of[0], back_of[1]).astype(BF16)
        return carry

    back_to = (x_low, x_up, y_low, y_up)
    back = [
        remote(backbuf.at[pl.ds(q * W, W)], ret.at[pl.ds(q * W, W)], ret_s.at[q], ret_r.at[q], back_to[q])
        for q in range(4)
    ]
    for u in (0, 1, 4, 5):
        backward(u, 0)
    backbuf[: 2 * W, :] = gp_ghost[: 2 * W, :].astype(BF16)
    back[0].start()
    back[1].start()

    def backward_near(k, c):
        return backward(k * 4 + 3, backward(k * 4 + 2, c))

    for u in (2, 3, 6, 7):
        backward(u, 0)
    backbuf[2 * W :, :] = gp_ghost[2 * W :, :].astype(BF16)
    back[2].start()
    back[3].start()

    gp_own[:TILE, :] += gp_own[ROWS:, :]
    own_b = gp_own[:ROWS, :].astype(BF16)
    put(late, 0, mm(lat_t[...], own_b) + mm(ghost_t[...], backbuf[...]), c_rows)
    put(late, 1, nt(lat_t[...], grecv_t[...]), c_rows)
    put(late, 2, dw_edge[...], c_rows)
    put(late, 3, dw_pout, c_rows)
    reduce_out(late, late_in, l1s, l1r)

    gfine_t[...] += (
        mm(w_self[...], gpn_t[...]) + mm(w_recv[...], grecv_t[...]) + nt(w_send[...], own_b)
    )
    reduce_mid(early, early_in, early_mid, e1s, e1r, e2s, e2r)
    for c in back:
        c.wait()
    side_a = jnp.concatenate([ret[q * TILE : (q + 1) * TILE, :] for q in (2, 3, 0, 1)], axis=0)
    side_b = jnp.concatenate([ret[q * TILE : (q + 1) * TILE, :] for q in (6, 4, 7, 5)], axis=0)
    ret_t = (nt(w_send[...], side_a) + nt(w_send[...], side_b)).astype(BF16)
    gfine_t[...] += mm(ret_t, oh_send[...])
    mixed = fine_t[...].astype(F32) + mm(delta[...], oh_clus[...])
    for b in range(PAIRS):
        mixed_o[b * W : (b + 1) * W, :] = jnp.transpose(mixed[:, b * W : (b + 1) * W]).astype(BF16)
    reduce_mid(late, late_in, late_mid, l1s, l1r, l2s, l2r)
    gather_out(early_mid, early_out, e2s, e2r, e3s, e3r)
    for b in range(PAIRS):
        grad_o[b * W : (b + 1) * W, :] = jnp.transpose(gfine_t[:, b * W : (b + 1) * W])

    def emit(out, index, place):
        per = W // c_rows
        mat = out[index * per : (index + 1) * per, :c_rows, :].astype(F32).reshape(W, W)
        mats_o[place] = mat * lax.rsqrt(jnp.mean(mat * mat, keepdims=True) + 1e-06)

    finish(early, early_mid, early_out, e1s, e2s, e3s, e3r)
    for index, place in enumerate((3, 4, 5, 6)):
        emit(early_out, index, place)
    scale = float(ROWS * n_x * n_y * n_z) ** (-0.5)
    gains_o[...] = early_out[0, c_rows : c_rows + 2, :].astype(F32) * scale
    pool_wait(pg, pg_s)
    pool_wait(pf, pf_s)
    gather_out(late_mid, late_out, l2s, l2r, l3s, l3r)
    finish(late, late_mid, late_out, l1s, l2s, l3s, l3r)
    for index, place in enumerate((0, 1, 2, 7)):
        emit(late_out, index, place)


def pass_on(*refs):
    sems = refs[-1]
    copies = [pltpu.make_async_copy(a, b, sems.at[i]) for i, (a, b) in enumerate(zip(refs[:4], refs[4:8]))]
    for c in copies:
        c.start()
    for c in copies:
        c.wait()


def solution(mesh):
    sizes = tuple(mesh.shape[name] for name in ("gx", "gy", "gz"))
    n_a, n_b, n_z = sizes[0] * sizes[2], sizes[1], sizes[2]
    c_rows = 4 * W // n_a
    tiles = ROWS // TILE
    edges = TILE * NEIGH
    v = pltpu.VMEM
    dma = pltpu.SemaphoreType.DMA

    def reduce_bufs(rows):
        return [v((n_a, rows, W), BF16), v((n_a, rows, W), BF16), v((n_b, rows, W), BF16), v((n_a, rows, W), BF16)]

    scratch = [
        v((GHOSTS, W), BF16),
        v((GHOSTS, W), BF16),
        v((GHOSTS, W), BF16),
        v((GHOSTS, W), BF16),
        v((n_z, W, CLUSTERS), BF16),
        v((n_z, W, CLUSTERS), BF16),
        *reduce_bufs(c_rows + GAIN_ROWS),
        *reduce_bufs(c_rows),
        v((W, ROWS), BF16),
        v((W, ROWS), BF16),
        v((4 * TILE, ROWS), BF16),
        v((CLUSTERS, ROWS), BF16),
        v((W, ROWS), BF16),
        v((W, ROWS), BF16),
        v((W, GHOSTS), BF16),
        v((W, GHOSTS), BF16),
        v((W, ROWS), F32),
        v((W, 2 * W), BF16),
        v((W, 2 * W), BF16),
        v((W, 2 * W), BF16),
        v((W, CLUSTERS), BF16),
        v((W, GHOSTS), BF16),
        v((tiles, edges // W, SLOTS, W), BF16),
        v((tiles, edges // W, W, W), BF16),
        v((tiles, W, edges), BF16),
        v((tiles, W, edges), BF16),
        v((tiles, W, edges), BF16),
        v((tiles, 1, edges), F32),
        v((W, ROWS), F32),
        v((W, ROWS), BF16),
        v((W, ROWS), BF16),
        v((W, ROWS), F32),
        v((W, ROWS), F32),
        v((1, ROWS), F32),
        v((W, ROWS), BF16),
        v((W, ROWS), F32),
        v((W, ROWS), BF16),
        v((W, ROWS), BF16),
        v((W, ROWS), F32),
        v((W, ROWS), BF16),
        v((ROWS + TILE, W), F32),
        v((GHOSTS, W), F32),
        v((W, W), F32),
        v((2, W, W), F32),
        dma((4,)), dma((4,)), dma((4,)), dma((4,)),
        *[dma for _ in range(16)],
        v((ROWS, W), BF16), v((ROWS, W), BF16), v((NEIGH, ROWS), jnp.int32), v((4, TILE), jnp.int32),
        v((1, ROWS), jnp.int32), *[v((W, W), BF16) for _ in range(8)], v((1, W), F32), v((1, W), F32),
        dma((15,)),
    ]

    def step(latents, grad_mixed, neighbours, send_list, cluster, w_send, w_recv, w_edge, edge_gain, w_self, w_agg,
             w_node, node_gain, w_pool_in, w_pool_out):
        results = pl.pallas_call(
            functools.partial(kernel, sizes),
            out_shape=(
                jax.ShapeDtypeStruct((ROWS, W), BF16),
                jax.ShapeDtypeStruct((ROWS, W), F32),
                jax.ShapeDtypeStruct((8, W, W), F32),
                jax.ShapeDtypeStruct((2, W), F32),
            ),
            in_specs=[pl.BlockSpec(memory_space=pltpu.HBM)] * 15,
            out_specs=tuple([pl.BlockSpec(memory_space=pltpu.VMEM)] * 4),
            scratch_shapes=scratch,
            compiler_params=pltpu.CompilerParams(
                collective_id=0, has_side_effects=True, vmem_limit_bytes=44 * 1024 * 1024
            ),
        )(*[pltpu.with_memory_space_constraint(x, pltpu.HBM) for x in (
            latents, grad_mixed, neighbours.T, send_list, cluster.reshape(1, ROWS), w_send, w_recv, w_edge, w_self,
            w_agg, w_node, w_pool_in, w_pool_out, edge_gain.reshape(1, W), node_gain.reshape(1, W))])
        return pl.pallas_call(
            pass_on,
            out_shape=tuple(jax.ShapeDtypeStruct(r.shape, r.dtype) for r in results),
            in_specs=[pl.BlockSpec(memory_space=pltpu.VMEM)] * 4,
            out_specs=tuple([pl.BlockSpec(memory_space=pltpu.HBM)] * 4),
            scratch_shapes=[pltpu.SemaphoreType.DMA((4,))],
            compiler_params=pltpu.CompilerParams(vmem_limit_bytes=8 * 1024 * 1024),
        )(*results)

    rows = P(("gx", "gy", "gz"), None)
    in_specs = (rows, rows, rows, rows, P(("gx", "gy", "gz"))) + (P(),) * 10
    out_specs = (rows, rows, P(), P())
    return jax.shard_map(step, mesh=mesh, in_specs=in_specs, out_specs=out_specs, check_vma=False)
```
